128 devices in a mesh: seq: 32 (over z, x_lo, y), fsdp: 4 (over x_hi, core).
Axes of the slice: x: 4 (x_hi: 2, x_lo: 2; x = x_hi * 2 + x_lo), y: 4, z: 4, core: 2. Of those that a mesh axis runs over, the one named last changes fastest.
Arguments:
- inputs: bfloat16 [4, 16384, 640], P('fsdp', 'seq'), may hold values from -6 to 6
- doc_start: int32 [4, 16384], P('fsdp', 'seq'), may hold values from 0 to 15360, as said below
- w_query: bfloat16 [640, 1024], P('fsdp'), may hold values from -0.25 to 0.25
- w_key: bfloat16 [640, 256], P('fsdp'), may hold values from -0.25 to 0.25
- w_value: bfloat16 [640, 256], P('fsdp'), may hold values from -0.25 to 0.25
- w_output: bfloat16 [1024, 640], P('fsdp'), may hold values from -0.375 to 0.375
- w_gate: bfloat16 [640, 2048], P('fsdp'), may hold values from -0.25 to 0.25
- w_up: bfloat16 [640, 2048], P('fsdp'), may hold values from -0.25 to 0.25
- w_down: bfloat16 [2048, 640], P('fsdp'), may hold values from -0.125 to 0.125
- norm_attn_in: bfloat16 [640], P('fsdp'), may hold values from 0.099609375 to 1.8984375
- norm_attn_out: bfloat16 [640], P('fsdp'), may hold values from 0.099609375 to 1.8984375
- norm_ffn_in: bfloat16 [640], P('fsdp'), may hold values from 0.099609375 to 1.8984375
- norm_ffn_out: bfloat16 [640], P('fsdp'), may hold values from 0.099609375 to 1.8984375
- norm_query: bfloat16 [256], P('fsdp'), may hold values from 0.099609375 to 1.8984375
- norm_key: bfloat16 [256], P('fsdp'), may hold values from 0.099609375 to 1.8984375
- cotangent: bfloat16 [4, 16384, 640], P('fsdp', 'seq'), may hold values from -6 to 6
Outputs:
- layer_out: bfloat16 [4, 16384, 640], P('fsdp', 'seq')
- input_grad: float32 [4, 16384, 640], P('fsdp', 'seq')
- query_grad: float32 [640, 1024], P('fsdp')
- key_grad: float32 [640, 256], P('fsdp')
- value_grad: float32 [640, 256], P('fsdp')
- output_grad: float32 [1024, 640], P('fsdp')
- gate_grad: float32 [640, 2048], P('fsdp')
- up_grad: float32 [640, 2048], P('fsdp')
- down_grad: float32 [2048, 640], P('fsdp')
- attn_in_grad: float32 [640], P('fsdp')
- attn_out_grad: float32 [640], P('fsdp')
- ffn_in_grad: float32 [640], P('fsdp')
- ffn_out_grad: float32 [640], P('fsdp')
- query_norm_grad: float32 [256], P('fsdp')
- key_norm_grad: float32 [256], P('fsdp')
The draws below stay inside these ranges and needn't reach their ends.
Inputs may be any that keep to these rules, and one draw needn't show every extreme that they name: Each row of 16384 tokens holds exactly two documents, each of 1024 tokens or more: doc_start is 0 up to the second document's first index and that index from there on; in some row the second document is exactly 1024 tokens long.
All inputs are finite; a program needn't handle non-finite values.
Results may differ from the reference program's by a relative error of at most 0.034.
Values may be sent and summed in bfloat16 or wider, within the bound.
A program may use at most 192 MiB of HBM per device.

```python
import jax
import jax.numpy as jnp
from jax import lax

MODEL_WIDTH = 640
HEADS = 4
HD = 256
FF = 2048
WINDOW = 512
LEAST_DOC_TOKENS = 1024
PACKED_ROWS = 4
PACKED_ROW_TOKENS = 16384


def draw_doc_start(key, part):
    unclipped_start = jax.random.randint(key, (PACKED_ROWS, 1), LEAST_DOC_TOKENS, PACKED_ROW_TOKENS - LEAST_DOC_TOKENS + 1, dtype=jnp.int32)
    document_boundary = unclipped_start + (PACKED_ROW_TOKENS - LEAST_DOC_TOKENS - jnp.max(unclipped_start))
    token_index = jnp.arange(PACKED_ROW_TOKENS, dtype=jnp.int32)[None, :]
    return jnp.where(token_index >= document_boundary, document_boundary, jnp.zeros_like(document_boundary)).astype(jnp.int32)


def spiked(values, stream_key, source, target, parts, factor):
    owner, partner = [(jnp.arange(values.shape[axis_at]) // (values.shape[axis_at] // parts)).reshape([-1 if axis == axis_at else 1 for axis in range(values.ndim)]) for axis_at in (source, target)]
    chosen = jax.random.permutation(stream_key, parts)[partner]
    strong = (owner == chosen) | (owner == (partner + parts // 2) % parts)
    return jnp.where(strong, factor * values, values)


def levels(stream_key, shape, shards, smallest, top_value):
    gain, own = 1.0, jax.random.fold_in(stream_key, 6)
    for dim, parts in shards:
        heights = jnp.exp(jax.random.uniform(jax.random.fold_in(own, dim), (parts,), jnp.float32, smallest / len(shards), top_value / len(shards)))
        gain = gain * jnp.repeat(heights, shape[dim] // parts).reshape([-1 if axis == dim else 1 for axis in range(len(shape))])
    return gain


def bell_draw(stream_key, dims, deviation, bound, pieces=(), held_as=jnp.bfloat16):
    entries = deviation * jax.random.normal(stream_key, dims, jnp.float32)
    if pieces:
        entries = entries * levels(stream_key, dims, pieces, -0.22, 0.18)
    return jnp.clip(entries, -bound, bound).astype(held_as)


def heavy_noise(rng, shape, deviation, reach, cuts, heavy, kind=jnp.bfloat16):
    values = deviation * jax.random.normal(rng, shape, jnp.float32)
    if cuts:
        values = values * levels(rng, shape, cuts, -0.22, 0.18)
    return jnp.clip(spiked(values, jax.random.fold_in(rng, 3), *heavy), -reach, reach).astype(kind)


def setup_inputs(seed: int = 0) -> dict:
    splits = jax.random.split(jax.random.key(seed), 17)
    return {
        "inputs": heavy_noise(splits[0], (PACKED_ROWS, PACKED_ROW_TOKENS, MODEL_WIDTH), 1.0, 6.0, ((0, 4), (1, 32)), (0, 2, 4, 2.0)),
        "doc_start": draw_doc_start(jax.random.fold_in(splits[16], 71), 0),
        "w_query": bell_draw(splits[2], (MODEL_WIDTH, HEADS * HD), MODEL_WIDTH ** -0.5, 0.25, ((0, 4),)),
        "w_key": bell_draw(splits[3], (MODEL_WIDTH, HD), MODEL_WIDTH ** -0.5, 0.25, ((0, 4),)),
        "w_value": bell_draw(splits[4], (MODEL_WIDTH, HD), MODEL_WIDTH ** -0.5, 0.25, ((0, 4),)),
        "w_output": bell_draw(splits[5], (HEADS * HD, MODEL_WIDTH), HD ** -0.5, 0.375, ((0, 4),)),
        "w_gate": bell_draw(splits[6], (MODEL_WIDTH, FF), MODEL_WIDTH ** -0.5, 0.25, ((0, 4),)),
        "w_up": bell_draw(splits[7], (MODEL_WIDTH, FF), MODEL_WIDTH ** -0.5, 0.25, ((0, 4),)),
        "w_down": bell_draw(splits[8], (FF, MODEL_WIDTH), FF ** -0.5, 0.125, ((0, 4),)),
        "norm_attn_in": jnp.clip(1.0 + 0.18 * jax.random.normal(splits[9], (MODEL_WIDTH,), jnp.float32), 0.099609375, 1.8984375).astype(jnp.bfloat16),
        "norm_attn_out": jnp.clip(1.0 + 0.18 * jax.random.normal(splits[10], (MODEL_WIDTH,), jnp.float32), 0.099609375, 1.8984375).astype(jnp.bfloat16),
        "norm_ffn_in": jnp.clip(1.0 + 0.18 * jax.random.normal(splits[11], (MODEL_WIDTH,), jnp.float32), 0.099609375, 1.8984375).astype(jnp.bfloat16),
        "norm_ffn_out": jnp.clip(1.0 + 0.18 * jax.random.normal(splits[12], (MODEL_WIDTH,), jnp.float32), 0.099609375, 1.8984375).astype(jnp.bfloat16),
        "norm_query": jnp.clip(1.0 + 0.18 * jax.random.normal(splits[13], (HD,), jnp.float32), 0.099609375, 1.8984375).astype(jnp.bfloat16),
        "norm_key": jnp.clip(1.0 + 0.18 * jax.random.normal(splits[14], (HD,), jnp.float32), 0.099609375, 1.8984375).astype(jnp.bfloat16),
        "cotangent": bell_draw(splits[15], (PACKED_ROWS, PACKED_ROW_TOKENS, MODEL_WIDTH), 1.0, 6.0, ((0, 4), (1, 32))),
    }


epsilon = 1e-06
rope_base = 10000.0
masked_value = -1e+30
highest = lax.Precision.HIGHEST

@jax.custom_vjp
def low(v):
    return lax.optimization_barrier(v.astype(jnp.bfloat16)).astype(jnp.float32)

@jax.custom_vjp
def low_back(v):
    return v

def low_keep(v):
    return (low(v), None)

def low_pass(kept, grad):
    return (grad,)

def back_keep(v):
    return (v, None)

def back_low(kept, grad):
    return (low(grad),)
low.defvjp(low_keep, low_pass)
low_back.defvjp(back_keep, back_low)

def matmul(left, right):
    return jnp.dot(left, right, preferred_element_type=jnp.float32, precision=highest)

def rms_scale(values, gains):
    return values * lax.rsqrt(lax.optimization_barrier(jnp.mean(values * values, -1, keepdims=True)) + epsilon) * gains

def rope_tables(positions, head_width):
    half_width = head_width // 2
    frequency = rope_base ** (-(jnp.arange(half_width, dtype=jnp.float32) * (2.0 / head_width)))
    angles = positions[:, None] * frequency[None, :]
    cosine = jnp.cos(angles)
    sine_part = jnp.sin(angles)
    return (jnp.concatenate([cosine, cosine], -1), jnp.concatenate([sine_part, sine_part], -1))

def rotate(values, cosine, sine_part):
    half_width = values.shape[-1] // 2
    turned = jnp.concatenate([-values[..., half_width:], values[..., :half_width]], -1)
    return values * cosine + turned * sine_part

def attend(queries, key_rows, value_rows, doc_row):
    length = queries.shape[0]
    block_rows = 512 if length % 512 == 0 else length
    reach_rows = -(-(WINDOW - 1) // block_rows) * block_rows
    padding = jnp.zeros((reach_rows, key_rows.shape[1]), jnp.float32)
    padded_keys = jnp.concatenate([padding, key_rows], 0)
    padded_values = jnp.concatenate([padding, value_rows], 0)
    score_scale = key_rows.shape[1] ** (-0.5)

    def one_block(number):
        first_row = number * block_rows
        query_block = lax.dynamic_slice_in_dim(queries, first_row, block_rows, 0)
        key_block = lax.dynamic_slice_in_dim(padded_keys, first_row, block_rows + reach_rows, 0)
        value_block = lax.dynamic_slice_in_dim(padded_values, first_row, block_rows + reach_rows, 0)
        doc_block = lax.dynamic_slice_in_dim(doc_row, first_row, block_rows, 0)
        query_index = first_row + jnp.arange(block_rows, dtype=jnp.int32)
        key_index = first_row - reach_rows + jnp.arange(block_rows + reach_rows, dtype=jnp.int32)
        visible = (key_index[None, :] >= doc_block[:, None]) & (key_index[None, :] <= query_index[:, None]) & (query_index[:, None] - key_index[None, :] < WINDOW)
        scores = jnp.einsum('thd,kd->htk', query_block, key_block, precision=highest) * score_scale
        scores = low_back(jnp.where(visible[None], scores, masked_value))
        soft_low = low(jax.nn.softmax(scores, axis=-1))
        return jnp.einsum('htk,kd->thd', soft_low, value_block, precision=highest)
    outputs = lax.map(jax.checkpoint(one_block), jnp.arange(length // block_rows, dtype=jnp.int32))
    return outputs.reshape(length, queries.shape[1], queries.shape[2])

def layer_row(source, doc_row, w_query, w_key, w_value, w_output, w_gate, w_up, w_down, norm_attn_in, norm_attn_out, norm_ffn_in, norm_ffn_out, norm_query, norm_key):
    length = source.shape[0]
    head_width = w_key.shape[1]
    head_count = w_query.shape[1] // head_width
    positions = (jnp.arange(length, dtype=jnp.int32) - doc_row).astype(jnp.float32)
    cosine, sine_part = rope_tables(positions, head_width)
    normed = low(rms_scale(source, norm_attn_in))
    query_raw = low_back(matmul(normed, w_query))
    key_raw = low_back(matmul(normed, w_key))
    value_raw = low_back(matmul(normed, w_value))
    queries = low(rotate(rms_scale(query_raw.reshape(length, head_count, head_width), norm_query), cosine[:, None, :], sine_part[:, None, :]))
    key_rows = low(rotate(rms_scale(key_raw, norm_key), cosine, sine_part))
    value_rows = low(value_raw)
    attended = attend(queries, key_rows, value_rows, doc_row)
    attended = low(low_back(attended)).reshape(length, head_count * head_width)
    projected = low_back(matmul(attended, w_output))
    hidden_one = source + rms_scale(projected, norm_attn_out)
    normed_two = low(rms_scale(hidden_one, norm_ffn_in))
    gate_value = low_back(matmul(normed_two, w_gate))
    up_value = low_back(matmul(normed_two, w_up))
    product = low(jax.nn.gelu(gate_value, approximate=True) * up_value)
    down_value = low_back(matmul(product, w_down))
    return hidden_one + rms_scale(down_value, norm_ffn_out)

def reference(inputs, doc_start, w_query, w_key, w_value, w_output, w_gate, w_up, w_down, norm_attn_in, norm_attn_out, norm_ffn_in, norm_ffn_out, norm_query, norm_key, cotangent):
    params = tuple((member.astype(jnp.float32) for member in (w_query, w_key, w_value, w_output, w_gate, w_up, w_down, norm_attn_in, norm_attn_out, norm_ffn_in, norm_ffn_out, norm_query, norm_key)))

    def row_step(totals, row_data):
        source, doc_row, upstream = row_data

        def forward(source_in, *weights_in):
            return layer_row(source_in, doc_row, *weights_in)
        result, pull = jax.vjp(forward, source, *params)
        grads = pull(upstream)
        totals = tuple((left + right for left, right in zip(totals, grads[1:])))
        return (totals, (result, grads[0]))
    zeros = tuple((jnp.zeros_like(member) for member in params))
    totals, (results, input_grads) = lax.scan(row_step, zeros, (inputs.astype(jnp.float32), doc_start, cotangent.astype(jnp.float32)))
    return (results.astype(jnp.bfloat16), input_grads, totals[0], totals[1], totals[2], totals[3], totals[4], totals[5], totals[6], totals[7], totals[8], totals[9], totals[10], totals[11], totals[12])
```

```python
import jax
import jax.numpy as jnp
from jax import lax
from jax.experimental import pallas as pl
from jax.experimental.pallas import tpu as pltpu
from jax.sharding import PartitionSpec as P

WINDOW = 512


epsilon = 1e-06
rope_base = 10000.0
masked_value = -1e30


def from_behind(shard, axis, by):
    count = lax.axis_size(axis)
    pairs = [(i, i + by) for i in range(count) if 0 <= i + by < count]
    return lax.ppermute(shard, axis, pairs)


MESH = pl.DeviceIdType.MESH
DIMS = ("C", "X1", "X0", "Y1", "Y0", "Z1", "Z0")


def place():
    return lax.axis_index("seq"), lax.axis_index("fsdp")


def bit_of(dim, s, f):
    if dim == "C":
        return lax.rem(f, 2)
    if dim == "X1":
        return lax.div(f, 2)
    if dim == "X0":
        return lax.rem(lax.rem(lax.div(s, 4), 2) + lax.div(f, 2), 2)
    at = lax.rem(s, 4) if dim[0] == "Y" else lax.div(s, 8)
    if dim[1] == "1":
        return lax.div(at, 2)
    return lax.rem(lax.rem(at, 2) + lax.div(at, 2), 2)


def partner(dim, s, f):
    if dim == "C":
        return (s, f + 1 - 2 * lax.rem(f, 2))
    step = 1 - 2 * lax.rem(lax.div(s, 4), 2)
    if dim == "X0":
        return (s + 4 * step, f)
    if dim == "X1":
        return (s + 4 * step, f + 2 - 4 * lax.div(f, 2))
    at, scale = (lax.rem(s, 4), 1) if dim[0] == "Y" else (lax.div(s, 8), 8)
    if dim[1] == "1":
        return (s + scale * (3 - 2 * at), f)
    return (s + scale * (1 - 2 * lax.rem(at, 2)), f)


def greet(s, f):
    barrier = pltpu.get_barrier_semaphore()
    for dim in DIMS:
        pl.semaphore_signal(barrier, inc=1, device_id=partner(dim, s, f), device_id_type=MESH)
    pl.semaphore_wait(barrier, len(DIMS))


def span(start, size, tile):
    if isinstance(start, int):
        return pl.ds(start, size)
    return pl.ds(pl.multiple_of(start, tile), size)


class Region:
    def __init__(self, q, r, c):
        self.q, self.r, self.c = q, r, c

    def of(self, ref):
        return ref.at[pl.ds(*self.q), span(*self.r, 16), span(*self.c, 128)]

    def flat(self, ref, r0=0, c0=0):
        return ref.at[span(self.r[0] + r0, self.r[1], 16), span(self.c[0] + c0, self.c[1], 128)]

    def halved(self, axis, bit):
        start, size = getattr(self, axis)
        half = size // 2
        mine = Region(self.q, self.r, self.c)
        setattr(mine, axis, (start + bit * half, half))
        theirs = Region(self.q, self.r, self.c)
        setattr(theirs, axis, (start + (1 - bit) * half, half))
        return mine, theirs

    @property
    def shape(self):
        return (self.q[1], self.r[1], self.c[1])


def rows_per_step(rows, cols):
    best = 16
    for n in (32, 48, 64, 80, 96, 128, 160):
        if rows % n == 0 and n * cols <= 48 * 2048:
            best = n
    return best


def add_blocks(out, first, second, shape):
    quarters, rows, cols = shape
    step = rows_per_step(rows, cols)
    for q in range(quarters):

        def body(i, carry, q=q):
            at = i * step
            ref, index = out(q, at, step)
            ref_a, index_a = first(q, at, step)
            ref_b, index_b = second(q, at, step)
            ref[index] = ref_a[index_a] + ref_b[index_b]
            return carry

        lax.fori_loop(0, rows // step, body, 0)


def view(ref, region):
    def pick(q, at, step):
        rows = span(region.r[0] + at, step, 16)
        return ref, (region.q[0] + q, rows, span(region.c[0], region.c[1], 128))

    return pick


def flat_view(ref, region, r0, c0):
    def pick(q, at, step):
        return ref, (span(region.r[0] + r0 + at, step, 16), span(region.c[0] + c0, region.c[1], 128))

    return pick


def whole_view(ref):
    def pick(q, at, step):
        return ref, (q, span(at, step, 16), slice(None))

    return pick


ORDERS = (
    ("X1", "Y1", "Z1", "X0", "Y0", "Z0"),
    ("Y1", "Z1", "X0", "X1", "Y0", "Z0"),
    ("Z1", "X0", "Y0", "X1", "Z0", "Y1"),
    ("X0", "Y0", "Z0", "X1", "Y1", "Z1"),
    ("Y0", "Z0", "X1", "Y1", "Z1", "X0"),
    ("Z0", "X1", "Y1", "Z1", "X0", "Y0"),
)
PARTS = (
    (0, 0, 384, 0, 640, ORDERS[0], "rrr"),
    (1, 0, 160, 0, 1536, ORDERS[1], "ccr"),
    (1, 0, 160, 1536, 1536, ORDERS[2], "ccr"),
    (1, 0, 160, 3072, 1024, ORDERS[3], "ccc"),
    (0, 384, 128, 0, 640, ORDERS[3], "rrr"),
    (2, 0, 256, 0, 640, ORDERS[4], "rrr"),
    (3, 0, 160, 0, 1536, ORDERS[5], "ccr"),
)
SHARES = ((512, 640), (160, 4096), (256, 640), (160, 1536))


def part_shapes(part):
    _, _, rows, _, cols, order, splits = part
    shapes, shape, cut = [], [2, rows, cols], iter(splits)
    for dim in order[:4]:
        axis = 0 if dim == "X1" else {"r": 1, "c": 2}[next(cut)]
        shape[axis] //= 2
        shapes.append(tuple(shape))
    return shapes


def reduce_kernel(*refs):
    n = len(SHARES)
    grads, gains = refs[:n], refs[n]
    totals, gain_total = refs[n + 1 : 2 * n + 1], refs[2 * n + 1]
    scratch = list(refs[2 * n + 2 :])
    acc, from_core, inbox, extra = [], [], [], []
    for _ in PARTS:
        acc.append(scratch.pop(0))
        from_core.append(scratch.pop(0))
        inbox.append([scratch.pop(0) for _ in range(4)])
        extra.append([scratch.pop(0) for _ in range(3)])
    gain_in, gain_sum, send_sem, recv_sem, local_sem = scratch

    s, f = place()
    greet(s, f)
    pending, count = [], [0]

    def send(src, dst, dim):
        copy = pltpu.make_async_remote_copy(
            src_ref=src,
            dst_ref=dst,
            send_sem=send_sem.at[count[0]],
            recv_sem=recv_sem.at[count[0]],
            device_id=partner(dim, s, f),
            device_id_type=MESH,
        )
        copy.start()
        count[0] += 1
        pending.append(copy)
        return copy

    core = bit_of("C", s, f)
    flights, loads, where = [], [], []
    gain_flight = send(gains, gain_in.at[0], "C")
    for p, (tensor, r0, rows, c0, cols, order, splits) in enumerate(PARTS):
        block = (pl.ds(0, 2), pl.ds(r0, rows), pl.ds(c0, cols))
        flights.append(send(grads[tensor].at[block[0], 1 - core, block[1], block[2]], from_core[p], "C"))
        load = pltpu.make_async_copy(
            grads[tensor].at[block[0], core, block[1], block[2]], acc[p], local_sem.at[p]
        )
        load.start()
        loads.append(load)
        where.append(Region((0, 2), (0, rows), (0, cols)))
    cuts = [iter(part[6]) for part in PARTS]
    trail = [[] for _ in PARTS]

    gain_dims = ("C", "X1", "X0", "Y1", "Y0", "Z1", "Z0")

    def gain_step(step):
        gain_flight.wait_recv()
        before = gains if step == 0 else gain_sum.at[step - 1]
        gain_sum[step] = before[...] + gain_in[step]
        if step < 6:
            return send(gain_sum.at[step], gain_in.at[step + 1], gain_dims[step + 1])
        return None

    for step in range(5):
        for p, part in enumerate(PARTS):
            order = part[5]
            flights[p].wait_recv()
            if step == 0:
                loads[p].wait()
                source = whole_view(from_core[p])
            else:
                source = whole_view(inbox[p][step - 1])
            add_blocks(view(acc[p], where[p]), view(acc[p], where[p]), source, where[p].shape)
            if step == 4:
                flights[p] = send(where[p].of(acc[p]), extra[p][0], order[4])
                continue
            dim = order[step]
            axis = "q" if dim == "X1" else next(cuts[p])
            trail[p].append((dim, axis))
            where[p], theirs = where[p].halved(axis, bit_of(dim, s, f))
            flights[p] = send(theirs.of(acc[p]), inbox[p][step], dim)
        gain_flight = gain_step(step)
    for p, part in enumerate(PARTS):
        flights[p].wait_recv()
        add_blocks(whole_view(extra[p][1]), view(acc[p], where[p]), whole_view(extra[p][0]), where[p].shape)
        flights[p] = send(extra[p][1], extra[p][2], part[5][5])
    gain_flight = gain_step(5)
    back = []
    for p, part in enumerate(PARTS):
        tensor, r0, _, c0, _, _, _ = part
        flights[p].wait_recv()
        add_blocks(
            flat_view(totals[tensor], where[p], r0, c0),
            whole_view(extra[p][1]),
            whole_view(extra[p][2]),
            where[p].shape,
        )
        back.append([move for move in reversed(trail[p]) if move[1] != "q"])
        region = where[p].flat(totals[tensor], r0, c0)
        flights[p] = send(region, region, back[p][0][0])
    gain_step(6)
    for step in range(3):
        for p, part in enumerate(PARTS):
            tensor, r0, _, c0, _, _, _ = part
            dim, axis = back[p][step]
            flights[p].wait_recv()
            start, size = getattr(where[p], axis)
            setattr(where[p], axis, (start - bit_of(dim, s, f) * size, 2 * size))
            if step < 2:
                region = where[p].flat(totals[tensor], r0, c0)
                flights[p] = send(region, region, back[p][step + 1][0])
    gain_total[...] = gain_sum[6, bit_of("X1", s, f) * 2 + core]
    for copy in pending:
        copy.wait_send()


def reduce_gradients(grads, gains):
    scratch, sends = [], 7
    for part in PARTS:
        shapes = part_shapes(part)
        scratch += [pltpu.VMEM((2, part[2], part[4]), jnp.bfloat16)] * 2
        scratch += [pltpu.VMEM(shape, jnp.bfloat16) for shape in shapes]
        scratch += [pltpu.VMEM(shapes[-1], jnp.bfloat16)] * 3
        sends += 10
    scratch += [
        pltpu.VMEM((7, 4, 8, 128), jnp.float32),
        pltpu.VMEM((7, 4, 8, 128), jnp.float32),
        pltpu.SemaphoreType.DMA((sends,)),
        pltpu.SemaphoreType.DMA((sends,)),
        pltpu.SemaphoreType.DMA((len(PARTS),)),
    ]
    return pl.pallas_call(
        reduce_kernel,
        out_shape=[jax.ShapeDtypeStruct(shape, jnp.bfloat16) for shape in SHARES]
        + [jax.ShapeDtypeStruct((8, 128), jnp.float32)],
        in_specs=[pl.BlockSpec(memory_space=pl.ANY)] * len(SHARES)
        + [pl.BlockSpec(memory_space=pltpu.VMEM)],
        out_specs=[pl.BlockSpec(memory_space=pltpu.VMEM)] * (len(SHARES) + 1),
        scratch_shapes=scratch,
        compiler_params=pltpu.CompilerParams(
            collective_id=1, has_side_effects=True, vmem_limit_bytes=48 << 20
        ),
        name="reduce_gradients",
    )(*grads, gains)


PIECES = (
    (0, 0, 0, 160, 1024, "X0", "Z0", "c"),
    (1, 0, 1024, 160, 256, "Z0", "X0", "c"),
    (2, 0, 1280, 160, 256, "Z0", "X0", "c"),
    (3, 1, 0, 256, 640, "Y0", "X0", "r"),
    (4, 2, 0, 160, 2048, "Z1", "Y1", "c"),
    (5, 2, 2048, 160, 2048, "Z0", "Y0", "c"),
    (6, 3, 0, 512, 640, "Y1", "Z1", "r"),
)
WHOLES = ((4, 160, 1536), (4, 256, 640), (4, 160, 4096), (4, 512, 640))


def gather_kernel(*refs):
    shards, gains = refs[:7], refs[7]
    outs, gain_out = refs[8:12], refs[12]
    send_sem, recv_sem, local_sem = refs[13:]
    s, f = place()
    greet(s, f)
    copies, count = [], [0]

    def send(src, dst, dim):
        copy = pltpu.make_async_remote_copy(
            src_ref=src,
            dst_ref=dst,
            send_sem=send_sem.at[count[0]],
            recv_sem=recv_sem.at[count[0]],
            device_id=partner(dim, s, f),
            device_id_type=MESH,
        )
        copy.start()
        count[0] += 1
        copies.append(copy)
        return copy

    core, high = bit_of("C", s, f), bit_of("X1", s, f)
    far = 2 * (1 - high) + core
    own, locals_ = f, []
    flights = []
    gain_flight = send(gains, gain_out.at[own], "X1")
    load = pltpu.make_async_copy(gains, gain_out.at[own], local_sem.at[7])
    load.start()
    locals_.append(load)
    sides = [send(gains, gain_out.at[own], "C")]

    def boxes(piece, bit_one, bit_two):
        _, _, c0, rows, cols, _, _, cut = piece
        half = rows // 2
        if cut == "c":
            quarter = ((bit_two * half, half), (bit_one * (cols // 2), cols // 2))
        else:
            quarter = ((bit_two * half + bit_one * (half // 2), half // 2), (0, cols))
        return quarter, ((bit_two * half, half), (0, cols))

    def cut_of(ref, box, c0=0):
        (r, nr), (c, nc) = box
        return ref.at[span(r, nr, 16), span(c + c0, nc, 128)]

    for i, piece in enumerate(PIECES):
        quarter, _ = boxes(piece, bit_of(piece[5], s, f), bit_of(piece[6], s, f))
        flights.append(send(cut_of(shards[i], quarter), cut_of(outs[piece[1]].at[own], quarter, piece[2]), "X1"))
    for i, piece in enumerate(PIECES):
        out, c0, cols = outs[piece[1]].at[own], piece[2], piece[4]
        sides.append(send(shards[i], out.at[:, pl.ds(c0, cols)], "C"))
        load = pltpu.make_async_copy(shards[i], out.at[:, pl.ds(c0, cols)], local_sem.at[i])
        load.start()
        locals_.append(load)
    gain_flight.wait_recv()
    sides.append(send(gain_out.at[far], gain_out.at[far], "C"))
    for step in range(3):
        for i, piece in enumerate(PIECES):
            out, c0 = outs[piece[1]].at[far], piece[2]
            one, two = bit_of(piece[5], s, f), bit_of(piece[6], s, f)
            quarter, half = boxes(piece, one, two)
            flights[i].wait_recv()
            if step == 0:
                flights[i] = send(cut_of(out, quarter, c0), cut_of(out, quarter, c0), piece[5])
                sides.append(send(cut_of(out, quarter, c0), cut_of(out, quarter, c0), "C"))
            elif step == 1:
                other, _ = boxes(piece, 1 - one, two)
                flights[i] = send(cut_of(out, half, c0), cut_of(out, half, c0), piece[6])
                sides.append(send(cut_of(out, other, c0), cut_of(out, other, c0), "C"))
            else:
                _, other = boxes(piece, one, 1 - two)
                sides.append(send(cut_of(out, other, c0), cut_of(out, other, c0), "C"))
    for copy in sides:
        copy.wait_recv()
    for copy in copies:
        copy.wait_send()
    for load in locals_:
        load.wait()


def gather_weights(shards, gains):
    sends = 7 * len(PIECES) + 3
    return pl.pallas_call(
        gather_kernel,
        out_shape=[jax.ShapeDtypeStruct(shape, jnp.bfloat16) for shape in WHOLES]
        + [jax.ShapeDtypeStruct((4, 8, 128), jnp.float32)],
        in_specs=[pl.BlockSpec(memory_space=pl.ANY)] * 8,
        out_specs=[pl.BlockSpec(memory_space=pl.ANY)] * 5,
        scratch_shapes=[
            pltpu.SemaphoreType.DMA((sends,)),
            pltpu.SemaphoreType.DMA((sends,)),
            pltpu.SemaphoreType.DMA((8,)),
        ],
        compiler_params=pltpu.CompilerParams(collective_id=0, has_side_effects=True),
        name="gather_weights",
    )(*shards, gains)


def rms_scale(values, gains):
    return values * lax.rsqrt(jnp.mean(values * values, -1, keepdims=True) + epsilon) * gains


def rope_tables(positions, head_width):
    half_width = head_width // 2
    frequency = rope_base ** (-(jnp.arange(half_width, dtype=jnp.float32) * (2.0 / head_width)))
    angles = positions[:, None] * frequency[None, :]
    cosine = jnp.cos(angles)
    sine_part = jnp.sin(angles)
    return (jnp.concatenate([cosine, cosine], -1), jnp.concatenate([sine_part, sine_part], -1))


def rotate(values, cosine, sine_part):
    half_width = values.shape[-1] // 2
    turned = jnp.concatenate([-values[..., half_width:], values[..., :half_width]], -1)
    return values * cosine + turned * sine_part


def forward_dot(left, right):
    return jnp.dot(left, right, preferred_element_type=jnp.float32)


def contract_rows(left, right):
    return lax.dot_general(
        left, right, (((0,), (0,)), ((), ())), preferred_element_type=jnp.float32
    )


def contract_cols(left, right):
    return lax.dot_general(
        left, right, (((1,), (1,)), ((), ())), preferred_element_type=jnp.float32
    )


def gated_product(gate_value, up_value):
    return jax.nn.gelu(gate_value, approximate=True) * up_value


def body(
    inputs,
    doc_start,
    w_query,
    w_key,
    w_value,
    w_output,
    w_gate,
    w_up,
    w_down,
    norm_attn_in,
    norm_attn_out,
    norm_ffn_in,
    norm_ffn_out,
    norm_query,
    norm_key,
    cotangent,
):
    gain_shards = jnp.concatenate(
        [norm_attn_in, norm_attn_out, norm_ffn_in, norm_ffn_out, norm_query, norm_key]
    ).astype(jnp.float32)
    gain_shards = jnp.pad(gain_shards, (0, 256)).reshape(8, 128)
    full_qkv, full_output, full_gate_up, full_down, all_gains = gather_weights(
        (w_query, w_key, w_value, w_output, w_gate, w_up, w_down), gain_shards
    )
    full_qkv = full_qkv.reshape(640, 1536)
    full_output = full_output.reshape(1024, 640)
    full_gate_up = full_gate_up.reshape(640, 4096)
    full_down = full_down.reshape(2048, 640)
    all_gains = all_gains.reshape(4, 1024)
    gain_attn_in, gain_attn_out, gain_ffn_in, gain_ffn_out = [
        all_gains[:, 160 * i : 160 * (i + 1)].reshape(640) for i in range(4)
    ]
    gain_query = all_gains[:, 640:704].reshape(256)
    gain_key = all_gains[:, 704:768].reshape(256)
    length = inputs.shape[1]
    head_width, head_count = 256, 4
    span_count = -(-(WINDOW - 1) // length)
    block_index = lax.axis_index("seq")
    row_index = block_index * length + jnp.arange(length, dtype=jnp.int32)
    doc_local = doc_start[0]
    positions = (row_index - doc_local).astype(jnp.float32)
    cosine, sine_part = rope_tables(positions, head_width)
    source = inputs[0].astype(jnp.float32)
    normed, pull_attn_in = jax.vjp(rms_scale, source, gain_attn_in)
    normed_low = normed.astype(jnp.bfloat16)
    raw = forward_dot(normed_low, full_qkv)
    query_raw, key_raw, value_raw = raw[:, :1024], raw[:, 1024:1280], raw[:, 1280:]

    def shape_query(raw_rows, gains):
        return rotate(
            rms_scale(raw_rows.reshape(length, head_count, head_width), gains),
            cosine[:, None, :],
            sine_part[:, None, :],
        )

    def shape_key(raw_rows, gains):
        return rotate(rms_scale(raw_rows, gains), cosine, sine_part)

    query_rows, pull_query = jax.vjp(shape_query, query_raw, gain_query)
    key_rows, pull_key = jax.vjp(shape_key, key_raw, gain_key)
    query_low = query_rows.astype(jnp.bfloat16)
    key_low = key_rows.astype(jnp.bfloat16)
    value_low = value_raw.astype(jnp.bfloat16)
    pair = jnp.concatenate([key_low, value_low], 1)
    pair = jnp.concatenate([from_behind(pair, "seq", 1), pair], 0)
    all_keys, all_values = pair[:, :256], pair[:, 256:]
    key_index = (block_index - span_count) * length + jnp.arange(
        (span_count + 1) * length, dtype=jnp.int32
    )
    visible = (
        (key_index[None, :] >= doc_local[:, None])
        & (key_index[None, :] <= row_index[:, None])
        & (row_index[:, None] - key_index[None, :] < WINDOW)
    )
    score_scale = head_width ** (-0.5)

    def score_rows():
        raw_scores = (
            jnp.einsum("thd,kd->htk", query_low, all_keys, preferred_element_type=jnp.float32)
            * score_scale
        )
        return jnp.where(visible[None], raw_scores, masked_value)

    scores = score_rows()
    row_max = jnp.max(scores, -1, keepdims=True)
    shifted = jnp.exp(scores - row_max)
    row_total = jnp.sum(shifted, -1, keepdims=True)
    soft_weights = shifted / row_total
    log_total = row_max + jnp.log(row_total)
    weights_low = soft_weights.astype(jnp.bfloat16)
    attended = jnp.einsum(
        "htk,kd->thd", weights_low, all_values, preferred_element_type=jnp.float32
    )
    attended = attended.reshape(length, head_count * head_width).astype(jnp.bfloat16)
    projected = forward_dot(attended, full_output)
    branch_one, pull_attn_out = jax.vjp(rms_scale, projected, gain_attn_out)
    hidden_one = source + branch_one
    normed_two, pull_ffn_in = jax.vjp(rms_scale, hidden_one, gain_ffn_in)
    normed_two_low = normed_two.astype(jnp.bfloat16)
    gate_up = forward_dot(normed_two_low, full_gate_up)
    gate_value, up_value = gate_up[:, :2048], gate_up[:, 2048:]
    product, pull_product = jax.vjp(gated_product, gate_value, up_value)
    product_low = product.astype(jnp.bfloat16)
    down_value = forward_dot(product_low, full_down)
    branch_two, pull_ffn_out = jax.vjp(rms_scale, down_value, gain_ffn_out)
    layer_out = (hidden_one + branch_two).astype(jnp.bfloat16)[None]
    upstream = cotangent[0].astype(jnp.float32)
    d_down, grad_ffn_out = pull_ffn_out(upstream)
    d_down_low = d_down.astype(jnp.bfloat16)
    grad_down = contract_rows(product_low, d_down_low)
    d_product = contract_cols(d_down_low, full_down)
    d_gate, d_up = pull_product(d_product)
    d_gate_up = jnp.concatenate([d_gate.astype(jnp.bfloat16), d_up.astype(jnp.bfloat16)], 1)
    grad_gate_up = contract_rows(normed_two_low, d_gate_up)
    d_normed_two = contract_cols(d_gate_up, full_gate_up)
    d_hidden_part, grad_ffn_in = pull_ffn_in(d_normed_two)
    d_hidden = upstream + d_hidden_part
    d_projected, grad_attn_out = pull_attn_out(d_hidden)
    d_projected_low = d_projected.astype(jnp.bfloat16)
    grad_output = contract_rows(attended, d_projected_low)
    d_attended = (
        contract_cols(d_projected_low, full_output)
        .astype(jnp.bfloat16)
        .reshape(length, head_count, head_width)
    )
    soft_again = jnp.exp(score_rows() - log_total)
    d_soft = jnp.einsum("thd,kd->htk", d_attended, all_values, preferred_element_type=jnp.float32)
    inner_sum = jnp.sum(soft_again * d_soft, -1, keepdims=True)
    d_scores = (soft_again * (d_soft - inner_sum)).astype(jnp.bfloat16)
    d_queries = (
        jnp.einsum("htk,kd->thd", d_scores, all_keys, preferred_element_type=jnp.float32)
        * score_scale
    )
    d_keys = (
        jnp.einsum("htk,thd->kd", d_scores, query_low, preferred_element_type=jnp.float32)
        * score_scale
    )
    d_values = jnp.einsum(
        "htk,thd->kd",
        soft_again.astype(jnp.bfloat16),
        d_attended,
        preferred_element_type=jnp.float32,
    )
    d_key_own = d_keys[span_count * length :]
    d_value_own = d_values[span_count * length :]
    first = jnp.concatenate([d_keys[:length], d_values[:length]], 1).astype(jnp.bfloat16)
    back = from_behind(first, "seq", -1).astype(jnp.float32)
    key_back, value_back = back[:, :256], back[:, 256:]
    d_key_own = d_key_own + key_back
    d_value_own = d_value_own + value_back
    d_key_raw, grad_key_norm = pull_key(d_key_own)
    d_query_raw, grad_query_norm = pull_query(d_queries)
    d_raw = jnp.concatenate(
        [
            d_query_raw.astype(jnp.bfloat16),
            d_key_raw.astype(jnp.bfloat16),
            d_value_own.astype(jnp.bfloat16),
        ],
        1,
    )
    grad_qkv = contract_rows(normed_low, d_raw)
    d_normed = contract_cols(d_raw, full_qkv)
    d_source, grad_attn_in = pull_attn_in(d_normed)
    input_grad = (d_hidden + d_source)[None]
    gain_grads = jnp.concatenate(
        [g.reshape(4, -1) for g in (grad_attn_in, grad_attn_out, grad_ffn_in, grad_ffn_out, grad_query_norm, grad_key_norm)],
        1,
    )
    gain_grads = jnp.pad(gain_grads, ((0, 0), (0, 256))).reshape(4, 8, 128)
    down, gate_up_share, output, qkv, gains = reduce_gradients(
        [
            grad.astype(jnp.bfloat16).reshape(2, 2, grad.shape[0] // 4, grad.shape[1])
            for grad in (grad_down, grad_gate_up, grad_output, grad_qkv)
        ],
        gain_grads,
    )
    gains = gains.reshape(1024)
    return (
        layer_out,
        input_grad,
        qkv[:, :1024].astype(jnp.float32),
        qkv[:, 1024:1280].astype(jnp.float32),
        qkv[:, 1280:].astype(jnp.float32),
        output.astype(jnp.float32),
        gate_up_share[:, :2048].astype(jnp.float32),
        gate_up_share[:, 2048:].astype(jnp.float32),
        down.astype(jnp.float32),
        gains[:160],
        gains[160:320],
        gains[320:480],
        gains[480:640],
        gains[640:704],
        gains[704:768],
    )


def solution(mesh):
    in_specs = (
        P("fsdp", "seq", None),
        P("fsdp", "seq"),
        P("fsdp", None),
        P("fsdp", None),
        P("fsdp", None),
        P("fsdp", None),
        P("fsdp", None),
        P("fsdp", None),
        P("fsdp", None),
        P("fsdp"),
        P("fsdp"),
        P("fsdp"),
        P("fsdp"),
        P("fsdp"),
        P("fsdp"),
        P("fsdp", "seq", None),
    )
    out_specs = (
        P("fsdp", "seq", None),
        P("fsdp", "seq", None),
        P("fsdp", None),
        P("fsdp", None),
        P("fsdp", None),
        P("fsdp", None),
        P("fsdp", None),
        P("fsdp", None),
        P("fsdp", None),
        P("fsdp"),
        P("fsdp"),
        P("fsdp"),
        P("fsdp"),
        P("fsdp"),
        P("fsdp"),
    )
    return jax.shard_map(body, mesh=mesh, in_specs=in_specs, out_specs=out_specs, check_vma=False)
```

```python
import jax
import jax.numpy as jnp
from jax import lax
from jax.experimental import pallas as pl
from jax.experimental.pallas import tpu as pltpu
from jax.sharding import PartitionSpec as P

epsilon = 1e-06
rope_base = 10000.0


MESH = pl.DeviceIdType.MESH
DIMS = ("C", "X1", "X0", "Y1", "Y0", "Z1", "Z0")


def place():
    return lax.axis_index("seq"), lax.axis_index("fsdp")


def bit_of(dim, s, f):
    if dim == "C":
        return lax.rem(f, 2)
    if dim == "X1":
        return lax.div(f, 2)
    if dim == "X0":
        return lax.rem(lax.rem(lax.div(s, 4), 2) + lax.div(f, 2), 2)
    at = lax.rem(s, 4) if dim[0] == "Y" else lax.div(s, 8)
    if dim[1] == "1":
        return lax.div(at, 2)
    return lax.rem(lax.rem(at, 2) + lax.div(at, 2), 2)


def partner(dim, s, f):
    if dim == "C":
        return (s, f + 1 - 2 * lax.rem(f, 2))
    step = 1 - 2 * lax.rem(lax.div(s, 4), 2)
    if dim == "X0":
        return (s + 4 * step, f)
    if dim == "X1":
        return (s + 4 * step, f + 2 - 4 * lax.div(f, 2))
    at, scale = (lax.rem(s, 4), 1) if dim[0] == "Y" else (lax.div(s, 8), 8)
    if dim[1] == "1":
        return (s + scale * (3 - 2 * at), f)
    return (s + scale * (1 - 2 * lax.rem(at, 2)), f)


def greet(s, f):
    barrier = pltpu.get_barrier_semaphore()
    for dim in DIMS:
        pl.semaphore_signal(barrier, inc=1, device_id=partner(dim, s, f), device_id_type=MESH)
    pl.semaphore_wait(barrier, len(DIMS))


def span(start, size, tile):
    if isinstance(start, int):
        return pl.ds(start, size)
    return pl.ds(pl.multiple_of(start, tile), size)


class Region:
    def __init__(self, q, r, c):
        self.q, self.r, self.c = q, r, c

    def of(self, ref):
        return ref.at[pl.ds(*self.q), span(*self.r, 16), span(*self.c, 128)]

    def flat(self, ref, r0=0, c0=0):
        return ref.at[span(self.r[0] + r0, self.r[1], 16), span(self.c[0] + c0, self.c[1], 128)]

    def halved(self, axis, bit):
        start, size = getattr(self, axis)
        half = size // 2
        mine = Region(self.q, self.r, self.c)
        setattr(mine, axis, (start + bit * half, half))
        theirs = Region(self.q, self.r, self.c)
        setattr(theirs, axis, (start + (1 - bit) * half, half))
        return mine, theirs

    @property
    def shape(self):
        return (self.q[1], self.r[1], self.c[1])


def rows_per_step(rows, cols):
    best = 16
    for n in (32, 48, 64, 80, 96, 128, 160):
        if rows % n == 0 and n * cols <= 48 * 2048:
            best = n
    return best


def add_blocks(out, first, second, shape):
    quarters, rows, cols = shape
    step = rows_per_step(rows, cols)
    for q in range(quarters):

        def body(i, carry, q=q):
            at = i * step
            ref, index = out(q, at, step)
            ref_a, index_a = first(q, at, step)
            ref_b, index_b = second(q, at, step)
            ref[index] = ref_a[index_a] + ref_b[index_b]
            return carry

        lax.fori_loop(0, rows // step, body, 0)


def view(ref, region):
    def pick(q, at, step):
        rows = span(region.r[0] + at, step, 16)
        return ref, (region.q[0] + q, rows, span(region.c[0], region.c[1], 128))

    return pick


def flat_view(ref, region, r0, c0):
    def pick(q, at, step):
        return ref, (span(region.r[0] + r0 + at, step, 16), span(region.c[0] + c0, region.c[1], 128))

    return pick


def whole_view(ref):
    def pick(q, at, step):
        return ref, (q, span(at, step, 16), slice(None))

    return pick


ORDERS = (
    ("X1", "Y1", "Z1", "X0", "Y0", "Z0"),
    ("Y1", "Z1", "X0", "X1", "Y0", "Z0"),
    ("Z1", "X0", "Y0", "X1", "Z0", "Y1"),
    ("X0", "Y0", "Z0", "X1", "Y1", "Z1"),
    ("Y0", "Z0", "X1", "Y1", "Z1", "X0"),
    ("Z0", "X1", "Y1", "Z1", "X0", "Y0"),
)
PARTS = (
    (0, 0, 384, 0, 640, ORDERS[0], "rrr"),
    (1, 0, 160, 0, 1536, ORDERS[1], "ccr"),
    (1, 0, 160, 1536, 1536, ORDERS[2], "ccr"),
    (1, 0, 160, 3072, 1024, ORDERS[3], "ccc"),
    (0, 384, 128, 0, 640, ORDERS[3], "rrr"),
    (2, 0, 256, 0, 640, ORDERS[4], "rrr"),
    (3, 0, 160, 0, 1536, ORDERS[5], "ccr"),
)
SHARES = ((512, 640), (160, 4096), (256, 640), (160, 1536))


def part_shapes(part):
    _, _, rows, _, cols, order, splits = part
    shapes, shape, cut = [], [2, rows, cols], iter(splits)
    for dim in order[:4]:
        axis = 0 if dim == "X1" else {"r": 1, "c": 2}[next(cut)]
        shape[axis] //= 2
        shapes.append(tuple(shape))
    return shapes


def reduce_kernel(*refs):
    n = len(SHARES)
    grads, gains = refs[:n], refs[n]
    totals, gain_total = refs[n + 1 : 2 * n + 1], refs[2 * n + 1]
    scratch = list(refs[2 * n + 2 :])
    acc, from_core, inbox, extra = [], [], [], []
    for _ in PARTS:
        acc.append(scratch.pop(0))
        from_core.append(scratch.pop(0))
        inbox.append([scratch.pop(0) for _ in range(4)])
        extra.append([scratch.pop(0) for _ in range(3)])
    gain_in, gain_sum, send_sem, recv_sem, local_sem = scratch

    s, f = place()
    greet(s, f)
    pending, count = [], [0]

    def send(src, dst, dim):
        copy = pltpu.make_async_remote_copy(
            src_ref=src,
            dst_ref=dst,
            send_sem=send_sem.at[count[0]],
            recv_sem=recv_sem.at[count[0]],
            device_id=partner(dim, s, f),
            device_id_type=MESH,
        )
        copy.start()
        count[0] += 1
        pending.append(copy)
        return copy

    core = bit_of("C", s, f)
    flights, loads, where = [], [], []
    gain_flight = send(gains, gain_in.at[0], "C")
    for p, (tensor, r0, rows, c0, cols, order, splits) in enumerate(PARTS):
        block = (pl.ds(0, 2), pl.ds(r0, rows), pl.ds(c0, cols))
        flights.append(send(grads[tensor].at[block[0], 1 - core, block[1], block[2]], from_core[p], "C"))
        load = pltpu.make_async_copy(
            grads[tensor].at[block[0], core, block[1], block[2]], acc[p], local_sem.at[p]
        )
        load.start()
        loads.append(load)
        where.append(Region((0, 2), (0, rows), (0, cols)))
    cuts = [iter(part[6]) for part in PARTS]
    trail = [[] for _ in PARTS]

    gain_dims = ("C", "X1", "X0", "Y1", "Y0", "Z1", "Z0")

    def gain_step(step):
        gain_flight.wait_recv()
        before = gains if step == 0 else gain_sum.at[step - 1]
        gain_sum[step] = before[...] + gain_in[step]
        if step < 6:
            return send(gain_sum.at[step], gain_in.at[step + 1], gain_dims[step + 1])
        return None

    for step in range(5):
        for p, part in enumerate(PARTS):
            order = part[5]
            flights[p].wait_recv()
            if step == 0:
                loads[p].wait()
                source = whole_view(from_core[p])
            else:
                source = whole_view(inbox[p][step - 1])
            add_blocks(view(acc[p], where[p]), view(acc[p], where[p]), source, where[p].shape)
            if step == 4:
                flights[p] = send(where[p].of(acc[p]), extra[p][0], order[4])
                continue
            dim = order[step]
            axis = "q" if dim == "X1" else next(cuts[p])
            trail[p].append((dim, axis))
            where[p], theirs = where[p].halved(axis, bit_of(dim, s, f))
            flights[p] = send(theirs.of(acc[p]), inbox[p][step], dim)
        gain_flight = gain_step(step)
    for p, part in enumerate(PARTS):
        flights[p].wait_recv()
        add_blocks(whole_view(extra[p][1]), view(acc[p], where[p]), whole_view(extra[p][0]), where[p].shape)
        flights[p] = send(extra[p][1], extra[p][2], part[5][5])
    gain_flight = gain_step(5)
    back = []
    for p, part in enumerate(PARTS):
        tensor, r0, _, c0, _, _, _ = part
        flights[p].wait_recv()
        add_blocks(
            flat_view(totals[tensor], where[p], r0, c0),
            whole_view(extra[p][1]),
            whole_view(extra[p][2]),
            where[p].shape,
        )
        back.append([move for move in reversed(trail[p]) if move[1] != "q"])
        region = where[p].flat(totals[tensor], r0, c0)
        flights[p] = send(region, region, back[p][0][0])
    gain_step(6)
    for step in range(3):
        for p, part in enumerate(PARTS):
            tensor, r0, _, c0, _, _, _ = part
            dim, axis = back[p][step]
            flights[p].wait_recv()
            start, size = getattr(where[p], axis)
            setattr(where[p], axis, (start - bit_of(dim, s, f) * size, 2 * size))
            if step < 2:
                region = where[p].flat(totals[tensor], r0, c0)
                flights[p] = send(region, region, back[p][step + 1][0])
    gain_total[...] = gain_sum[6]
    for copy in pending:
        copy.wait_send()


def reduce_gradients(grads, gains):
    scratch, sends = [], 7
    for part in PARTS:
        shapes = part_shapes(part)
        scratch += [pltpu.VMEM((2, part[2], part[4]), jnp.bfloat16)] * 2
        scratch += [pltpu.VMEM(shape, jnp.bfloat16) for shape in shapes]
        scratch += [pltpu.VMEM(shapes[-1], jnp.bfloat16)] * 3
        sends += 10
    scratch += [
        pltpu.VMEM((7, 8, 640), jnp.float32),
        pltpu.VMEM((7, 8, 640), jnp.float32),
        pltpu.SemaphoreType.DMA((sends,)),
        pltpu.SemaphoreType.DMA((sends,)),
        pltpu.SemaphoreType.DMA((len(PARTS),)),
    ]
    return pl.pallas_call(
        reduce_kernel,
        out_shape=[jax.ShapeDtypeStruct(shape, jnp.bfloat16) for shape in SHARES]
        + [jax.ShapeDtypeStruct((8, 640), jnp.float32)],
        in_specs=[pl.BlockSpec(memory_space=pl.ANY)] * len(SHARES)
        + [pl.BlockSpec(memory_space=pltpu.VMEM)],
        out_specs=[pl.BlockSpec(memory_space=pltpu.VMEM)] * (len(SHARES) + 1),
        scratch_shapes=scratch,
        compiler_params=pltpu.CompilerParams(
            collective_id=1, has_side_effects=True, vmem_limit_bytes=48 << 20
        ),
        name="reduce_gradients",
    )(*grads, gains)


PIECES = (
    (0, 0, 0, 160, 1024, "X0", "Z0", "c"),
    (1, 0, 1024, 160, 256, "Z0", "X0", "c"),
    (2, 0, 1280, 160, 256, "Z0", "X0", "c"),
    (3, 1, 0, 256, 640, "Y0", "X0", "r"),
    (4, 2, 0, 160, 2048, "Z1", "Y1", "c"),
    (5, 2, 2048, 160, 2048, "Z0", "Y0", "c"),
    (6, 3, 0, 512, 640, "Y1", "Z1", "r"),
)
WHOLES = ((640, 1536), (1024, 640), (640, 4096), (2048, 640))


def own_gains(gain_shards, gain_own, f):
    gain_own[...] = jnp.zeros_like(gain_own)
    for i, shard in enumerate(gain_shards):
        share = shard.shape[1]
        shift = lax.broadcasted_iota(jnp.int32, (share, 4 * share), 1) - lax.broadcasted_iota(
            jnp.int32, (share, 4 * share), 0
        )
        chosen = jnp.where(shift == share * f, 1.0, 0.0).astype(jnp.bfloat16)
        row = jnp.dot(shard[...], chosen, preferred_element_type=jnp.float32)
        if i < 4:
            gain_own[i : i + 1, :] = row
        else:
            gain_own[4:5, 256 * (i - 4) : 256 * (i - 3)] = row


class Gather:
    def __init__(self, s, f, shards, outs, send_sem, recv_sem, local_sem):
        self.s, self.f, self.shards, self.outs = s, f, shards, outs
        self.send_sem, self.recv_sem, self.local_sem = send_sem, recv_sem, local_sem
        self.copies, self.count = [], 0
        self.core, high = bit_of("C", s, f), bit_of("X1", s, f)
        self.far = 2 * (1 - high) + self.core
        self.flights, self.sides, self.loads = {}, {}, {}

    def send(self, src, dst, dim):
        copy = pltpu.make_async_remote_copy(
            src_ref=src,
            dst_ref=dst,
            send_sem=self.send_sem.at[self.count],
            recv_sem=self.recv_sem.at[self.count],
            device_id=partner(dim, self.s, self.f),
            device_id_type=MESH,
        )
        copy.start()
        self.count += 1
        self.copies.append(copy)
        return copy

    def boxes(self, piece, bit_one, bit_two):
        _, _, c0, rows, cols, _, _, cut = piece
        half = rows // 2
        if cut == "c":
            quarter = ((bit_two * half, half), (bit_one * (cols // 2), cols // 2))
        else:
            quarter = ((bit_two * half + bit_one * (half // 2), half // 2), (0, cols))
        return quarter, ((bit_two * half, half), (0, cols))

    def spot(self, piece, share, box):
        (r, nr), (c, nc) = box
        return self.outs[piece[1]].at[span(r + share * piece[3], nr, 16), span(c + piece[2], nc, 128)]

    def begin(self):
        for i, piece in enumerate(PIECES):
            (r, nr), (c, nc) = quarter = self.boxes(
                piece, bit_of(piece[5], self.s, self.f), bit_of(piece[6], self.s, self.f)
            )[0]
            src = self.shards[i].at[span(r, nr, 16), span(c, nc, 128)]
            self.flights[i] = self.send(src, self.spot(piece, self.f, quarter), "X1")
        for i, piece in enumerate(PIECES):
            dst = self.spot(piece, self.f, ((0, piece[3]), (0, piece[4])))
            self.sides[i] = [self.send(self.shards[i], dst, "C")]
            self.loads[i] = pltpu.make_async_copy(self.shards[i], dst, self.local_sem.at[i])
            self.loads[i].start()

    def step(self, i, number):
        piece, s, f, far = PIECES[i], self.s, self.f, self.far
        one, two = bit_of(piece[5], s, f), bit_of(piece[6], s, f)
        quarter, half = self.boxes(piece, one, two)
        self.flights[i].wait_recv()
        if number == 0:
            here = self.spot(piece, far, quarter)
            self.flights[i] = self.send(here, here, piece[5])
        elif number == 1:
            here = self.spot(piece, far, half)
            self.flights[i] = self.send(here, here, piece[6])
            here = self.spot(piece, far, self.boxes(piece, 1 - one, two)[0])
        else:
            here = self.spot(piece, far, self.boxes(piece, one, 1 - two)[1])
        self.sides[i].append(self.send(here, here, "C"))

    def arrive(self, i):
        for copy in self.sides[i]:
            copy.wait_recv()
        self.loads[i].wait()


def gather_kernel(*refs):
    shards, gain_shards = refs[:7], refs[7:13]
    outs, gain_out = refs[13:17], refs[17]
    gain_own, gain_mid, gain_in, send_sem, recv_sem, local_sem = refs[18:]
    s, f = place()
    greet(s, f)
    gather = Gather(s, f, shards, outs, send_sem, recv_sem, local_sem)
    gather.begin()
    own_gains(gain_shards, gain_own, f)
    flight = gather.send(gain_own, gain_in.at[0], "C")
    for i in range(7):
        gather.step(i, 0)
    flight.wait_recv()
    gain_mid[...] = gain_own[...] + gain_in[0]
    flight = gather.send(gain_mid, gain_in.at[1], "X1")
    for number in (1, 2):
        for i in range(7):
            gather.step(i, number)
    flight.wait_recv()
    gain_out[...] = gain_mid[...] + gain_in[1]
    for i in range(7):
        gather.arrive(i)
    for copy in gather.copies:
        copy.wait_send()


SENDS = 7 * len(PIECES) + 2


def gather_weights(shards, gain_shards):
    return pl.pallas_call(
        gather_kernel,
        out_shape=[jax.ShapeDtypeStruct(shape, jnp.bfloat16) for shape in WHOLES]
        + [jax.ShapeDtypeStruct((8, 640), jnp.float32)],
        in_specs=[pl.BlockSpec(memory_space=pl.ANY)] * 7 + [pl.BlockSpec(memory_space=pltpu.VMEM)] * 6,
        out_specs=[pl.BlockSpec(memory_space=pltpu.VMEM)] * 5,
        scratch_shapes=[
            pltpu.VMEM((8, 640), jnp.float32),
            pltpu.VMEM((8, 640), jnp.float32),
            pltpu.VMEM((2, 8, 640), jnp.float32),
            pltpu.SemaphoreType.DMA((SENDS,)),
            pltpu.SemaphoreType.DMA((SENDS,)),
            pltpu.SemaphoreType.DMA((7,)),
        ],
        compiler_params=pltpu.CompilerParams(
            collective_id=0, has_side_effects=True, vmem_limit_bytes=24 << 20
        ),
        name="gather_weights",
    )(*shards, *gain_shards)


NT = (((1,), (1,)), ((), ()))


def dot(left, right):
    return jnp.dot(left, right, preferred_element_type=jnp.float32)


def dot_nt(left, right):
    return lax.dot_general(left, right, NT, preferred_element_type=jnp.float32)


def block(i, size):
    return pl.ds(pl.multiple_of(i * size, size), size)


def each(count, body):
    def step(i, carry):
        body(i)
        return carry

    lax.fori_loop(0, count, step, 0)


def scale_of(y):
    return lax.rsqrt(jnp.mean(y * y, -1, keepdims=True) + epsilon)


def norm_back(dz, y, r, g):
    gained = g * dz
    return r * gained - y * (r * r * r) * jnp.mean(gained * y, -1, keepdims=True)


def fold(terms):
    rows, cols = terms.shape
    return jnp.sum(terms.reshape(rows // 8, 8, cols), 0)


def turn(v, cosine, sine):
    a, b = v[:, :128], v[:, 128:]
    return jnp.concatenate([a * cosine - b * sine, b * cosine + a * sine], 1)


def turn_back(v, cosine, sine):
    a, b = v[:, :128], v[:, 128:]
    return jnp.concatenate([a * cosine + b * sine, b * cosine - a * sine], 1)


def neighbour(s, f, by):
    return (lax.rem(s + 32 + by, 32), f)


def meet(s, f):
    barrier = pltpu.get_barrier_semaphore()
    for by in (1, -1):
        pl.semaphore_signal(barrier, inc=1, device_id=neighbour(s, f, by), device_id_type=MESH)
    pl.semaphore_wait(barrier, 2)


def forward_kernel(
    x, cot, cosine, sine, doc, gains, w_qkv, w_output, w_gate_up, w_down,
    layer_out, d_hidden, d_att, queries, pair, soft, raw, normed,
    grad_down, grad_gate_up, grad_output, gain_grads,
    turned_v, att, att_t, projected, hidden, normed_two, normed_two_t,
    product, slope, level, gate, up, down, d_down, d_proj, sums, send_sem, recv_sem,
):
    s, f = place()
    meet(s, f)
    lanes = lambda i: gains[pl.ds(i, 1), :]

    def norm_in(i):
        rows = block(i, 64)
        y = x[rows, :].astype(jnp.float32)
        normed[rows, :] = (y * scale_of(y) * lanes(0)).astype(jnp.bfloat16)

    each(8, norm_in)
    pair_raw = dot(normed[...], w_qkv[:, 1024:1536])
    raw[:, 1024:1280] = pair_raw[:, :256]
    pair[512:1024, 256:512] = pair_raw[:, 256:].astype(jnp.bfloat16)

    def shape_key(i):
        rows = block(i, 128)
        y = raw[rows, 1024:1280]
        y = turn(y * scale_of(y) * gains[pl.ds(4, 1), 256:512], cosine[rows, :], sine[rows, :])
        pair[pl.ds(pl.multiple_of(512 + i * 128, 128), 128), 0:256] = y.astype(jnp.bfloat16)

    each(4, shape_key)
    pass_on = pltpu.make_async_remote_copy(
        src_ref=pair.at[pl.ds(512, 512), :],
        dst_ref=pair.at[pl.ds(0, 512), :],
        send_sem=send_sem,
        recv_sem=recv_sem,
        device_id=neighbour(s, f, 1),
        device_id_type=MESH,
    )
    pass_on.start()

    def shape_query(h):
        raw[:, block(h, 256)] = dot(normed[...], w_qkv[:, block(h, 256)])

        def rows_of(i):
            rows = block(i, 128)
            y = raw[rows, block(h, 256)]
            y = turn(y * scale_of(y) * gains[pl.ds(4, 1), 0:256], cosine[rows, :], sine[rows, :])
            at = pl.ds(pl.multiple_of(h * 256 + lax.rem(i, 2) * 128, 128), 128)
            queries[lax.div(i, 2), at, :] = (y * 0.0625).astype(jnp.bfloat16)

        each(4, rows_of)

    each(4, shape_query)
    pass_on.wait_recv()
    turned_v[...] = pair[:, 256:512].T

    def attend(n):
        i, h = lax.div(n, 4), lax.rem(n, 4)
        keys = pl.ds(pl.multiple_of(i * 256, 256), 768)
        own = block(i, 256)
        gate[0:384, :] = dot_nt(pair[pl.ds(pl.multiple_of(i * 256, 256), 384), 0:256], queries[i, block(h, 256), :])
        gate[384:768, :] = dot_nt(
            pair[pl.ds(pl.multiple_of(i * 256 + 384, 128), 384), 0:256], queries[i, block(h, 256), :]
        )
        row = lax.broadcasted_iota(jnp.int32, (1, 256), 1) + i * 256
        lowest = jnp.maximum(row + 1, doc[0:1, own] - (s - 1) * 512)

        def weigh(c, total):
            rows = block(c, 128)
            key = lax.broadcasted_iota(jnp.int32, (128, 256), 0) + (i * 256 + c * 128)
            seen = (key >= lowest) & (key <= row + 512)
            p = jnp.where(seen, jnp.exp(gate[rows, :]), 0.0)
            gate[rows, :] = p
            return total + fold(p)

        total = lax.fori_loop(0, 6, weigh, jnp.zeros((8, 256), jnp.float32))
        inverse = 1.0 / jnp.sum(total, 0, keepdims=True)

        def settle(c):
            rows = block(c, 128)
            soft[i, rows, block(h, 256)] = (gate[rows, :] * inverse).astype(jnp.bfloat16)

        each(6, settle)
        mixed = dot(turned_v[:, keys], soft[i, :, block(h, 256)])
        att_t[block(h, 256), own] = mixed.astype(jnp.bfloat16)
        att[own, block(h, 256)] = mixed.T.astype(jnp.bfloat16)

    each(8, attend)
    projected[...] = dot(att[...], w_output[...])

    def mid(i):
        rows = block(i, 64)
        y = projected[rows, :]
        z = x[rows, :].astype(jnp.float32) + y * scale_of(y) * lanes(1)
        hidden[rows, :] = z
        normed_two[rows, :] = (z * scale_of(z) * lanes(2)).astype(jnp.bfloat16)

    each(8, mid)
    normed_two_t[...] = normed_two[...].T

    def feed(j):
        cols = block(j, 256)
        gate[0:512, :] = dot(normed_two[...], w_gate_up[:, cols])
        up[...] = dot(normed_two[...], w_gate_up[:, pl.ds(pl.multiple_of(2048 + j * 256, 256), 256)])

        def bend(i):
            rows = block(i, 64)
            g, u = gate[rows, :], up[rows, :]
            square = g * g
            t = jnp.tanh(0.7978845608028654 * g * (1.0 + 0.044715 * square))
            half = 0.5 * (1.0 + t)
            gelu = g * half
            rise = half + 0.5 * g * (1.0 - t * t) * (0.7978845608028654 * (1.0 + 0.134145 * square))
            product[rows, cols] = (gelu * u).astype(jnp.bfloat16)
            slope[rows, cols] = (rise * u).astype(jnp.bfloat16)
            level[rows, cols] = gelu.astype(jnp.bfloat16)

        each(8, bend)

    each(8, feed)
    down[...] = dot(product[...], w_down[...])
    sums[...] = jnp.zeros_like(sums)

    def end(i):
        rows = block(i, 64)
        y, dz = down[rows, :], cot[rows, :].astype(jnp.float32)
        r = scale_of(y)
        layer_out[rows, :] = (hidden[rows, :] + y * r * lanes(3)).astype(jnp.bfloat16)
        d_down[rows, :] = norm_back(dz, y, r, lanes(3)).astype(jnp.bfloat16)
        sums[2] += fold(dz * y * r)

    each(8, end)

    def feed_back(j):
        cols = block(j, 256)
        gate[0:512, :] = dot_nt(d_down[...], w_down[cols, :])
        grad_down[cols, :] = dot(product[:, cols].T, d_down[...]).astype(jnp.bfloat16)

        def bend(i):
            rows = block(i, 128)
            d = gate[rows, :]
            slope[rows, cols] = (d * slope[rows, cols].astype(jnp.float32)).astype(jnp.bfloat16)
            level[rows, cols] = (d * level[rows, cols].astype(jnp.float32)).astype(jnp.bfloat16)

        each(4, bend)
        grad_gate_up[:, cols] = dot(normed_two_t[...], slope[:, cols]).astype(jnp.bfloat16)
        grad_gate_up[:, pl.ds(pl.multiple_of(2048 + j * 256, 256), 256)] = dot(
            normed_two_t[...], level[:, cols]
        ).astype(jnp.bfloat16)

    each(8, feed_back)
    down[...] = dot_nt(slope[...], w_gate_up[:, 0:2048])
    down[...] += dot_nt(level[...], w_gate_up[:, 2048:4096])

    def mid_back(i):
        rows = block(i, 64)
        dz, y = down[rows, :], hidden[rows, :]
        r = scale_of(y)
        total = cot[rows, :].astype(jnp.float32) + norm_back(dz, y, r, lanes(2))
        sums[1] += fold(dz * y * r)
        d_hidden[rows, :] = total
        y = projected[rows, :]
        r = scale_of(y)
        d_proj[rows, :] = norm_back(total, y, r, lanes(1)).astype(jnp.bfloat16)
        sums[0] += fold(total * y * r)

    each(8, mid_back)

    def attend_back(h):
        grad_output[block(h, 256), :] = dot(att_t[block(h, 256), :], d_proj[...]).astype(jnp.bfloat16)
        back = dot_nt(d_proj[...], w_output[block(h, 256), :]).astype(jnp.bfloat16)
        d_att[0, block(h, 256), :] = back[:256, :]
        d_att[1, block(h, 256), :] = back[256:, :]

    each(4, attend_back)
    gain_grads[...] = jnp.zeros_like(gain_grads)
    for i in range(3):
        gain_grads[pl.ds(i + 1, 1), :] = jnp.sum(sums[i], 0, keepdims=True)
    pass_on.wait_send()


def forward(x, cot, cosine, sine, doc, gains, w_qkv, w_output, w_gate_up, w_down):
    b, f32 = jnp.bfloat16, jnp.float32
    outs = [
        ((512, 640), b), ((512, 640), f32), ((2, 1024, 256), b), ((2, 1024, 256), b), ((1024, 512), b),
        ((2, 768, 1024), b), ((512, 1280), f32), ((512, 640), b),
        ((2048, 640), b), ((640, 4096), b), ((1024, 640), b), ((8, 640), f32),
    ]
    scratch = [
        ((256, 1024), b), ((512, 1024), b), ((1024, 512), b), ((512, 640), f32), ((512, 640), f32),
        ((512, 640), b), ((640, 512), b), ((512, 2048), b), ((512, 2048), b), ((512, 2048), b),
        ((768, 256), f32), ((512, 256), f32), ((512, 640), f32), ((512, 640), b), ((512, 640), b),
        ((3, 8, 640), f32),
    ]
    return pl.pallas_call(
        forward_kernel,
        out_shape=[jax.ShapeDtypeStruct(*o) for o in outs],
        in_specs=[pl.BlockSpec(memory_space=pltpu.VMEM)] * 10,
        out_specs=[pl.BlockSpec(memory_space=pltpu.VMEM)] * len(outs),
        scratch_shapes=[pltpu.VMEM(*o) for o in scratch] + [pltpu.SemaphoreType.DMA] * 2,
        compiler_params=pltpu.CompilerParams(
            collective_id=2, has_side_effects=True, vmem_limit_bytes=60 << 20
        ),
        name="forward",
    )(x, cot, cosine, sine, doc, gains, w_qkv, w_output, w_gate_up, w_down)


def backward_kernel(
    x, d_hidden, cosine, sine, gains, w_qkv, d_att, queries, pair, soft, raw, normed, gain_grads,
    input_grad, grad_qkv, gain_sums,
    turned_k, d_soft, d_scores, d_queries, d_pair, first, other, d_raw, normed_t, d_normed,
    sums, head_sums, send_sem, recv_sem,
):
    s, f = place()
    meet(s, f)
    turned_k[...] = pair[:, 0:256].T
    d_pair[...] = jnp.zeros_like(d_pair)
    sums[...] = jnp.zeros_like(sums)
    head_sums[...] = jnp.zeros_like(head_sums)

    def attend_back(i):
        keys = pl.ds(pl.multiple_of(i * 256, 256), 768)

        def one_head(h):
            cols = block(h, 256)
            d_soft[0:384, :] = dot_nt(pair[pl.ds(pl.multiple_of(i * 256, 256), 384), 256:512], d_att[i, cols, :])
            d_soft[384:768, :] = dot_nt(
                pair[pl.ds(pl.multiple_of(i * 256 + 384, 128), 384), 256:512], d_att[i, cols, :]
            )

            def weigh(c, total):
                rows = block(c, 128)
                p = soft[i, rows, cols].astype(jnp.float32) * d_soft[rows, :]
                return total + fold(p)

            total = lax.fori_loop(0, 6, weigh, jnp.zeros((8, 256), jnp.float32))
            inner = jnp.sum(total, 0, keepdims=True)

            def settle(c):
                rows = block(c, 128)
                p = soft[i, rows, cols].astype(jnp.float32)
                d_scores[rows, cols] = (p * (d_soft[rows, :] - inner)).astype(jnp.bfloat16)

            each(6, settle)
            mixed = dot(turned_k[:, keys], d_scores[:, cols]) * 0.0625
            d_queries[block(i, 256), cols] = mixed.T

        each(4, one_head)
        for half in range(2):
            at = pl.ds(pl.multiple_of(i * 256 + half * 384, 128), 384)
            part = pl.ds(half * 384, 384)
            d_pair[at, 0:256] += dot(d_scores[part, :], queries[i])
            d_pair[at, 256:512] += dot(soft[i, part, :], d_att[i])

    each(2, attend_back)
    first[...] = d_pair[0:512, :].astype(jnp.bfloat16)
    pass_back = pltpu.make_async_remote_copy(
        src_ref=first,
        dst_ref=other,
        send_sem=send_sem,
        recv_sem=recv_sem,
        device_id=neighbour(s, f, -1),
        device_id_type=MESH,
    )
    pass_back.start()
    normed_t[...] = normed[...].T

    def query_back(n):
        h, i = lax.div(n, 4), lax.rem(n, 4)
        rows, cols = block(i, 128), block(h, 256)
        dz = turn_back(d_queries[rows, cols], cosine[rows, :], sine[rows, :])
        y = raw[rows, cols]
        r = scale_of(y)
        d_raw[rows, cols] = norm_back(dz, y, r, gains[pl.ds(4, 1), 0:256]).astype(jnp.bfloat16)
        head_sums[0] += fold(dz * y * r)

    each(16, query_back)
    pass_back.wait_recv()

    def key_back(i):
        rows = block(i, 128)
        own = pl.ds(pl.multiple_of(512 + i * 128, 128), 128)
        dz = d_pair[own, 0:256] + other[rows, 0:256].astype(jnp.float32)
        dz = turn_back(dz, cosine[rows, :], sine[rows, :])
        y = raw[rows, 1024:1280]
        r = scale_of(y)
        d_raw[rows, 1024:1280] = norm_back(dz, y, r, gains[pl.ds(4, 1), 256:512]).astype(jnp.bfloat16)
        head_sums[1] += fold(dz * y * r)
        d_value = d_pair[own, 256:512] + other[rows, 256:512].astype(jnp.float32)
        d_raw[rows, 1280:1536] = d_value.astype(jnp.bfloat16)

    each(4, key_back)

    def weigh_in(j):
        cols = block(j, 256)
        grad_qkv[:, cols] = dot(normed_t[...], d_raw[:, cols]).astype(jnp.bfloat16)

    each(6, weigh_in)
    d_normed[...] = dot_nt(d_raw[...], w_qkv[...])

    def norm_in_back(i):
        rows = block(i, 64)
        y, dz = x[rows, :].astype(jnp.float32), d_normed[rows, :]
        r = scale_of(y)
        input_grad[rows, :] = d_hidden[rows, :] + norm_back(dz, y, r, lanes_in)
        sums[...] += fold(dz * y * r)

    lanes_in = gains[pl.ds(0, 1), :]
    each(8, norm_in_back)
    gain_sums[...] = gain_grads[...]
    gain_sums[pl.ds(0, 1), :] = jnp.sum(sums[...], 0, keepdims=True)
    gain_sums[pl.ds(4, 1), 0:256] = jnp.sum(head_sums[0], 0, keepdims=True)
    gain_sums[pl.ds(4, 1), 256:512] = jnp.sum(head_sums[1], 0, keepdims=True)
    pass_back.wait_send()


def backward(*args):
    b, f32 = jnp.bfloat16, jnp.float32
    outs = [((512, 640), f32), ((640, 1536), b), ((8, 640), f32)]
    scratch = [
        ((256, 1024), b), ((768, 256), f32), ((768, 1024), b), ((512, 1024), f32), ((1024, 512), f32),
        ((512, 512), b), ((512, 512), b), ((512, 1536), b), ((640, 512), b), ((512, 640), f32),
        ((8, 640), f32), ((2, 8, 256), f32),
    ]
    return pl.pallas_call(
        backward_kernel,
        out_shape=[jax.ShapeDtypeStruct(*o) for o in outs],
        in_specs=[pl.BlockSpec(memory_space=pltpu.VMEM)] * len(args),
        out_specs=[pl.BlockSpec(memory_space=pltpu.VMEM)] * len(outs),
        scratch_shapes=[pltpu.VMEM(*o) for o in scratch] + [pltpu.SemaphoreType.DMA] * 2,
        compiler_params=pltpu.CompilerParams(
            collective_id=3, has_side_effects=True, vmem_limit_bytes=60 << 20
        ),
        name="backward",
    )(*args)


def rope_tables(positions):
    frequency = rope_base ** (-(jnp.arange(128, dtype=jnp.float32) * (2.0 / 256)))
    angles = positions[:, None] * frequency[None, :]
    return jnp.cos(angles), jnp.sin(angles)


def body(
    inputs,
    doc_start,
    w_query,
    w_key,
    w_value,
    w_output,
    w_gate,
    w_up,
    w_down,
    norm_attn_in,
    norm_attn_out,
    norm_ffn_in,
    norm_ffn_out,
    norm_query,
    norm_key,
    cotangent,
):
    row_index = lax.axis_index("seq") * 512 + jnp.arange(512, dtype=jnp.int32)
    cosine, sine = rope_tables((row_index - doc_start[0]).astype(jnp.float32))
    w_qkv, w_out, w_gate_up, w_dn, gains = gather_weights(
        (w_query, w_key, w_value, w_output, w_gate, w_up, w_down),
        [
            g.reshape(1, -1)
            for g in (norm_attn_in, norm_attn_out, norm_ffn_in, norm_ffn_out, norm_query, norm_key)
        ],
    )
    (
        layer_out, d_hidden, d_att, queries, pair, soft, raw, normed,
        grad_down, grad_gate_up, grad_output, gain_grads,
    ) = forward(
        inputs[0], cotangent[0], cosine, sine, doc_start, gains, w_qkv, w_out, w_gate_up, w_dn
    )
    input_grad, grad_qkv, gain_grads = backward(
        inputs[0], d_hidden, cosine, sine, gains, w_qkv, d_att, queries, pair, soft, raw, normed, gain_grads
    )
    down, gate_up_share, output, qkv, gain_grads = reduce_gradients(
        [
            grad.reshape(2, 2, grad.shape[0] // 4, grad.shape[1])
            for grad in (grad_down, grad_gate_up, grad_output, grad_qkv)
        ],
        gain_grads,
    )
    at = lax.axis_index("fsdp")
    wide = lax.dynamic_slice(gain_grads, (0, at * 160), (4, 160))
    return (
        layer_out[None],
        input_grad[None],
        qkv[:, :1024].astype(jnp.float32),
        qkv[:, 1024:1280].astype(jnp.float32),
        qkv[:, 1280:].astype(jnp.float32),
        output.astype(jnp.float32),
        gate_up_share[:, :2048].astype(jnp.float32),
        gate_up_share[:, 2048:].astype(jnp.float32),
        down.astype(jnp.float32),
        wide[0],
        wide[1],
        wide[2],
        wide[3],
        lax.dynamic_slice(gain_grads[4, :256], (at * 64,), (64,)),
        lax.dynamic_slice(gain_grads[4, 256:512], (at * 64,), (64,)),
    )


def solution(mesh):
    in_specs = (
        P("fsdp", "seq", None),
        P("fsdp", "seq"),
        P("fsdp", None),
        P("fsdp", None),
        P("fsdp", None),
        P("fsdp", None),
        P("fsdp", None),
        P("fsdp", None),
        P("fsdp", None),
        P("fsdp"),
        P("fsdp"),
        P("fsdp"),
        P("fsdp"),
        P("fsdp"),
        P("fsdp"),
        P("fsdp", "seq", None),
    )
    out_specs = (
        P("fsdp", "seq", None),
        P("fsdp", "seq", None),
        P("fsdp", None),
        P("fsdp", None),
        P("fsdp", None),
        P("fsdp", None),
        P("fsdp", None),
        P("fsdp", None),
        P("fsdp", None),
        P("fsdp"),
        P("fsdp"),
        P("fsdp"),
        P("fsdp"),
        P("fsdp"),
        P("fsdp"),
    )
    return jax.shard_map(body, mesh=mesh, in_specs=in_specs, out_specs=out_specs, check_vma=False)
```

```python
import jax
import jax.numpy as jnp
from jax import lax
from jax.experimental import pallas as pl
from jax.experimental.pallas import tpu as pltpu
from jax.sharding import PartitionSpec as P

epsilon = 1e-06
rope_base = 10000.0


MESH = pl.DeviceIdType.MESH
DIMS = ("C", "X1", "X0", "Y1", "Y0", "Z1", "Z0")


def place():
    return lax.axis_index("seq"), lax.axis_index("fsdp")


def bit_of(dim, s, f):
    if dim == "C":
        return lax.rem(f, 2)
    if dim == "X1":
        return lax.div(f, 2)
    if dim == "X0":
        return lax.rem(lax.rem(lax.div(s, 4), 2) + lax.div(f, 2), 2)
    at = lax.rem(s, 4) if dim[0] == "Y" else lax.div(s, 8)
    if dim[1] == "1":
        return lax.div(at, 2)
    return lax.rem(lax.rem(at, 2) + lax.div(at, 2), 2)


def partner(dim, s, f):
    if dim == "C":
        return (s, f + 1 - 2 * lax.rem(f, 2))
    step = 1 - 2 * lax.rem(lax.div(s, 4), 2)
    if dim == "X0":
        return (s + 4 * step, f)
    if dim == "X1":
        return (s + 4 * step, f + 2 - 4 * lax.div(f, 2))
    at, scale = (lax.rem(s, 4), 1) if dim[0] == "Y" else (lax.div(s, 8), 8)
    if dim[1] == "1":
        return (s + scale * (3 - 2 * at), f)
    return (s + scale * (1 - 2 * lax.rem(at, 2)), f)


def neighbour(s, f, by):
    return (lax.rem(s + 32 + by, 32), f)


def greet(s, f):
    barrier = pltpu.get_barrier_semaphore()
    for dim in DIMS:
        pl.semaphore_signal(barrier, inc=1, device_id=partner(dim, s, f), device_id_type=MESH)
    for by in (1, -1):
        pl.semaphore_signal(barrier, inc=1, device_id=neighbour(s, f, by), device_id_type=MESH)
    pl.semaphore_wait(barrier, len(DIMS) + 2)


def span(start, size, tile):
    if isinstance(start, int):
        return pl.ds(start, size)
    return pl.ds(pl.multiple_of(start, tile), size)


class Region:
    def __init__(self, q, r, c):
        self.q, self.r, self.c = q, r, c

    def of(self, ref):
        return ref.at[pl.ds(*self.q), span(*self.r, 16), span(*self.c, 128)]

    def flat(self, ref, r0=0, c0=0):
        return ref.at[span(self.r[0] + r0, self.r[1], 16), span(self.c[0] + c0, self.c[1], 128)]

    def halved(self, axis, bit):
        start, size = getattr(self, axis)
        half = size // 2
        mine = Region(self.q, self.r, self.c)
        setattr(mine, axis, (start + bit * half, half))
        theirs = Region(self.q, self.r, self.c)
        setattr(theirs, axis, (start + (1 - bit) * half, half))
        return mine, theirs

    @property
    def shape(self):
        return (self.q[1], self.r[1], self.c[1])


def rows_per_step(rows, cols):
    best = 16
    for n in (32, 48, 64, 80, 96, 128, 160):
        if rows % n == 0 and n * cols <= 48 * 2048:
            best = n
    return best


def add_blocks(out, first, second, shape):
    quarters, rows, cols = shape
    step = rows_per_step(rows, cols)
    for q in range(quarters):

        def body(i, carry, q=q):
            at = i * step
            ref, index = out(q, at, step)
            ref_a, index_a = first(q, at, step)
            ref_b, index_b = second(q, at, step)
            ref[index] = ref_a[index_a] + ref_b[index_b]
            return carry

        lax.fori_loop(0, rows // step, body, 0)


def view(ref, region):
    def pick(q, at, step):
        rows = span(region.r[0] + at, step, 16)
        return ref, (region.q[0] + q, rows, span(region.c[0], region.c[1], 128))

    return pick


def flat_view(ref, region, r0, c0):
    def pick(q, at, step):
        return ref, (span(region.r[0] + r0 + at, step, 16), span(region.c[0] + c0, region.c[1], 128))

    return pick


def whole_view(ref):
    def pick(q, at, step):
        return ref, (q, span(at, step, 16), slice(None))

    return pick


ORDERS = (
    ("X1", "Y1", "Z1", "X0", "Y0", "Z0"),
    ("Y1", "Z1", "X0", "X1", "Y0", "Z0"),
    ("Z1", "X0", "Y0", "X1", "Z0", "Y1"),
    ("X0", "Y0", "Z0", "X1", "Y1", "Z1"),
    ("Y0", "Z0", "X1", "Y1", "Z1", "X0"),
    ("Z0", "X1", "Y1", "Z1", "X0", "Y0"),
)
PARTS = (
    (0, 0, 384, 0, 640, ORDERS[0], "rrr"),
    (1, 0, 160, 0, 1536, ORDERS[1], "ccr"),
    (1, 0, 160, 1536, 1536, ORDERS[2], "ccr"),
    (1, 0, 160, 3072, 1024, ORDERS[3], "ccc"),
    (0, 384, 128, 0, 640, ORDERS[5], "rrr"),
    (2, 0, 256, 0, 640, ORDERS[4], "rrr"),
    (3, 0, 160, 0, 512, ORDERS[5], "ccr"),
    (3, 0, 160, 512, 512, ORDERS[3], "ccr"),
    (3, 0, 160, 1024, 512, ORDERS[1], "ccr"),
)
EARLY, LATE = tuple(range(6)), (6, 7, 8)
SHARES = ((512, 640), (160, 4096), (256, 640), (160, 1536))


def part_shapes(part):
    _, _, rows, _, cols, order, splits = part
    shapes, shape, cut = [], [2, rows, cols], iter(splits)
    for dim in order[:4]:
        axis = 0 if dim == "X1" else {"r": 1, "c": 2}[next(cut)]
        shape[axis] //= 2
        shapes.append(tuple(shape))
    return shapes


class Reduce:
    STAGES = 10

    def __init__(self, s, f, grads, totals, scratch, send_sem, recv_sem, local_sem):
        self.s, self.f, self.grads, self.totals = s, f, grads, totals
        self.send_sem, self.recv_sem, self.local_sem = send_sem, recv_sem, local_sem
        self.acc, self.from_core, self.inbox, self.extra = [], [], [], []
        for _ in PARTS:
            self.acc.append(scratch.pop(0))
            self.from_core.append(scratch.pop(0))
            self.inbox.append([scratch.pop(0) for _ in range(4)])
            self.extra.append([scratch.pop(0) for _ in range(3)])
        n = len(PARTS)
        self.pending, self.count = [], 0
        self.flights, self.loads, self.where = [None] * n, [None] * n, [None] * n
        self.cuts = [iter(part[6]) for part in PARTS]
        self.trail, self.stage = [[] for _ in PARTS], [0] * n

    def send(self, src, dst, dim):
        copy = pltpu.make_async_remote_copy(
            src_ref=src,
            dst_ref=dst,
            send_sem=self.send_sem.at[self.count],
            recv_sem=self.recv_sem.at[self.count],
            device_id=partner(dim, self.s, self.f),
            device_id_type=MESH,
        )
        copy.start()
        self.count += 1
        self.pending.append(copy)
        return copy

    def begin(self, p):
        tensor, r0, rows, c0, cols, _, _ = PARTS[p]
        core = bit_of("C", self.s, self.f)
        grad = self.grads[tensor]
        if len(grad.shape) == 2:
            deep = grad.shape[0] // 4
            pick = lambda high, low: grad.at[span((2 * high + low) * deep + r0, rows, 16), pl.ds(c0, cols)]
            self.flights[p] = [
                self.send(pick(high, 1 - core), self.from_core[p].at[high], "C") for high in range(2)
            ]
            self.mine = getattr(self, "mine", {})
            self.mine[p] = [(span((2 * high + core) * deep + r0, rows, 16)) for high in range(2)]
        else:
            block_ = (pl.ds(0, 2), pl.ds(r0, rows), pl.ds(c0, cols))
            self.flights[p] = [
                self.send(grad.at[block_[0], 1 - core, block_[1], block_[2]], self.from_core[p], "C")
            ]
            self.loads[p] = pltpu.make_async_copy(
                grad.at[block_[0], core, block_[1], block_[2]], self.acc[p], self.local_sem.at[p]
            )
            self.loads[p].start()
        self.where[p] = Region((0, 2), (0, rows), (0, cols))

    def advance(self, p):
        part, stage, s, f = PARTS[p], self.stage[p], self.s, self.f
        tensor, r0, rows, c0, cols, order, _ = part
        acc, where, extra = self.acc[p], self.where[p], self.extra[p]
        self.stage[p] += 1
        for flight in self.flights[p]:
            flight.wait_recv()
        if stage < 5:
            if stage == 0 and self.loads[p] is None:
                grad, deep = self.grads[tensor], self.mine[p]
                for high in range(2):
                    acc[high] = grad[deep[high], pl.ds(c0, cols)] + self.from_core[p][high]
            else:
                if stage == 0:
                    self.loads[p].wait()
                source = self.from_core[p] if stage == 0 else self.inbox[p][stage - 1]
                add_blocks(view(acc, where), view(acc, where), whole_view(source), where.shape)
            if stage == 4:
                self.flights[p] = [self.send(where.of(acc), extra[0], order[4])]
                return
            dim = order[stage]
            axis = "q" if dim == "X1" else next(self.cuts[p])
            self.trail[p].append((dim, axis))
            self.where[p], theirs = where.halved(axis, bit_of(dim, s, f))
            self.flights[p] = [self.send(theirs.of(acc), self.inbox[p][stage], dim)]
        elif stage == 5:
            add_blocks(whole_view(extra[1]), view(acc, where), whole_view(extra[0]), where.shape)
            self.flights[p] = [self.send(extra[1], extra[2], order[5])]
        elif stage == 6:
            total = self.totals[tensor]
            add_blocks(flat_view(total, where, r0, c0), whole_view(extra[1]), whole_view(extra[2]), where.shape)
            self.trail[p] = [move for move in reversed(self.trail[p]) if move[1] != "q"]
            self.spread(p)
        else:
            dim, axis = self.trail[p].pop(0)
            start, size = getattr(where, axis)
            setattr(where, axis, (start - bit_of(dim, s, f) * size, 2 * size))
            if self.trail[p]:
                self.spread(p)

    def spread(self, p):
        tensor, r0, _, c0, _, _, _ = PARTS[p]
        region = self.where[p].flat(self.totals[tensor], r0, c0)
        self.flights[p] = [self.send(region, region, self.trail[p][0][0])]


def reduce_scratch():
    scratch, sends = [], 7
    for part in PARTS:
        shapes = part_shapes(part)
        scratch += [pltpu.VMEM((2, part[2], part[4]), jnp.bfloat16)] * 2
        scratch += [pltpu.VMEM(shape, jnp.bfloat16) for shape in shapes]
        scratch += [pltpu.VMEM(shapes[-1], jnp.bfloat16)] * 3
        sends += 11
    return scratch, sends


PIECES = (
    (0, 0, 0, 160, 1024, "X0", "Z0", "c"),
    (1, 0, 1024, 160, 256, "Z0", "X0", "c"),
    (2, 0, 1280, 160, 256, "Z0", "X0", "c"),
    (3, 1, 0, 256, 640, "Y0", "X0", "r"),
    (4, 2, 0, 160, 2048, "Z1", "Y1", "c"),
    (5, 2, 2048, 160, 2048, "Z0", "Y0", "c"),
    (6, 3, 0, 512, 640, "Y1", "Z1", "r"),
)
WHOLES = ((640, 1536), (1024, 640), (640, 4096), (2048, 640))


def own_gains(gain_shards, gain_own, f):
    gain_own[...] = jnp.zeros_like(gain_own)
    for i, shard in enumerate(gain_shards):
        share = shard.shape[1]
        shift = lax.broadcasted_iota(jnp.int32, (share, 4 * share), 1) - lax.broadcasted_iota(
            jnp.int32, (share, 4 * share), 0
        )
        chosen = jnp.where(shift == share * f, 1.0, 0.0).astype(jnp.bfloat16)
        row = jnp.dot(shard[...], chosen, preferred_element_type=jnp.float32)
        if i < 4:
            gain_own[i : i + 1, :] = row
        else:
            gain_own[4:5, 256 * (i - 4) : 256 * (i - 3)] = row


class Gather:
    def __init__(self, s, f, shards, outs, send_sem, recv_sem, local_sem):
        self.s, self.f, self.shards, self.outs = s, f, shards, outs
        self.send_sem, self.recv_sem, self.local_sem = send_sem, recv_sem, local_sem
        self.copies, self.count = [], 0
        self.core, high = bit_of("C", s, f), bit_of("X1", s, f)
        self.far = 2 * (1 - high) + self.core
        self.flights, self.sides, self.loads = {}, {}, {}

    def send(self, src, dst, dim):
        copy = pltpu.make_async_remote_copy(
            src_ref=src,
            dst_ref=dst,
            send_sem=self.send_sem.at[self.count],
            recv_sem=self.recv_sem.at[self.count],
            device_id=partner(dim, self.s, self.f),
            device_id_type=MESH,
        )
        copy.start()
        self.count += 1
        self.copies.append(copy)
        return copy

    def boxes(self, piece, bit_one, bit_two):
        _, _, c0, rows, cols, _, _, cut = piece
        half = rows // 2
        if cut == "c":
            quarter = ((bit_two * half, half), (bit_one * (cols // 2), cols // 2))
        else:
            quarter = ((bit_two * half + bit_one * (half // 2), half // 2), (0, cols))
        return quarter, ((bit_two * half, half), (0, cols))

    def spot(self, piece, share, box):
        (r, nr), (c, nc) = box
        return self.outs[piece[1]].at[span(r + share * piece[3], nr, 16), span(c + piece[2], nc, 128)]

    def begin(self, pieces):
        for i in pieces:
            piece = PIECES[i]
            (r, nr), (c, nc) = quarter = self.boxes(
                piece, bit_of(piece[5], self.s, self.f), bit_of(piece[6], self.s, self.f)
            )[0]
            src = self.shards[i].at[span(r, nr, 16), span(c, nc, 128)]
            self.flights[i] = self.send(src, self.spot(piece, self.f, quarter), "X1")
        for i in pieces:
            piece = PIECES[i]
            dst = self.spot(piece, self.f, ((0, piece[3]), (0, piece[4])))
            self.sides[i] = [self.send(self.shards[i], dst, "C")]
            self.loads[i] = pltpu.make_async_copy(self.shards[i], dst, self.local_sem.at[i])
            self.loads[i].start()

    def step(self, i, number):
        piece, s, f, far = PIECES[i], self.s, self.f, self.far
        one, two = bit_of(piece[5], s, f), bit_of(piece[6], s, f)
        quarter, half = self.boxes(piece, one, two)
        self.flights[i].wait_recv()
        if number == 0:
            here = self.spot(piece, far, quarter)
            self.flights[i] = self.send(here, here, piece[5])
        elif number == 1:
            here = self.spot(piece, far, half)
            self.flights[i] = self.send(here, here, piece[6])
            here = self.spot(piece, far, self.boxes(piece, 1 - one, two)[0])
        else:
            here = self.spot(piece, far, self.boxes(piece, one, 1 - two)[1])
        self.sides[i].append(self.send(here, here, "C"))

    def arrive(self, i):
        for copy in self.sides[i]:
            copy.wait_recv()
        self.loads[i].wait()


SENDS = 7 * len(PIECES) + 2


NT = (((1,), (1,)), ((), ()))


def dot(left, right):
    return jnp.dot(left, right, preferred_element_type=jnp.float32)


def dot_nt(left, right):
    return lax.dot_general(left, right, NT, preferred_element_type=jnp.float32)


def block(i, size):
    return pl.ds(pl.multiple_of(i * size, size), size)


def each(count, body):
    def step(i, carry):
        body(i)
        return carry

    lax.fori_loop(0, count, step, 0)


def scale_of(y):
    return lax.rsqrt(jnp.mean(y * y, -1, keepdims=True) + epsilon)


def norm_back(dz, y, r, g):
    gained = g * dz
    return r * gained - y * (r * r * r) * jnp.mean(gained * y, -1, keepdims=True)


def fold(terms):
    rows, cols = terms.shape
    return jnp.sum(terms.reshape(rows // 8, 8, cols), 0)


def turn(v, cosine, sine):
    a, b = v[:, :128], v[:, 128:]
    return jnp.concatenate([a * cosine - b * sine, b * cosine + a * sine], 1)


def turn_back(v, cosine, sine):
    a, b = v[:, :128], v[:, 128:]
    return jnp.concatenate([a * cosine + b * sine, b * cosine - a * sine], 1)


def forward_kernel(*refs):
    x_far, cot_far, cosine, sine, doc = refs[:5]
    shards, gain_shards = refs[5:12], refs[12:18]
    outs, gains, gain_grads, weight = refs[18:31], refs[31], refs[32], refs[33]
    (
        x, cot, d_hidden, d_att, d_att_scaled, queries, pair, soft, raw, normed,
        grad_down, grad_gate_up, grad_output, w_qkv, w_output, w_gate_up, w_down,
        turned_v, att, att_t, projected, hidden, normed_two, normed_two_t,
        product, slope, level, gate, up, down, d_down, d_proj, layer_out, sums, weight_sums,
        gain_own, gain_mid, gain_in,
        send_sem, recv_sem, local_sem, out_sem, in_sem, pair_sem,
    ) = refs[34:]
    s, f = place()
    greet(s, f)
    gather = Gather(s, f, shards, (w_qkv, w_output, w_gate_up, w_down), send_sem, recv_sem, local_sem)
    gather.begin((1, 2, 0))
    load_x = pltpu.make_async_copy(x_far, x, in_sem.at[0])
    load_x.start()
    load_cot = pltpu.make_async_copy(cot_far, cot, in_sem.at[1])
    load_cot.start()
    own_gains(gain_shards, gain_own, f)
    flight = gather.send(gain_own, gain_in.at[0], "C")
    lanes = lambda i: gains[pl.ds(i, 1), :]
    written = []

    def write(src, number):
        copy = pltpu.make_async_copy(src, outs[number], out_sem.at[number])
        copy.start()
        written.append(copy)

    flight.wait_recv()
    gain_mid[...] = gain_own[...] + gain_in[0]
    flight = gather.send(gain_mid, gain_in.at[1], "X1")
    for i in (1, 2, 0):
        gather.step(i, 0)
    gather.begin((3, 4, 5, 6))
    for i in (1, 2, 0):
        gather.step(i, 1)
    flight.wait_recv()
    gains[...] = gain_mid[...] + gain_in[1]
    load_x.wait()

    def norm_in(i):
        rows = block(i, 64)
        y = x[rows, :].astype(jnp.float32)
        normed[rows, :] = (y * scale_of(y) * lanes(0)).astype(jnp.bfloat16)

    each(8, norm_in)
    write(normed, 7)
    for i in (1, 2, 0):
        gather.step(i, 2)
    gather.arrive(1)
    gather.arrive(2)
    pair_raw = dot(normed[...], w_qkv[:, 1024:1536])
    raw[:, 1024:1280] = pair_raw[:, :256]
    pair[512:1024, 256:512] = pair_raw[:, 256:].astype(jnp.bfloat16)

    def shape_key(i):
        rows = block(i, 128)
        y = raw[rows, 1024:1280]
        y = turn(y * scale_of(y) * gains[pl.ds(4, 1), 256:512], cosine[rows, :], sine[rows, :])
        pair[pl.ds(pl.multiple_of(512 + i * 128, 128), 128), 0:256] = y.astype(jnp.bfloat16)

    each(4, shape_key)
    pass_on = pltpu.make_async_remote_copy(
        src_ref=pair.at[pl.ds(512, 512), :],
        dst_ref=pair.at[pl.ds(0, 512), :],
        send_sem=pair_sem.at[0],
        recv_sem=pair_sem.at[1],
        device_id=neighbour(s, f, 1),
        device_id_type=MESH,
    )
    pass_on.start()
    gather.arrive(0)
    write(w_qkv, 11)

    def shape_query(h):
        raw[:, block(h, 256)] = dot(normed[...], w_qkv[:, block(h, 256)])

        def rows_of(i):
            rows = block(i, 128)
            y = raw[rows, block(h, 256)]
            y = turn(y * scale_of(y) * gains[pl.ds(4, 1), 0:256], cosine[rows, :], sine[rows, :])
            at = pl.ds(pl.multiple_of(h * 256 + lax.rem(i, 2) * 128, 128), 128)
            queries[lax.div(i, 2), at, :] = (y * 0.0625).astype(jnp.bfloat16)

        each(4, rows_of)

    each(4, shape_query)
    write(raw, 6)
    write(queries, 3)
    for i in (3, 4, 5, 6):
        gather.step(i, 0)
    row = [lax.broadcasted_iota(jnp.int32, (1, 256), 1) + i * 256 for i in range(2)]
    lowest = [
        jnp.maximum(row[i] + 1, doc[0:1, 256 * i : 256 * (i + 1)] - (s - 1) * 512) for i in range(2)
    ]

    def weigh(i, h, first, count):
        total = None
        query = queries[i, block(h, 256), :]
        for c in range(first, first + count, 2):
            low = i * 256 + c * 128
            score = dot_nt(pair[low : low + 256, 0:256], query)
            key = lax.broadcasted_iota(jnp.int32, (256, 256), 0) + low
            seen = (key >= lowest[i]) & (key <= row[i] + 512)
            p = jnp.where(seen, jnp.exp(score), 0.0)
            soft[i, c * 128 : c * 128 + 256, block(h, 256)] = p.astype(jnp.bfloat16)
            total = fold(p) if total is None else total + fold(p)
        return total

    for i, first, count in ((0, 4, 2), (1, 2, 4)):

        def own_keys(h, i=i, first=first, count=count):
            weight_sums[i, h] = weigh(i, h, first, count)

        each(4, own_keys)
    for i in (3, 4, 5, 6):
        gather.step(i, 1)
    pass_on.wait_recv()
    write(pair, 4)
    turned_v[...] = pair[:, 256:512].T
    for i, first, count in ((0, 0, 4), (1, 0, 2)):

        def attend(h, i=i, first=first, count=count):
            total = weight_sums[i, h] + weigh(i, h, first, count)
            inverse = 1.0 / jnp.sum(total, 0, keepdims=True)
            weight[pl.ds(4 * i + h, 1), :] = inverse
            mixed = dot(turned_v[:, 256 * i : 256 * i + 768], soft[i, :, block(h, 256)]) * inverse
            att_t[block(h, 256), 256 * i : 256 * (i + 1)] = mixed.astype(jnp.bfloat16)
            att[256 * i : 256 * (i + 1), block(h, 256)] = mixed.T.astype(jnp.bfloat16)

        each(4, attend)
    write(soft, 5)
    for i in (3, 4, 5, 6):
        gather.step(i, 2)
    gather.arrive(3)
    projected[...] = dot(att[...], w_output[...])

    def mid(i):
        rows = block(i, 64)
        y = projected[rows, :]
        z = x[rows, :].astype(jnp.float32) + y * scale_of(y) * lanes(1)
        hidden[rows, :] = z
        normed_two[rows, :] = (z * scale_of(z) * lanes(2)).astype(jnp.bfloat16)

    each(8, mid)
    normed_two_t[...] = normed_two[...].T
    gather.arrive(4)
    gather.arrive(5)

    def feed(j):
        cols = block(j, 256)
        gate[...] = dot(normed_two[...], w_gate_up[:, cols])
        up[...] = dot(normed_two[...], w_gate_up[:, pl.ds(pl.multiple_of(2048 + j * 256, 256), 256)])

        def bend(i):
            rows = block(i, 64)
            g, u = gate[rows, :], up[rows, :]
            square = g * g
            t = jnp.tanh(0.7978845608028654 * g * (1.0 + 0.044715 * square))
            half = 0.5 * (1.0 + t)
            gelu = g * half
            rise = half + 0.5 * g * (1.0 - t * t) * (0.7978845608028654 * (1.0 + 0.134145 * square))
            product[rows, cols] = (gelu * u).astype(jnp.bfloat16)
            slope[rows, cols] = (rise * u).astype(jnp.bfloat16)
            level[rows, cols] = gelu.astype(jnp.bfloat16)

        each(8, bend)

    each(8, feed)
    gather.arrive(6)
    down[...] = dot(product[...], w_down[...])
    sums[...] = jnp.zeros_like(sums)
    load_cot.wait()

    def end(i):
        rows = block(i, 64)
        y, dz = down[rows, :], cot[rows, :].astype(jnp.float32)
        r = scale_of(y)
        layer_out[rows, :] = (hidden[rows, :] + y * r * lanes(3)).astype(jnp.bfloat16)
        d_down[rows, :] = norm_back(dz, y, r, lanes(3)).astype(jnp.bfloat16)
        sums[2] += fold(dz * y * r)

    each(8, end)
    write(layer_out, 0)

    def feed_back(j):
        cols = block(j, 256)
        gate[...] = dot_nt(d_down[...], w_down[cols, :])
        grad_down[cols, :] = dot(product[:, cols].T, d_down[...]).astype(jnp.bfloat16)

        def bend(i):
            rows = block(i, 128)
            d = gate[rows, :]
            slope[rows, cols] = (d * slope[rows, cols].astype(jnp.float32)).astype(jnp.bfloat16)
            level[rows, cols] = (d * level[rows, cols].astype(jnp.float32)).astype(jnp.bfloat16)

        each(4, bend)
        grad_gate_up[:, cols] = dot(normed_two_t[...], slope[:, cols]).astype(jnp.bfloat16)
        grad_gate_up[:, pl.ds(pl.multiple_of(2048 + j * 256, 256), 256)] = dot(
            normed_two_t[...], level[:, cols]
        ).astype(jnp.bfloat16)

    each(8, feed_back)
    write(grad_down, 8)
    write(grad_gate_up, 9)
    down[...] = dot_nt(slope[...], w_gate_up[:, 0:2048])
    down[...] += dot_nt(level[...], w_gate_up[:, 2048:4096])

    def mid_back(i):
        rows = block(i, 64)
        dz, y = down[rows, :], hidden[rows, :]
        r = scale_of(y)
        total = cot[rows, :].astype(jnp.float32) + norm_back(dz, y, r, lanes(2))
        sums[1] += fold(dz * y * r)
        d_hidden[rows, :] = total
        y = projected[rows, :]
        r = scale_of(y)
        d_proj[rows, :] = norm_back(total, y, r, lanes(1)).astype(jnp.bfloat16)
        sums[0] += fold(total * y * r)

    each(8, mid_back)
    write(d_hidden, 1)
    columns = weight[...].T
    for h in range(4):
        part = pl.ds(256 * h, 256)
        back = dot_nt(d_proj[...], w_output[part, :])
        for i in range(2):
            mine = back[256 * i : 256 * (i + 1), :]
            n = 4 * i + h
            d_att[i, part, :] = mine.astype(jnp.bfloat16)
            d_att_scaled[i, part, :] = (mine * columns[:, n : n + 1]).astype(jnp.bfloat16)
    write(d_att, 2)
    write(d_att_scaled, 10)

    def output_back(h):
        grad_output[block(h, 256), :] = dot(att_t[block(h, 256), :], d_proj[...]).astype(jnp.bfloat16)

    each(4, output_back)
    write(grad_output, 12)
    gain_grads[...] = jnp.zeros_like(gain_grads)
    for i in range(3):
        gain_grads[pl.ds(i + 1, 1), :] = jnp.sum(sums[i], 0, keepdims=True)
    for copy in written:
        copy.wait()
    pass_on.wait_send()
    for copy in gather.copies:
        copy.wait_send()


def forward(x, cot, cosine, sine, doc, shards, gain_shards):
    b, f32 = jnp.bfloat16, jnp.float32
    outs = [
        ((512, 640), b), ((512, 640), f32), ((2, 1024, 256), b), ((2, 1024, 256), b), ((1024, 512), b),
        ((2, 768, 1024), b), ((512, 1280), f32), ((512, 640), b),
        ((2048, 640), b), ((640, 4096), b), ((2, 1024, 256), b), ((640, 1536), b), ((1024, 640), b),
    ]
    near = [((8, 640), f32), ((8, 640), f32), ((8, 256), f32)]
    scratch = [
        ((512, 640), b), ((512, 640), b), ((512, 640), f32), ((2, 1024, 256), b), ((2, 1024, 256), b),
        ((2, 1024, 256), b), ((1024, 512), b), ((2, 768, 1024), b), ((512, 1280), f32), ((512, 640), b),
        ((2048, 640), b), ((640, 4096), b), ((1024, 640), b),
        ((640, 1536), b), ((1024, 640), b), ((640, 4096), b), ((2048, 640), b),
        ((256, 1024), b), ((512, 1024), b), ((1024, 512), b), ((512, 640), f32), ((512, 640), f32),
        ((512, 640), b), ((640, 512), b), ((512, 2048), b), ((512, 2048), b), ((512, 2048), b),
        ((512, 256), f32), ((512, 256), f32), ((512, 640), f32), ((512, 640), b), ((512, 640), b),
        ((512, 640), b), ((3, 8, 640), f32), ((2, 4, 8, 256), f32),
        ((8, 640), f32), ((8, 640), f32), ((2, 8, 640), f32),
    ]
    sems = (SENDS, SENDS, 7, len(outs), 2, 2)
    far, vmem = pl.BlockSpec(memory_space=pl.ANY), pl.BlockSpec(memory_space=pltpu.VMEM)
    return pl.pallas_call(
        forward_kernel,
        out_shape=[jax.ShapeDtypeStruct(*o) for o in outs + near],
        in_specs=[far] * 2 + [vmem] * 3 + [far] * 7 + [vmem] * 6,
        out_specs=[far] * len(outs) + [vmem] * len(near),
        scratch_shapes=[pltpu.VMEM(*o) for o in scratch] + [pltpu.SemaphoreType.DMA((n,)) for n in sems],
        compiler_params=pltpu.CompilerParams(
            collective_id=2, has_side_effects=True, vmem_limit_bytes=60 << 20
        ),
        name="forward",
    )(x, cot, cosine, sine, doc, *shards, *gain_shards)


def backward_kernel(*refs):
    fars, near = refs[:10], refs[10:15]
    cosine, sine, gains, gain_grads, weight = near
    grads, refs = refs[15:18], refs[18:]
    input_grad, totals, gain_total = refs[0], refs[1:5], refs[5]
    (
        d_att, d_att_scaled, soft, pair, queries, raw, normed, w_qkv, x, d_hidden, *rest
    ) = refs[6:]
    (
        turned_k, d_soft, d_scores, d_queries, d_pair, first, other, d_raw, normed_t, d_normed,
        grad_qkv, sums, head_sums, gain_in, gain_sum, *rest
    ) = rest
    in_sem, pair_sem, send_sem, recv_sem, local_sem = rest[-5:]
    s, f = place()
    greet(s, f)
    reduce = Reduce(s, f, (*grads, grad_qkv), totals, list(rest[:-5]), send_sem, recv_sem, local_sem)
    loads = []
    for i, (src, dst) in enumerate(
        zip(fars, (d_att, pair, soft, d_att_scaled, queries, raw, normed, w_qkv, x, d_hidden))
    ):
        loads.append(pltpu.make_async_copy(src, dst, in_sem.at[i]))
        loads[-1].start()
    for p in EARLY:
        reduce.begin(p)

    def all_of(parts):
        for p in parts:
            reduce.advance(p)

    d_pair[...] = jnp.zeros_like(d_pair)
    sums[...] = jnp.zeros_like(sums)
    head_sums[...] = jnp.zeros_like(head_sums)
    for load in loads[:5]:
        load.wait()
    turned_k[...] = pair[:, 0:256].T
    for i in range(2):

        def one_head(h, i=i):
            cols = block(h, 256)
            inverse = weight[pl.ds(4 * i + h, 1), :]
            total = None
            for c in range(3):
                low = 256 * (i + c)
                back = dot_nt(pair[low : low + 256, 256:512], d_att[i, cols, :])
                d_soft[256 * c : 256 * (c + 1), :] = back
                part = fold(soft[i, 256 * c : 256 * (c + 1), cols].astype(jnp.float32) * back)
                total = part if total is None else total + part
            inner = jnp.sum(total, 0, keepdims=True) * inverse
            for c in range(3):
                rows = pl.ds(256 * c, 256)
                p = soft[i, rows, cols].astype(jnp.float32)
                d_scores[i, rows, cols] = (p * ((d_soft[rows, :] - inner) * inverse)).astype(jnp.bfloat16)

        each(4, one_head)

    def to_pair(i, low, count):
        at, here = pl.ds(low, count), pl.ds(low - 256 * i, count)
        d_pair[at, 0:256] += dot(d_scores[i, here, :], queries[i])
        d_pair[at, 256:512] += dot(soft[i, here, :], d_att_scaled[i])

    to_pair(0, 0, 512)
    to_pair(1, 256, 256)
    first[...] = d_pair[0:512, :].astype(jnp.bfloat16)
    pass_back = pltpu.make_async_remote_copy(
        src_ref=first,
        dst_ref=other,
        send_sem=pair_sem.at[0],
        recv_sem=pair_sem.at[1],
        device_id=neighbour(s, f, -1),
        device_id_type=MESH,
    )
    pass_back.start()
    all_of(EARLY)
    to_pair(0, 512, 256)
    to_pair(1, 512, 512)
    for load in loads[5:]:
        load.wait()
    normed_t[...] = normed[...].T
    for i in range(2):

        def query_back(h, i=i):
            cols = block(h, 256)
            mixed = dot(turned_k[:, 256 * i : 256 * i + 768], d_scores[i, :, cols]) * 0.0625
            d_queries[...] = mixed.T

            def rows_of(n):
                rows = pl.ds(pl.multiple_of(256 * i + n * 128, 128), 128)
                dz = turn_back(d_queries[block(n, 128), :], cosine[rows, :], sine[rows, :])
                y = raw[rows, cols]
                r = scale_of(y)
                d_raw[rows, cols] = norm_back(dz, y, r, gains[pl.ds(4, 1), 0:256]).astype(jnp.bfloat16)
                head_sums[0] += fold(dz * y * r)

            each(2, rows_of)

        each(4, query_back)
    pass_back.wait_recv()

    def key_back(i):
        rows = block(i, 128)
        own = pl.ds(pl.multiple_of(512 + i * 128, 128), 128)
        dz = d_pair[own, 0:256] + other[rows, 0:256].astype(jnp.float32)
        dz = turn_back(dz, cosine[rows, :], sine[rows, :])
        y = raw[rows, 1024:1280]
        r = scale_of(y)
        d_raw[rows, 1024:1280] = norm_back(dz, y, r, gains[pl.ds(4, 1), 256:512]).astype(jnp.bfloat16)
        head_sums[1] += fold(dz * y * r)
        d_value = d_pair[own, 256:512] + other[rows, 256:512].astype(jnp.float32)
        d_raw[rows, 1280:1536] = d_value.astype(jnp.bfloat16)

    each(4, key_back)

    def weigh_in(j):
        cols = block(j, 256)
        grad_qkv[:, cols] = dot(normed_t[...], d_raw[:, cols]).astype(jnp.bfloat16)

    each(6, weigh_in)
    for p in LATE:
        reduce.begin(p)
    all_of(EARLY)
    d_normed[...] = dot_nt(d_raw[...], w_qkv[...])
    lanes_in = gains[pl.ds(0, 1), :]

    def norm_in_back(i):
        rows = block(i, 64)
        y, dz = x[rows, :].astype(jnp.float32), d_normed[rows, :]
        r = scale_of(y)
        input_grad[rows, :] = d_hidden[rows, :] + norm_back(dz, y, r, lanes_in)
        sums[...] += fold(dz * y * r)

    each(8, norm_in_back)
    gain_sum[0] = gain_grads[...]
    gain_sum[0, pl.ds(0, 1), :] = jnp.sum(sums[...], 0, keepdims=True)
    gain_sum[0, pl.ds(4, 1), 0:256] = jnp.sum(head_sums[0], 0, keepdims=True)
    gain_sum[0, pl.ds(4, 1), 256:512] = jnp.sum(head_sums[1], 0, keepdims=True)
    gain_dims = ("C", "X1", "X0", "Y1", "Y0", "Z1", "Z0")
    flight = reduce.send(gain_sum.at[0], gain_in.at[0], gain_dims[0])
    for stage in range(Reduce.STAGES):
        all_of(LATE)
        if stage < 7:
            flight.wait_recv()
            gain_sum[stage + 1] = gain_sum[stage] + gain_in[stage]
            if stage < 6:
                flight = reduce.send(gain_sum.at[stage + 1], gain_in.at[stage + 1], gain_dims[stage + 1])
        if stage < Reduce.STAGES - 2:
            all_of(EARLY)
    gain_total[...] = gain_sum[7]
    pass_back.wait_send()
    for copy in reduce.pending:
        copy.wait_send()


def backward(fars, near, grads):
    b, f32 = jnp.bfloat16, jnp.float32
    outs = [((512, 640), f32)] + [(shape, b) for shape in SHARES] + [((8, 640), f32)]
    held = [
        ((2, 1024, 256), b), ((2, 1024, 256), b), ((2, 768, 1024), b), ((1024, 512), b), ((2, 1024, 256), b),
        ((512, 1280), f32), ((512, 640), b), ((640, 1536), b), ((512, 640), b), ((512, 640), f32),
    ]
    scratch = [
        ((256, 1024), b), ((768, 256), f32), ((2, 768, 1024), b), ((256, 256), f32), ((1024, 512), f32),
        ((512, 512), b), ((512, 512), b), ((512, 1536), b), ((640, 512), b), ((512, 640), f32),
        ((640, 1536), b), ((8, 640), f32), ((2, 8, 256), f32), ((7, 8, 640), f32), ((8, 8, 640), f32),
    ]
    parts, sends = reduce_scratch()
    sems = (len(held), 2, sends, sends, len(PARTS))
    far, vmem = pl.BlockSpec(memory_space=pl.ANY), pl.BlockSpec(memory_space=pltpu.VMEM)
    return pl.pallas_call(
        backward_kernel,
        out_shape=[jax.ShapeDtypeStruct(*o) for o in outs],
        in_specs=[far] * 10 + [vmem] * 5 + [far] * 3,
        out_specs=[vmem] * len(outs),
        scratch_shapes=[pltpu.VMEM(*o) for o in held + scratch]
        + parts
        + [pltpu.SemaphoreType.DMA((n,)) for n in sems],
        compiler_params=pltpu.CompilerParams(
            collective_id=3, has_side_effects=True, vmem_limit_bytes=60 << 20
        ),
        name="backward",
    )(*fars, *near, *grads)


def rope_tables(positions):
    frequency = rope_base ** (-(jnp.arange(128, dtype=jnp.float32) * (2.0 / 256)))
    angles = positions[:, None] * frequency[None, :]
    return jnp.cos(angles), jnp.sin(angles)


def body(
    inputs,
    doc_start,
    w_query,
    w_key,
    w_value,
    w_output,
    w_gate,
    w_up,
    w_down,
    norm_attn_in,
    norm_attn_out,
    norm_ffn_in,
    norm_ffn_out,
    norm_query,
    norm_key,
    cotangent,
):
    row_index = lax.axis_index("seq") * 512 + jnp.arange(512, dtype=jnp.int32)
    cosine, sine = rope_tables((row_index - doc_start[0]).astype(jnp.float32))
    (
        layer_out, d_hidden, d_att, queries, pair, soft, raw, normed,
        grad_down, grad_gate_up, d_att_scaled, w_qkv, grad_output, gains, gain_grads, weight,
    ) = forward(
        inputs[0], cotangent[0], cosine, sine, doc_start,
        (w_query, w_key, w_value, w_output, w_gate, w_up, w_down),
        [
            g.reshape(1, -1)
            for g in (norm_attn_in, norm_attn_out, norm_ffn_in, norm_ffn_out, norm_query, norm_key)
        ],
    )
    input_grad, down, gate_up_share, output, qkv, gain_grads = backward(
        (d_att, pair, soft, d_att_scaled, queries, raw, normed, w_qkv, inputs[0], d_hidden),
        (cosine, sine, gains, gain_grads, weight),
        [
            grad.reshape(2, 2, grad.shape[0] // 4, grad.shape[1])
            for grad in (grad_down, grad_gate_up, grad_output)
        ],
    )
    at = lax.axis_index("fsdp")
    wide = lax.dynamic_slice(gain_grads, (0, at * 160), (4, 160))
    return (
        layer_out[None],
        input_grad[None],
        qkv[:, :1024].astype(jnp.float32),
        qkv[:, 1024:1280].astype(jnp.float32),
        qkv[:, 1280:].astype(jnp.float32),
        output.astype(jnp.float32),
        gate_up_share[:, :2048].astype(jnp.float32),
        gate_up_share[:, 2048:].astype(jnp.float32),
        down.astype(jnp.float32),
        wide[0],
        wide[1],
        wide[2],
        wide[3],
        lax.dynamic_slice(gain_grads[4, :256], (at * 64,), (64,)),
        lax.dynamic_slice(gain_grads[4, 256:512], (at * 64,), (64,)),
    )


def solution(mesh):
    in_specs = (
        P("fsdp", "seq", None),
        P("fsdp", "seq"),
        P("fsdp", None),
        P("fsdp", None),
        P("fsdp", None),
        P("fsdp", None),
        P("fsdp", None),
        P("fsdp", None),
        P("fsdp", None),
        P("fsdp"),
        P("fsdp"),
        P("fsdp"),
        P("fsdp"),
        P("fsdp"),
        P("fsdp"),
        P("fsdp", "seq", None),
    )
    out_specs = (
        P("fsdp", "seq", None),
        P("fsdp", "seq", None),
        P("fsdp", None),
        P("fsdp", None),
        P("fsdp", None),
        P("fsdp", None),
        P("fsdp", None),
        P("fsdp", None),
        P("fsdp", None),
        P("fsdp"),
        P("fsdp"),
        P("fsdp"),
        P("fsdp"),
        P("fsdp"),
        P("fsdp"),
    )
    return jax.shard_map(body, mesh=mesh, in_specs=in_specs, out_specs=out_specs, check_vma=False)
```

```python
import jax
import jax.numpy as jnp
import numpy as np
from jax import lax
from jax.experimental import pallas as pl
from jax.experimental.pallas import tpu as pltpu
from jax.sharding import PartitionSpec as P

epsilon = 1e-06
rope_base = 10000.0


MESH = pl.DeviceIdType.MESH
DIMS = ("C", "X1", "X0", "Y1", "Y0", "Z1", "Z0")
AXES = {"X": ("X1", "X0"), "Y": ("Y1", "Y0"), "Z": ("Z1", "Z0")}
CORNERS = (("Y0", "Z0"), ("X0", "Z1"), ("Z1", "Y1"), ("X0", "Y1"))


def place():
    return lax.axis_index("seq"), lax.axis_index("fsdp")


def bit_of(dim, s, f):
    if dim == "C":
        return lax.rem(f, 2)
    if dim == "X1":
        return lax.div(f, 2)
    if dim == "X0":
        return lax.rem(lax.rem(lax.div(s, 4), 2) + lax.div(f, 2), 2)
    at = lax.rem(s, 4) if dim[0] == "Y" else lax.div(s, 8)
    if dim[1] == "1":
        return lax.div(at, 2)
    return lax.rem(lax.rem(at, 2) + lax.div(at, 2), 2)


def partner(dim, s, f):
    if dim == "C":
        return (s, f + 1 - 2 * lax.rem(f, 2))
    step = 1 - 2 * lax.rem(lax.div(s, 4), 2)
    if dim == "X0":
        return (s + 4 * step, f)
    if dim == "X1":
        return (s + 4 * step, f + 2 - 4 * lax.div(f, 2))
    at, scale = (lax.rem(s, 4), 1) if dim[0] == "Y" else (lax.div(s, 8), 8)
    if dim[1] == "1":
        return (s + scale * (3 - 2 * at), f)
    return (s + scale * (1 - 2 * lax.rem(at, 2)), f)


def target(dims, s, f):
    for dim in (dims,) if isinstance(dims, str) else dims:
        s, f = partner(dim, s, f)
    return s, f


def neighbour(s, f, by):
    return (lax.rem(s + 32 + by, 32), f)


def greet(s, f, corners):
    barrier = pltpu.get_barrier_semaphore()
    for dim in DIMS:
        pl.semaphore_signal(barrier, inc=1, device_id=partner(dim, s, f), device_id_type=MESH)
    for by in (1, -1):
        pl.semaphore_signal(barrier, inc=1, device_id=neighbour(s, f, by), device_id_type=MESH)
    for one, two in corners:
        corner = partner(two, *partner(one, s, f))
        pl.semaphore_signal(barrier, inc=1, device_id=corner, device_id_type=MESH)
    pl.semaphore_wait(barrier, len(DIMS) + 2 + len(corners))


def span(start, size, tile):
    if isinstance(start, int):
        return pl.ds(start, size)
    return pl.ds(pl.multiple_of(start, tile), size)


class Region:
    def __init__(self, q, r, c):
        self.q, self.r, self.c = q, r, c

    def of(self, ref):
        return ref.at[pl.ds(*self.q), span(*self.r, 16), span(*self.c, 128)]

    def flat(self, ref, r0=0, c0=0):
        return ref.at[span(self.r[0] + r0, self.r[1], 16), span(self.c[0] + c0, self.c[1], 128)]

    def halved(self, axis, bit):
        start, size = getattr(self, axis)
        half = size // 2
        mine = Region(self.q, self.r, self.c)
        setattr(mine, axis, (start + bit * half, half))
        theirs = Region(self.q, self.r, self.c)
        setattr(theirs, axis, (start + (1 - bit) * half, half))
        return mine, theirs

    @property
    def shape(self):
        return (self.q[1], self.r[1], self.c[1])


def rows_per_step(rows, cols):
    best = 16
    for n in (32, 48, 64, 80, 96, 128, 160):
        if rows % n == 0 and n * cols <= 48 * 2048:
            best = n
    return best


def add_blocks(out, first, second, shape):
    quarters, rows, cols = shape
    step = rows_per_step(rows, cols)
    for q in range(quarters):

        def body(i, carry, q=q):
            at = i * step
            ref, index = out(q, at, step)
            ref_a, index_a = first(q, at, step)
            ref_b, index_b = second(q, at, step)
            ref[index] = ref_a[index_a] + ref_b[index_b]
            return carry

        lax.fori_loop(0, rows // step, body, 0)


def view(ref, region):
    def pick(q, at, step):
        rows = span(region.r[0] + at, step, 16)
        return ref, (region.q[0] + q, rows, span(region.c[0], region.c[1], 128))

    return pick


def flat_view(ref, region, r0, c0):
    def pick(q, at, step):
        return ref, (span(region.r[0] + r0 + at, step, 16), span(region.c[0] + c0, region.c[1], 128))

    return pick


def whole_view(ref):
    def pick(q, at, step):
        return ref, (q, span(at, step, 16), slice(None))

    return pick


ORDERS = (
    ("X1", "Y1", "Z1", "X0", "Y0", "Z0"),
    ("Y1", "Z1", "X0", "X1", "Y0", "Z0"),
    ("Z1", "X0", "Y0", "X1", "Z0", "Y1"),
    ("X0", "Y0", "Z0", "X1", "Y1", "Z1"),
    ("Y0", "Z0", "X1", "Y1", "Z1", "X0"),
    ("Z0", "X1", "Y1", "Z1", "X0", "Y0"),
)
PARTS = (
    (0, 0, 256, 0, 640, ORDERS[3], "rrr"),
    (1, 0, 160, 0, 1536, ORDERS[0], "ccr"),
    (1, 0, 160, 1536, 1536, ORDERS[1], "ccr"),
    (1, 0, 160, 3072, 1024, ORDERS[2], "ccc"),
    (0, 256, 256, 0, 640, ORDERS[4], "rrr"),
    (2, 0, 256, 0, 640, ORDERS[5], "rrr"),
)
EARLY = (1, 2, 3, 0, 4, 5)
LATE = ((0, "XYZ"), (512, "YXZ"), (1024, "ZXY"))
SHARES = ((512, 640), (160, 4096), (256, 640), (160, 1536))


def part_shapes(part):
    _, _, rows, _, cols, order, splits = part
    shapes, shape, cut = [], [2, rows, cols], iter(splits)
    for dim in order[:4]:
        axis = 0 if dim == "X1" else {"r": 1, "c": 2}[next(cut)]
        shape[axis] //= 2
        shapes.append(tuple(shape))
    return shapes


class Reduce:
    STAGES = 10

    def __init__(self, s, f, grads, totals, scratch, send_sem, recv_sem, local_sem):
        self.s, self.f, self.grads, self.totals = s, f, grads, totals
        self.send_sem, self.recv_sem, self.local_sem = send_sem, recv_sem, local_sem
        self.acc, self.inbox, self.extra = [], [], []
        for _ in PARTS:
            self.acc.append(scratch.pop(0))
            self.inbox.append([scratch.pop(0) for _ in range(4)])
            self.extra.append([scratch.pop(0) for _ in range(3)])
        n = len(PARTS)
        self.pending, self.count = [], 0
        self.flights, self.loads, self.where = [None] * n, [None] * n, [None] * n
        self.cuts = [iter(part[6]) for part in PARTS]
        self.trail, self.stage = [[] for _ in PARTS], [0] * n

    def send(self, src, dst, dim):
        copy = pltpu.make_async_remote_copy(
            src_ref=src,
            dst_ref=dst,
            send_sem=self.send_sem.at[self.count],
            recv_sem=self.recv_sem.at[self.count],
            device_id=target(dim, self.s, self.f),
            device_id_type=MESH,
        )
        copy.start()
        self.count += 1
        self.pending.append(copy)
        return copy

    def load(self, p):
        tensor, r0, rows, c0, cols, _, _ = PARTS[p]
        self.loads[p] = pltpu.make_async_copy(
            self.grads[tensor].at[:, pl.ds(r0, rows), pl.ds(c0, cols)], self.acc[p], self.local_sem.at[p]
        )
        self.loads[p].start()

    def resume(self, p):
        _, _, rows, _, cols, order, _ = PARTS[p]
        self.loads[p].wait()
        self.loads[p] = None
        dim = order[0]
        axis = "q" if dim == "X1" else next(self.cuts[p])
        self.trail[p].append((dim, axis))
        region = Region((0, 2), (0, rows), (0, cols))
        self.where[p], theirs = region.halved(axis, bit_of(dim, self.s, self.f))
        self.flights[p] = [self.send(theirs.of(self.acc[p]), self.inbox[p][0], dim)]
        self.stage[p] = 1

    def advance(self, p):
        part, stage, s, f = PARTS[p], self.stage[p], self.s, self.f
        tensor, r0, rows, c0, cols, order, _ = part
        acc, where, extra = self.acc[p], self.where[p], self.extra[p]
        self.stage[p] += 1
        for flight in self.flights[p]:
            flight.wait_recv()
        if stage < 5:
            source = self.inbox[p][stage - 1]
            add_blocks(view(acc, where), view(acc, where), whole_view(source), where.shape)
            if stage == 4:
                self.flights[p] = [self.send(where.of(acc), extra[0], order[4])]
                return
            dim = order[stage]
            axis = "q" if dim == "X1" else next(self.cuts[p])
            self.trail[p].append((dim, axis))
            self.where[p], theirs = where.halved(axis, bit_of(dim, s, f))
            self.flights[p] = [self.send(theirs.of(acc), self.inbox[p][stage], dim)]
        elif stage == 5:
            add_blocks(whole_view(extra[1]), view(acc, where), whole_view(extra[0]), where.shape)
            self.flights[p] = [self.send(extra[1], extra[2], order[5])]
        elif stage == 6:
            total = self.totals[tensor]
            add_blocks(flat_view(total, where, r0, c0), whole_view(extra[1]), whole_view(extra[2]), where.shape)
            self.trail[p] = [move for move in reversed(self.trail[p]) if move[1] != "q"]
            self.spread(p)
        else:
            dim, axis = self.trail[p].pop(0)
            start, size = getattr(where, axis)
            setattr(where, axis, (start - bit_of(dim, s, f) * size, 2 * size))
            if self.trail[p]:
                self.spread(p)

    def spread(self, p):
        tensor, r0, _, c0, _, _, _ = PARTS[p]
        region = self.where[p].flat(self.totals[tensor], r0, c0)
        self.flights[p] = [self.send(region, region, self.trail[p][0][0])]


class Late:
    STAGES = 6
    FLIPS = ((1, 0), (0, 1), (1, 1))

    def __init__(self, reduce, number, grad, total, scratch):
        self.reduce, self.grad, self.total = reduce, grad, total
        self.c0, self.axes = LATE[number]
        self.acc, self.from_core, *self.inbox = scratch
        self.where = Region((0, 2), (0, 160), (0, 512))
        self.cuts, self.trail, self.stage = iter("ccr"), [], 0
        self.flights = []

    def bit(self, dim):
        return bit_of(dim, self.reduce.s, self.reduce.f)

    def begin(self):
        core = self.bit("C")
        for high in range(2):
            theirs = self.grad.at[span((2 * high + 1 - core) * 160, 160, 16), pl.ds(self.c0, 512)]
            self.flights.append(self.reduce.send(theirs, self.from_core.at[high], "C"))

    def scatter(self, axis, inbox):
        moves = [(dim, "q" if dim == "X1" else next(self.cuts)) for dim in AXES[axis]]
        self.trail.append(moves)
        here = self.where

        def cut(flips):
            region = here
            for (dim, along), flip in zip(moves, flips):
                bit = self.bit(dim)
                region = region.halved(along, 1 - bit if flip else bit)[0]
            return region

        self.flights = [
            self.reduce.send(
                cut(flips).of(self.acc),
                inbox.at[k],
                tuple(dim for (dim, _), flip in zip(moves, flips) if flip),
            )
            for k, flips in enumerate(self.FLIPS)
        ]
        self.where = cut((0, 0))

    def spread(self):
        moves = [move for move in self.trail.pop() if move[1] != "q"]
        self.grow = moves
        region = self.where.flat(self.total, 0, self.c0)
        choices = self.FLIPS if len(moves) == 2 else ((1,),)
        self.flights = [
            self.reduce.send(region, region, tuple(dim for (dim, _), flip in zip(moves, flips) if flip))
            for flips in choices
        ]

    def summed(self, inbox):
        spot = (
            pl.ds(*self.where.q),
            span(*self.where.r, 16),
            span(*self.where.c, 128),
        )
        terms = [self.acc[spot]] + [inbox[k] for k in range(3)]
        first, second, third, fourth = (term.astype(jnp.float32) for term in terms)
        return spot, ((first + second) + (third + fourth)).astype(jnp.bfloat16)

    def advance(self):
        for flight in self.flights:
            flight.wait_recv()
        stage = self.stage
        self.stage += 1
        if stage == 0:
            core = self.bit("C")
            for high in range(2):
                mine = span((2 * high + core) * 160, 160, 16)
                self.acc[high] = self.grad[mine, pl.ds(self.c0, 512)] + self.from_core[high]
            self.scatter(self.axes[0], self.inbox[0])
        elif stage == 1:
            spot, value = self.summed(self.inbox[0])
            self.acc[spot] = value
            self.scatter(self.axes[1], self.inbox[1])
        elif stage == 2:
            spot, value = self.summed(self.inbox[1])
            self.acc[spot] = value
            self.flights = [
                self.reduce.send(
                    self.where.of(self.acc),
                    self.inbox[2].at[k],
                    tuple(dim for dim, flip in zip(AXES[self.axes[2]], flips) if flip),
                )
                for k, flips in enumerate(self.FLIPS)
            ]
        elif stage == 3:
            _, value = self.summed(self.inbox[2])
            rows, cols = self.where.r, self.where.c
            self.total[span(*rows, 16), span(cols[0] + self.c0, cols[1], 128)] = value[0]
            self.spread()
        else:
            for dim, axis in reversed(self.grow):
                start, size = getattr(self.where, axis)
                setattr(self.where, axis, (start - self.bit(dim) * size, 2 * size))
            if self.trail:
                self.spread()


def late_scratch():
    shapes = []
    for _, axes in LATE:
        one = (1, 160, 256) if axes[0] == "X" else (2, 160, 128)
        shapes += [(2, 160, 512)] * 2 + [(3, *one), (3, 1, 80, 128), (3, 1, 80, 128)]
    return [pltpu.VMEM(shape, jnp.bfloat16) for shape in shapes]


def reduce_scratch():
    scratch, sends = [], 10 + 17 * len(LATE)
    for part in PARTS:
        shapes = part_shapes(part)
        scratch += [pltpu.VMEM((2, part[2], part[4]), jnp.bfloat16)]
        scratch += [pltpu.VMEM(shape, jnp.bfloat16) for shape in shapes]
        scratch += [pltpu.VMEM(shapes[-1], jnp.bfloat16)] * 3
        sends += 11
    return scratch, sends


PIECES = (
    (0, 0, 0, 160, 1024, "Y0", "Z0", "c"),
    (1, 0, 1024, 160, 256, None, None, "whole"),
    (2, 0, 1280, 160, 256, None, None, "whole"),
    (3, 1, 0, 256, 640, "X0", "Z1", "r"),
    (4, 2, 0, 160, 2048, "Z1", "Y1", "c"),
    (5, 2, 2048, 160, 2048, "Y0", "Z0", "c"),
    (6, 3, 0, 512, 640, "X0", "Y1", "r"),
)
WHOLES = ((640, 1536), (1024, 640), (640, 4096), (2048, 640))


def own_gains(gain_shards, gain_own, f):
    def placed(share):
        shift = lax.broadcasted_iota(jnp.int32, (256, 4 * share), 1) - lax.broadcasted_iota(
            jnp.int32, (256, 4 * share), 0
        )
        chosen = jnp.where(shift == share * f, 1.0, 0.0).astype(jnp.bfloat16)
        return jnp.dot(gain_shards[...].astype(jnp.bfloat16), chosen, preferred_element_type=jnp.float32)

    gain_own[...] = jnp.where(lax.broadcasted_iota(jnp.int32, (8, 640), 0) < 4, placed(160), 0.0)
    heads = placed(64)
    gain_own[4:5, 0:256] = heads[4:5, :]
    gain_own[4:5, 256:512] = heads[5:6, :]


class Gather:
    def __init__(self, s, f, shards, outs, send_sem, recv_sem, local_sem):
        self.s, self.f, self.shards, self.outs = s, f, shards, outs
        self.send_sem, self.recv_sem, self.local_sem = send_sem, recv_sem, local_sem
        self.copies, self.count = [], 0
        self.core, high = bit_of("C", s, f), bit_of("X1", s, f)
        self.far = 2 * (1 - high) + self.core
        self.flights, self.sides, self.loads = {}, {}, {}

    def send(self, src, dst, dim):
        copy = pltpu.make_async_remote_copy(
            src_ref=src,
            dst_ref=dst,
            send_sem=self.send_sem.at[self.count],
            recv_sem=self.recv_sem.at[self.count],
            device_id=target(dim, self.s, self.f),
            device_id_type=MESH,
        )
        copy.start()
        self.count += 1
        self.copies.append(copy)
        return copy

    def quarter(self, piece, bit_one, bit_two):
        _, _, c0, rows, cols, _, _, cut = piece
        half = rows // 2
        if cut == "c":
            return (bit_two * half, half), (bit_one * (cols // 2), cols // 2)
        return (bit_two * half + bit_one * (half // 2), half // 2), (0, cols)

    def spot(self, piece, share, box):
        (r, nr), (c, nc) = box
        return self.outs[piece[1]].at[span(r + share * piece[3], nr, 16), span(c + piece[2], nc, 128)]

    def first(self, piece):
        if piece[7] == "whole":
            return (0, piece[3]), (0, piece[4])
        return self.quarter(piece, bit_of(piece[5], self.s, self.f), bit_of(piece[6], self.s, self.f))

    def begin(self, pieces):
        for i in pieces:
            piece = PIECES[i]
            (r, nr), (c, nc) = quarter = self.first(piece)
            src = self.shards[i].at[span(r, nr, 16), span(c, nc, 128)]
            self.flights[i] = self.send(src, self.spot(piece, self.f, quarter), "X1")
        for i in pieces:
            piece = PIECES[i]
            dst = self.spot(piece, self.f, ((0, piece[3]), (0, piece[4])))
            self.sides[i] = [self.send(self.shards[i], dst, "C")]
            self.loads[i] = pltpu.make_async_copy(self.shards[i], dst, self.local_sem.at[i])
            self.loads[i].start()

    def fan(self, i):
        piece, s, f = PIECES[i], self.s, self.f
        self.flights[i].wait_recv()
        here = self.spot(piece, self.far, self.first(piece))
        self.sides[i].append(self.send(here, here, "C"))
        if piece[7] == "whole":
            return
        one, two = bit_of(piece[5], s, f), bit_of(piece[6], s, f)
        self.flights[i] = [
            (self.send(here, here, piece[5]), (1 - one, two)),
            (self.send(here, here, piece[6]), (one, 1 - two)),
            (self.send(here, here, (piece[5], piece[6])), (1 - one, 1 - two)),
        ]

    def relay(self, i):
        piece = PIECES[i]
        for flight, bits in self.flights[i]:
            flight.wait_recv()
            here = self.spot(piece, self.far, self.quarter(piece, *bits))
            self.sides[i].append(self.send(here, here, "C"))

    def arrive(self, i):
        for copy in self.sides[i]:
            copy.wait_recv()
        self.loads[i].wait()


SENDS = 9 * len(PIECES) + 7


NT = (((1,), (1,)), ((), ()))


def dot(left, right):
    return jnp.dot(left, right, preferred_element_type=jnp.float32)


def dot_nt(left, right):
    return lax.dot_general(left, right, NT, preferred_element_type=jnp.float32)


def block(i, size):
    if isinstance(i, int):
        return pl.ds(i * size, size)
    return pl.ds(pl.multiple_of(i * size, size), size)


def each(count, body):
    def step(i, carry):
        body(i)
        return carry

    lax.fori_loop(0, count, step, 0)


def unrolled(count, body):
    for i in range(count):
        body(i)


def scale_of(y):
    return lax.rsqrt(jnp.mean(y * y, -1, keepdims=True) + epsilon)


def norm_back(dz, y, r, g):
    gained = g * dz
    return r * gained - y * (r * r * r) * jnp.mean(gained * y, -1, keepdims=True)


def fold(terms):
    rows, cols = terms.shape
    return jnp.sum(terms.reshape(rows // 8, 8, cols), 0)


def turn(v, cosine, sine):
    a, b = v[:, :128], v[:, 128:]
    return jnp.concatenate([a * cosine - b * sine, b * cosine + a * sine], 1)


def turn_back(v, cosine, sine):
    a, b = v[:, :128], v[:, 128:]
    return jnp.concatenate([a * cosine + b * sine, b * cosine - a * sine], 1)


def forward_kernel(*refs):
    x_far, cot_far, doc, frequency, gain_shards = refs[:5]
    shards = refs[5:12]
    outs, gains, gain_grads, weight, cosine, sine = refs[12:25], *refs[25:30]
    (
        x, cot, d_hidden, d_att, d_att_scaled, queries, pair, soft, raw, normed,
        grad_down, grad_gate_up, grad_output, w_qkv, w_output, w_gate_up, w_down,
        turned_v, att, att_t, projected, hidden, normed_two, normed_two_t,
        product, slope, level, gate, up, down, d_down, d_proj, layer_out, sums, weight_sums,
        gain_own, gain_mid, gain_in, normed_spots, *from_core,
    ) = refs[30:-6]
    send_sem, recv_sem, local_sem, out_sem, in_sem, pair_sem = refs[-6:]
    s, f = place()
    greet(s, f, CORNERS)
    gather = Gather(s, f, shards, (w_qkv, w_output, w_gate_up, w_down), send_sem, recv_sem, local_sem)
    gather.begin((1, 2, 0))
    load_x = pltpu.make_async_copy(x_far, x, in_sem.at[0])
    load_x.start()
    load_cot = pltpu.make_async_copy(cot_far, cot, in_sem.at[1])
    load_cot.start()
    own_gains(gain_shards, gain_own, f)
    flight = gather.send(gain_own, gain_in.at[0], "C")
    lanes = lambda i: gains[pl.ds(i, 1), :]
    written = []

    def write(src, number):
        copy = pltpu.make_async_copy(src, outs[number], out_sem.at[number])
        copy.start()
        written.append(copy)

    token = lax.broadcasted_iota(jnp.int32, (1, 512), 1) + s * 512
    position = (token - doc[...]).astype(jnp.float32)
    position = jnp.broadcast_to(position, (8, 512)).T

    def table(i):
        rows = block(i, 64)
        angle = spots[rows, 0:1] * frequency[0:1, :]
        cosine[rows, :] = jnp.cos(angle)
        sine[rows, :] = jnp.sin(angle)

    spots = normed_spots
    spots[...] = position
    flight.wait_recv()
    gain_mid[...] = gain_own[...] + gain_in[0]
    flight = gather.send(gain_mid, gain_in.at[1], "X1")
    unrolled(8, table)
    for i in (1, 2, 0):
        gather.fan(i)
    gather.begin((3, 4, 5, 6))
    flight.wait_recv()
    gains[...] = gain_mid[...] + gain_in[1]
    load_x.wait()

    def norm_in(i):
        rows = block(i, 64)
        y = x[rows, :].astype(jnp.float32)
        normed[rows, :] = (y * scale_of(y) * lanes(0)).astype(jnp.bfloat16)

    unrolled(8, norm_in)
    write(normed, 7)
    gather.arrive(1)
    gather.arrive(2)
    pair_raw = dot(normed[...], w_qkv[:, 1024:1536])
    raw[:, 1024:1280] = pair_raw[:, :256]
    pair[512:1024, 256:512] = pair_raw[:, 256:].astype(jnp.bfloat16)

    def shape_key(i):
        rows = block(i, 128)
        y = raw[rows, 1024:1280]
        y = turn(y * scale_of(y) * gains[pl.ds(4, 1), 256:512], cosine[rows, :], sine[rows, :])
        pair[pl.ds(512 + i * 128, 128), 0:256] = y.astype(jnp.bfloat16)

    unrolled(4, shape_key)
    pass_on = pltpu.make_async_remote_copy(
        src_ref=pair.at[pl.ds(512, 512), :],
        dst_ref=pair.at[pl.ds(0, 512), :],
        send_sem=pair_sem.at[0],
        recv_sem=pair_sem.at[1],
        device_id=neighbour(s, f, 1),
        device_id_type=MESH,
    )
    pass_on.start()
    gather.relay(0)
    gather.arrive(0)
    write(w_qkv, 11)

    def shape_query(h):
        raw[:, block(h, 256)] = dot(normed[...], w_qkv[:, block(h, 256)])

        def rows_of(i):
            rows = block(i, 128)
            y = raw[rows, block(h, 256)]
            y = turn(y * scale_of(y) * gains[pl.ds(4, 1), 0:256], cosine[rows, :], sine[rows, :])
            at = pl.ds(pl.multiple_of(h * 256 + i % 2 * 128, 128), 128)
            queries[i // 2, at, :] = (y * 0.0625).astype(jnp.bfloat16)

        unrolled(4, rows_of)

    each(4, shape_query)
    write(raw, 6)
    write(queries, 3)
    gather.fan(3)
    gather.fan(4)
    row = [lax.broadcasted_iota(jnp.int32, (1, 256), 1) + i * 256 for i in range(2)]
    lowest = [
        jnp.maximum(row[i] + 1, doc[0:1, 256 * i : 256 * (i + 1)] - (s - 1) * 512) for i in range(2)
    ]

    def weigh(i, h, first, count):
        total = None
        query = queries[i, block(h, 256), :]
        for c in range(first, first + count, 2):
            low = i * 256 + c * 128
            score = dot_nt(pair[low : low + 256, 0:256], query)
            key = lax.broadcasted_iota(jnp.int32, (256, 256), 0) + low
            seen = (key >= lowest[i]) & (key <= row[i] + 512)
            p = jnp.where(seen, jnp.exp(score), 0.0)
            soft[i, c * 128 : c * 128 + 256, block(h, 256)] = p.astype(jnp.bfloat16)
            total = fold(p) if total is None else total + fold(p)
        return total

    for i, first, count in ((0, 4, 2), (1, 2, 4)):

        def own_keys(h, i=i, first=first, count=count):
            weight_sums[i, h] = weigh(i, h, first, count)

        each(4, own_keys)
        gather.fan(5 + i)
    gather.relay(3)
    pass_on.wait_recv()
    write(pair, 4)
    turned_v[...] = pair[:, 256:512].T
    for i, first, count in ((0, 0, 4), (1, 0, 2)):

        def attend(h, i=i, first=first, count=count):
            total = weight_sums[i, h] + weigh(i, h, first, count)
            inverse = 1.0 / jnp.sum(total, 0, keepdims=True)
            weight[pl.ds(4 * i + h, 1), :] = inverse
            mixed = dot(turned_v[:, 256 * i : 256 * i + 768], soft[i, :, block(h, 256)]) * inverse
            att_t[block(h, 256), 256 * i : 256 * (i + 1)] = mixed.astype(jnp.bfloat16)
            att[256 * i : 256 * (i + 1), block(h, 256)] = mixed.T.astype(jnp.bfloat16)

        each(4, attend)
        gather.relay(4 + i)
    write(soft, 5)
    gather.arrive(3)
    projected[...] = dot(att[...], w_output[...])

    def mid(i):
        rows = block(i, 64)
        y = projected[rows, :]
        z = x[rows, :].astype(jnp.float32) + y * scale_of(y) * lanes(1)
        hidden[rows, :] = z
        normed_two[rows, :] = (z * scale_of(z) * lanes(2)).astype(jnp.bfloat16)

    unrolled(8, mid)
    normed_two_t[...] = normed_two[...].T
    gather.relay(6)
    gather.arrive(4)
    gather.arrive(5)

    def feed(j):
        cols = block(j, 256)
        gate[...] = dot(normed_two[...], w_gate_up[:, cols])
        up[...] = dot(normed_two[...], w_gate_up[:, pl.ds(pl.multiple_of(2048 + j * 256, 256), 256)])

        def bend(i):
            rows = block(i, 64)
            g, u = gate[rows, :], up[rows, :]
            square = g * g
            t = jnp.tanh(0.7978845608028654 * g * (1.0 + 0.044715 * square))
            half = 0.5 * (1.0 + t)
            gelu = g * half
            rise = half + 0.5 * g * (1.0 - t * t) * (0.7978845608028654 * (1.0 + 0.134145 * square))
            product[rows, cols] = (gelu * u).astype(jnp.bfloat16)
            slope[rows, cols] = (rise * u).astype(jnp.bfloat16)
            level[rows, cols] = gelu.astype(jnp.bfloat16)

        unrolled(8, bend)

    each(8, feed)
    gather.arrive(6)
    down[...] = dot(product[...], w_down[...])
    sums[...] = jnp.zeros_like(sums)
    load_cot.wait()

    def end(i):
        rows = block(i, 64)
        y, dz = down[rows, :], cot[rows, :].astype(jnp.float32)
        r = scale_of(y)
        layer_out[rows, :] = (hidden[rows, :] + y * r * lanes(3)).astype(jnp.bfloat16)
        d_down[rows, :] = norm_back(dz, y, r, lanes(3)).astype(jnp.bfloat16)
        sums[2] += fold(dz * y * r)

    unrolled(8, end)
    write(layer_out, 0)

    def feed_back(j):
        cols = block(j, 256)
        gate[...] = dot_nt(d_down[...], w_down[cols, :])

        def bend(i):
            rows = block(i, 128)
            d = gate[rows, :]
            slope[rows, cols] = (d * slope[rows, cols].astype(jnp.float32)).astype(jnp.bfloat16)
            level[rows, cols] = (d * level[rows, cols].astype(jnp.float32)).astype(jnp.bfloat16)

        unrolled(4, bend)
        for grad, at in ((slope, 0), (level, 2048)):
            block_ = dot(normed_two_t[...], grad[:, cols]).astype(jnp.bfloat16)
            for q in range(4):
                grad_gate_up[q // 2, q % 2, :, pl.ds(pl.multiple_of(at + j * 256, 256), 256)] = block_[
                    160 * q : 160 * (q + 1), :
                ]

    def down_back(j):
        q = lax.div(j, 2)
        grad_down[lax.div(q, 2), lax.rem(q, 2), block(lax.rem(j, 2), 256), :] = dot(
            product[:, block(j, 256)].T, d_down[...]
        ).astype(jnp.bfloat16)

    core, exchanged = bit_of("C", s, f), {}
    tensors = (grad_down, grad_gate_up, grad_output)

    def exchange(p):
        tensor, r0, rows, c0, cols, _, _ = PARTS[p]
        theirs = tensors[tensor].at[pl.ds(0, 2), 1 - core, pl.ds(r0, rows), pl.ds(c0, cols)]
        exchanged[p] = gather.send(theirs, from_core[p], "C")

    def add_exchanged(p):
        tensor, r0, rows, c0, cols, _, _ = PARTS[p]
        exchanged[p].wait_recv()
        step = rows_per_step(rows, cols)
        for q in range(2):

            def add(i, q=q):
                at = pl.ds(pl.multiple_of(r0 + i * step, 16), step)
                tensors[tensor][q, core, at, pl.ds(c0, cols)] += from_core[p][q, block(i, step), :]

            each(rows // step, add)

    each(8, feed_back)
    for p in (1, 2, 3):
        exchange(p)
    each(8, down_back)
    for p in (0, 4):
        exchange(p)
    down[...] = dot_nt(slope[...], w_gate_up[:, 0:2048])
    down[...] += dot_nt(level[...], w_gate_up[:, 2048:4096])

    def mid_back(i):
        rows = block(i, 64)
        dz, y = down[rows, :], hidden[rows, :]
        r = scale_of(y)
        total = cot[rows, :].astype(jnp.float32) + norm_back(dz, y, r, lanes(2))
        sums[1] += fold(dz * y * r)
        d_hidden[rows, :] = total
        y = projected[rows, :]
        r = scale_of(y)
        d_proj[rows, :] = norm_back(total, y, r, lanes(1)).astype(jnp.bfloat16)
        sums[0] += fold(total * y * r)

    unrolled(8, mid_back)
    write(d_hidden, 1)
    columns = weight[...].T

    def output_back(h):
        grad_output[lax.div(h, 2), lax.rem(h, 2)] = dot(att_t[block(h, 256), :], d_proj[...]).astype(jnp.bfloat16)

    each(4, output_back)
    exchange(5)
    for h in range(4):
        part = pl.ds(256 * h, 256)
        back = dot_nt(d_proj[...], w_output[part, :])
        for i in range(2):
            mine = back[256 * i : 256 * (i + 1), :]
            n = 4 * i + h
            d_att[i, part, :] = mine.astype(jnp.bfloat16)
            d_att_scaled[i, part, :] = (mine * columns[:, n : n + 1]).astype(jnp.bfloat16)
    write(d_att, 2)
    write(d_att_scaled, 10)
    for p in (1, 2, 3):
        add_exchanged(p)
    write(grad_gate_up.at[:, core], 9)
    for p in (0, 4):
        add_exchanged(p)
    write(grad_down.at[:, core], 8)
    add_exchanged(5)
    write(grad_output.at[:, core], 12)
    gain_grads[...] = jnp.zeros_like(gain_grads)
    for i in range(3):
        gain_grads[pl.ds(i + 1, 1), :] = jnp.sum(sums[i], 0, keepdims=True)
    for copy in written:
        copy.wait()
    pass_on.wait_send()
    for copy in gather.copies:
        copy.wait_send()


def forward(x, cot, doc, frequency, gain_shards, shards):
    b, f32 = jnp.bfloat16, jnp.float32
    outs = [
        ((512, 640), b), ((512, 640), f32), ((2, 1024, 256), b), ((2, 1024, 256), b), ((1024, 512), b),
        ((2, 768, 1024), b), ((512, 1280), f32), ((512, 640), b),
        ((2, 512, 640), b), ((2, 160, 4096), b), ((2, 1024, 256), b), ((640, 1536), b), ((2, 256, 640), b),
    ]
    near = [((8, 640), f32), ((8, 640), f32), ((8, 256), f32), ((512, 128), f32), ((512, 128), f32)]
    scratch = [
        ((512, 640), b), ((512, 640), b), ((512, 640), f32), ((2, 1024, 256), b), ((2, 1024, 256), b),
        ((2, 1024, 256), b), ((1024, 512), b), ((2, 768, 1024), b), ((512, 1280), f32), ((512, 640), b),
        ((2, 2, 512, 640), b), ((2, 2, 160, 4096), b), ((2, 2, 256, 640), b),
        ((640, 1536), b), ((1024, 640), b), ((640, 4096), b), ((2048, 640), b),
        ((256, 1024), b), ((512, 1024), b), ((1024, 512), b), ((512, 640), f32), ((512, 640), f32),
        ((512, 640), b), ((640, 512), b), ((512, 2048), b), ((512, 2048), b), ((512, 2048), b),
        ((512, 256), f32), ((512, 256), f32), ((512, 640), f32), ((512, 640), b), ((512, 640), b),
        ((512, 640), b), ((3, 8, 640), f32), ((2, 4, 8, 256), f32),
        ((8, 640), f32), ((8, 640), f32), ((2, 8, 640), f32), ((512, 8), f32),
    ]
    scratch += [((2, part[2], part[4]), b) for part in PARTS]
    sems = (SENDS, SENDS, 7, len(outs), 2, 2)
    far, vmem = pl.BlockSpec(memory_space=pl.ANY), pl.BlockSpec(memory_space=pltpu.VMEM)
    return pl.pallas_call(
        forward_kernel,
        out_shape=[jax.ShapeDtypeStruct(*o) for o in outs + near],
        in_specs=[far] * 2 + [vmem] * 3 + [far] * 7,
        out_specs=[far] * len(outs) + [vmem] * len(near),
        scratch_shapes=[pltpu.VMEM(*o) for o in scratch] + [pltpu.SemaphoreType.DMA((n,)) for n in sems],
        compiler_params=pltpu.CompilerParams(
            collective_id=2, has_side_effects=True, vmem_limit_bytes=60 << 20
        ),
        name="forward",
    )(x, cot, doc, frequency, gain_shards, *shards)


def backward_kernel(*refs):
    fars, near = refs[:10], refs[10:15]
    cosine, sine, gains, gain_grads, weight = near
    grads, refs = refs[15:18], refs[18:]
    input_grad, totals, gain_total = refs[0], refs[1:5], refs[5]
    (
        d_att, d_att_scaled, soft, pair, queries, raw, normed, w_qkv, x, d_hidden, *rest
    ) = refs[6:]
    (
        turned_k, d_soft, d_scores, d_queries, d_pair, first, other, d_raw, normed_t, d_normed,
        grad_qkv, sums, head_sums, gain_in, gain_sum, *rest
    ) = rest
    in_sem, pair_sem, send_sem, recv_sem, local_sem = rest[-5:]
    s, f = place()
    boxes = list(rest[:-5])
    reduce = Reduce(s, f, grads, totals, boxes[15:], send_sem, recv_sem, local_sem)
    lates = [Late(reduce, n, grad_qkv, totals[3], boxes[5 * n : 5 * n + 5]) for n in range(len(LATE))]
    for p in EARLY:
        reduce.load(p)
    greet(s, f, tuple(AXES.values()))
    for p in EARLY:
        reduce.resume(p)
    loads = []
    for i, (src, dst) in enumerate(
        zip(fars, (d_att, pair, soft, d_att_scaled, queries, raw, normed, w_qkv, x, d_hidden))
    ):
        loads.append(pltpu.make_async_copy(src, dst, in_sem.at[i]))
        loads[-1].start()

    def all_of(parts):
        for p in parts:
            reduce.advance(p)

    d_pair[...] = jnp.zeros_like(d_pair)
    sums[...] = jnp.zeros_like(sums)
    head_sums[...] = jnp.zeros_like(head_sums)
    for load in loads[:5]:
        load.wait()
    turned_k[...] = pair[:, 0:256].T
    for i in range(2):

        def one_head(h, i=i):
            cols = block(h, 256)
            inverse = weight[pl.ds(4 * i + h, 1), :]
            total = None
            for c in range(3):
                low = 256 * (i + c)
                back = dot_nt(pair[low : low + 256, 256:512], d_att[i, cols, :])
                d_soft[256 * c : 256 * (c + 1), :] = back
                part = fold(soft[i, 256 * c : 256 * (c + 1), cols].astype(jnp.float32) * back)
                total = part if total is None else total + part
            inner = jnp.sum(total, 0, keepdims=True) * inverse
            for c in range(3):
                rows = pl.ds(256 * c, 256)
                p = soft[i, rows, cols].astype(jnp.float32)
                d_scores[i, rows, cols] = (p * ((d_soft[rows, :] - inner) * inverse)).astype(jnp.bfloat16)

        each(4, one_head)

    def to_pair(i, low, count):
        at, here = pl.ds(low, count), pl.ds(low - 256 * i, count)
        d_pair[at, 0:256] += dot(d_scores[i, here, :], queries[i])
        d_pair[at, 256:512] += dot(soft[i, here, :], d_att_scaled[i])

    to_pair(0, 0, 512)
    to_pair(1, 256, 256)
    first[...] = d_pair[0:512, :].astype(jnp.bfloat16)
    pass_back = pltpu.make_async_remote_copy(
        src_ref=first,
        dst_ref=other,
        send_sem=pair_sem.at[0],
        recv_sem=pair_sem.at[1],
        device_id=neighbour(s, f, -1),
        device_id_type=MESH,
    )
    pass_back.start()
    to_pair(0, 512, 256)
    to_pair(1, 512, 512)
    for load in loads[5:]:
        load.wait()
    normed_t[...] = normed[...].T
    for i in range(2):

        def query_back(h, i=i):
            cols = block(h, 256)
            mixed = dot(turned_k[:, 256 * i : 256 * i + 768], d_scores[i, :, cols]) * 0.0625
            d_queries[...] = mixed.T

            def rows_of(n):
                rows = pl.ds(256 * i + n * 128, 128)
                dz = turn_back(d_queries[block(n, 128), :], cosine[rows, :], sine[rows, :])
                y = raw[rows, cols]
                r = scale_of(y)
                d_raw[rows, cols] = norm_back(dz, y, r, gains[pl.ds(4, 1), 0:256]).astype(jnp.bfloat16)
                head_sums[0] += fold(dz * y * r)

            unrolled(2, rows_of)

        each(4, query_back)
    all_of(EARLY)
    pass_back.wait_recv()

    def key_back(i):
        rows = block(i, 128)
        own = pl.ds(512 + i * 128, 128)
        dz = d_pair[own, 0:256] + other[rows, 0:256].astype(jnp.float32)
        dz = turn_back(dz, cosine[rows, :], sine[rows, :])
        y = raw[rows, 1024:1280]
        r = scale_of(y)
        d_raw[rows, 1024:1280] = norm_back(dz, y, r, gains[pl.ds(4, 1), 256:512]).astype(jnp.bfloat16)
        head_sums[1] += fold(dz * y * r)
        d_value = d_pair[own, 256:512] + other[rows, 256:512].astype(jnp.float32)
        d_raw[rows, 1280:1536] = d_value.astype(jnp.bfloat16)

    unrolled(4, key_back)

    def weigh_in(j):
        cols = block(j, 256)
        grad_qkv[:, cols] = dot(normed_t[...], d_raw[:, cols]).astype(jnp.bfloat16)

    each(6, weigh_in)
    for late in lates:
        late.begin()
    all_of(EARLY)
    d_normed[...] = dot_nt(d_raw[...], w_qkv[...])
    lanes_in = gains[pl.ds(0, 1), :]

    def norm_in_back(i):
        rows = block(i, 64)
        y, dz = x[rows, :].astype(jnp.float32), d_normed[rows, :]
        r = scale_of(y)
        input_grad[rows, :] = d_hidden[rows, :] + norm_back(dz, y, r, lanes_in)
        sums[...] += fold(dz * y * r)

    unrolled(8, norm_in_back)
    gain_sum[0] = gain_grads[...]
    gain_sum[0, pl.ds(0, 1), :] = jnp.sum(sums[...], 0, keepdims=True)
    gain_sum[0, pl.ds(4, 1), 0:256] = jnp.sum(head_sums[0], 0, keepdims=True)
    gain_sum[0, pl.ds(4, 1), 256:512] = jnp.sum(head_sums[1], 0, keepdims=True)
    flights = [reduce.send(gain_sum.at[0], gain_in.at[0], "C")]
    for stage in range(7):
        if stage < Late.STAGES:
            for late in lates:
                late.advance()
        if stage < 4:
            total = gain_sum[stage]
            for k, flight in enumerate(flights):
                flight.wait_recv()
                total = total + gain_in[max(3 * stage - 2, 0) + k]
            gain_sum[stage + 1] = total
        if stage < 3:
            high, low = AXES["XYZ"[stage]]
            flights = [
                reduce.send(gain_sum.at[stage + 1], gain_in.at[3 * stage + 1 + k], dims)
                for k, dims in enumerate(((high,), (low,), (high, low)))
            ]
        all_of(EARLY)
    gain_total[...] = gain_sum[4]
    pass_back.wait_send()
    for copy in reduce.pending:
        copy.wait_send()


def backward(fars, near, grads):
    b, f32 = jnp.bfloat16, jnp.float32
    outs = [((512, 640), f32)] + [(shape, b) for shape in SHARES] + [((8, 640), f32)]
    held = [
        ((2, 1024, 256), b), ((2, 1024, 256), b), ((2, 768, 1024), b), ((1024, 512), b), ((2, 1024, 256), b),
        ((512, 1280), f32), ((512, 640), b), ((640, 1536), b), ((512, 640), b), ((512, 640), f32),
    ]
    scratch = [
        ((256, 1024), b), ((768, 256), f32), ((2, 768, 1024), b), ((256, 256), f32), ((1024, 512), f32),
        ((512, 512), b), ((512, 512), b), ((512, 1536), b), ((640, 512), b), ((512, 640), f32),
        ((640, 1536), b), ((8, 640), f32), ((2, 8, 256), f32), ((10, 8, 640), f32), ((5, 8, 640), f32),
    ]
    parts, sends = reduce_scratch()
    sems = (len(held), 2, sends, sends, len(PARTS))
    far, vmem = pl.BlockSpec(memory_space=pl.ANY), pl.BlockSpec(memory_space=pltpu.VMEM)
    return pl.pallas_call(
        backward_kernel,
        out_shape=[jax.ShapeDtypeStruct(*o) for o in outs],
        in_specs=[far] * 10 + [vmem] * 5 + [far] * 3,
        out_specs=[vmem] * len(outs),
        scratch_shapes=[pltpu.VMEM(*o) for o in held + scratch]
        + late_scratch()
        + parts
        + [pltpu.SemaphoreType.DMA((n,)) for n in sems],
        compiler_params=pltpu.CompilerParams(
            collective_id=3, has_side_effects=True, vmem_limit_bytes=60 << 20
        ),
        name="backward",
    )(*fars, *near, *grads)


FREQUENCY = (rope_base ** (-np.arange(128) / 128.0)).astype(np.float32)[None, :]


def finish_kernel(layer_out, input_grad, down, gate_up, output, qkv, *outs):
    outs[0][...] = layer_out[...]
    outs[1][...] = input_grad[...]
    cuts = ((qkv, 0), (qkv, 1024), (qkv, 1280), (output, 0), (gate_up, 0), (gate_up, 2048), (down, 0))
    for out, (src, at) in zip(outs[2:], cuts):
        rows, cols = out.shape

        def widen(i, out=out, src=src, at=at, cols=cols):
            part = block(i, 32)
            out[part, :] = src[part, at : at + cols].astype(jnp.float32)

        each(rows // 32, widen)


def finish(layer_out, input_grad, down, gate_up, output, qkv):
    shapes = ((160, 1024), (160, 256), (160, 256), (256, 640), (160, 2048), (160, 2048), (512, 640))
    return pl.pallas_call(
        finish_kernel,
        out_shape=[
            jax.ShapeDtypeStruct((512, 640), jnp.bfloat16),
            jax.ShapeDtypeStruct((512, 640), jnp.float32),
        ]
        + [jax.ShapeDtypeStruct(shape, jnp.float32) for shape in shapes],
        in_specs=[pl.BlockSpec(memory_space=pltpu.VMEM)] * 6,
        out_specs=[pl.BlockSpec(memory_space=pltpu.VMEM)] * 9,
        compiler_params=pltpu.CompilerParams(vmem_limit_bytes=40 << 20),
        name="finish",
    )(layer_out, input_grad, down, gate_up, output, qkv)


def body(
    inputs,
    doc_start,
    w_query,
    w_key,
    w_value,
    w_output,
    w_gate,
    w_up,
    w_down,
    norm_attn_in,
    norm_attn_out,
    norm_ffn_in,
    norm_ffn_out,
    norm_query,
    norm_key,
    cotangent,
):
    packed = sum(
        jnp.pad(g.astype(jnp.float32)[None, :], ((i, 7 - i), (0, 256 - g.shape[0])))
        for i, g in enumerate((norm_attn_in, norm_attn_out, norm_ffn_in, norm_ffn_out, norm_query, norm_key))
    )
    (
        layer_out, d_hidden, d_att, queries, pair, soft, raw, normed, grad_down, grad_gate_up,
        d_att_scaled, w_qkv, grad_output, gains, gain_grads, weight, cosine, sine,
    ) = forward(
        inputs[0], cotangent[0], doc_start, jnp.asarray(FREQUENCY), packed,
        (w_query, w_key, w_value, w_output, w_gate, w_up, w_down),
    )
    input_grad, down, gate_up_share, output, qkv, gain_grads = backward(
        (d_att, pair, soft, d_att_scaled, queries, raw, normed, w_qkv, inputs[0], d_hidden),
        (cosine, sine, gains, gain_grads, weight),
        (grad_down, grad_gate_up, grad_output),
    )
    layer_out, input_grad, *shares = finish(layer_out, input_grad, down, gate_up_share, output, qkv)
    at = lax.axis_index("fsdp")
    wide = lax.dynamic_slice(gain_grads, (0, at * 160), (4, 160))
    return (
        layer_out[None],
        input_grad[None],
        *shares,
        wide[0],
        wide[1],
        wide[2],
        wide[3],
        lax.dynamic_slice(gain_grads[4, :256], (at * 64,), (64,)),
        lax.dynamic_slice(gain_grads[4, 256:512], (at * 64,), (64,)),
    )


def solution(mesh):
    in_specs = (
        P("fsdp", "seq", None),
        P("fsdp", "seq"),
        P("fsdp", None),
        P("fsdp", None),
        P("fsdp", None),
        P("fsdp", None),
        P("fsdp", None),
        P("fsdp", None),
        P("fsdp", None),
        P("fsdp"),
        P("fsdp"),
        P("fsdp"),
        P("fsdp"),
        P("fsdp"),
        P("fsdp"),
        P("fsdp", "seq", None),
    )
    out_specs = (
        P("fsdp", "seq", None),
        P("fsdp", "seq", None),
        P("fsdp", None),
        P("fsdp", None),
        P("fsdp", None),
        P("fsdp", None),
        P("fsdp", None),
        P("fsdp", None),
        P("fsdp", None),
        P("fsdp"),
        P("fsdp"),
        P("fsdp"),
        P("fsdp"),
        P("fsdp"),
        P("fsdp"),
    )
    return jax.shard_map(body, mesh=mesh, in_specs=in_specs, out_specs=out_specs, check_vma=False)
```

```python
import jax
import jax.numpy as jnp
import numpy as np
from jax import lax
from jax.experimental import pallas as pl
from jax.experimental.pallas import tpu as pltpu
from jax.sharding import PartitionSpec as P

epsilon = 1e-06
rope_base = 10000.0


MESH = pl.DeviceIdType.MESH
DIMS = ("C", "X1", "X0", "Y1", "Y0", "Z1", "Z0")
AXES = {"X": ("X1", "X0"), "Y": ("Y1", "Y0"), "Z": ("Z1", "Z0")}
CORNERS = (("Y0", "Z0"), ("X0", "Z1"), ("Z1", "Y1"), ("X0", "Y1"))


def place():
    return lax.axis_index("seq"), lax.axis_index("fsdp")


def bit_of(dim, s, f):
    if dim == "C":
        return lax.rem(f, 2)
    if dim == "X1":
        return lax.div(f, 2)
    if dim == "X0":
        return lax.rem(lax.rem(lax.div(s, 4), 2) + lax.div(f, 2), 2)
    at = lax.rem(s, 4) if dim[0] == "Y" else lax.div(s, 8)
    if dim[1] == "1":
        return lax.div(at, 2)
    return lax.rem(lax.rem(at, 2) + lax.div(at, 2), 2)


def partner(dim, s, f):
    if dim == "C":
        return (s, f + 1 - 2 * lax.rem(f, 2))
    step = 1 - 2 * lax.rem(lax.div(s, 4), 2)
    if dim == "X0":
        return (s + 4 * step, f)
    if dim == "X1":
        return (s + 4 * step, f + 2 - 4 * lax.div(f, 2))
    at, scale = (lax.rem(s, 4), 1) if dim[0] == "Y" else (lax.div(s, 8), 8)
    if dim[1] == "1":
        return (s + scale * (3 - 2 * at), f)
    return (s + scale * (1 - 2 * lax.rem(at, 2)), f)


def target(dims, s, f):
    for dim in (dims,) if isinstance(dims, str) else dims:
        s, f = partner(dim, s, f)
    return s, f


def neighbour(s, f, by):
    return (lax.rem(s + 32 + by, 32), f)


def greet(s, f, corners):
    barrier = pltpu.get_barrier_semaphore()
    for dim in DIMS:
        pl.semaphore_signal(barrier, inc=1, device_id=partner(dim, s, f), device_id_type=MESH)
    for by in (1, -1):
        pl.semaphore_signal(barrier, inc=1, device_id=neighbour(s, f, by), device_id_type=MESH)
    for one, two in corners:
        corner = partner(two, *partner(one, s, f))
        pl.semaphore_signal(barrier, inc=1, device_id=corner, device_id_type=MESH)
    pl.semaphore_wait(barrier, len(DIMS) + 2 + len(corners))


def span(start, size, tile):
    if isinstance(start, int):
        return pl.ds(start, size)
    return pl.ds(pl.multiple_of(start, tile), size)


class Region:
    def __init__(self, q, r, c):
        self.q, self.r, self.c = q, r, c

    def of(self, ref):
        return ref.at[pl.ds(*self.q), span(*self.r, 16), span(*self.c, 128)]

    def flat(self, ref, r0=0, c0=0):
        return ref.at[span(self.r[0] + r0, self.r[1], 16), span(self.c[0] + c0, self.c[1], 128)]

    def halved(self, axis, bit):
        start, size = getattr(self, axis)
        half = size // 2
        mine = Region(self.q, self.r, self.c)
        setattr(mine, axis, (start + bit * half, half))
        theirs = Region(self.q, self.r, self.c)
        setattr(theirs, axis, (start + (1 - bit) * half, half))
        return mine, theirs

    @property
    def shape(self):
        return (self.q[1], self.r[1], self.c[1])


def rows_per_step(rows, cols):
    best = 16
    for n in (32, 48, 64, 80, 96, 128, 160):
        if rows % n == 0 and n * cols <= 48 * 2048:
            best = n
    return best


def add_blocks(out, first, second, shape):
    quarters, rows, cols = shape
    step = rows_per_step(rows, cols)
    for q in range(quarters):

        def body(i, carry, q=q):
            at = i * step
            ref, index = out(q, at, step)
            ref_a, index_a = first(q, at, step)
            ref_b, index_b = second(q, at, step)
            ref[index] = ref_a[index_a] + ref_b[index_b]
            return carry

        lax.fori_loop(0, rows // step, body, 0)


def view(ref, region):
    def pick(q, at, step):
        rows = span(region.r[0] + at, step, 16)
        return ref, (region.q[0] + q, rows, span(region.c[0], region.c[1], 128))

    return pick


def flat_view(ref, region, r0, c0):
    def pick(q, at, step):
        return ref, (span(region.r[0] + r0 + at, step, 16), span(region.c[0] + c0, region.c[1], 128))

    return pick


def whole_view(ref):
    def pick(q, at, step):
        return ref, (q, span(at, step, 16), slice(None))

    return pick


ORDERS = (
    ("X1", "Y1", "Z1", "X0", "Y0", "Z0"),
    ("Y1", "Z1", "X0", "X1", "Y0", "Z0"),
    ("Z1", "X0", "Y0", "X1", "Z0", "Y1"),
    ("X0", "Y0", "Z0", "X1", "Y1", "Z1"),
    ("Y0", "Z0", "X1", "Y1", "Z1", "X0"),
    ("Z0", "X1", "Y1", "Z1", "X0", "Y0"),
)
PARTS = (
    (0, 0, 256, 0, 640, ORDERS[3], "rrr"),
    (1, 0, 160, 0, 1536, ORDERS[0], "ccr"),
    (1, 0, 160, 1536, 1536, ORDERS[2], "ccr"),
    (1, 0, 160, 3072, 1024, ORDERS[1], "ccc"),
    (0, 256, 256, 0, 640, ORDERS[4], "rrr"),
    (2, 0, 256, 0, 640, ORDERS[5], "rrr"),
)
EARLY = (1, 2, 3, 0, 4, 5)
LATE = ((0, "XYZ"), (512, "YXZ"), (1024, "ZXY"))
SHARES = ((512, 640), (160, 4096), (256, 640), (160, 1536))


def part_shapes(part):
    _, _, rows, _, cols, order, splits = part
    shapes, shape, cut = [], [2, rows, cols], iter(splits)
    for dim in order[:4]:
        axis = 0 if dim == "X1" else {"r": 1, "c": 2}[next(cut)]
        shape[axis] //= 2
        shapes.append(tuple(shape))
    return shapes


class Reduce:
    STAGES = 10

    def __init__(self, s, f, grads, totals, scratch, send_sem, recv_sem, local_sem):
        self.s, self.f, self.grads, self.totals = s, f, grads, totals
        self.send_sem, self.recv_sem, self.local_sem = send_sem, recv_sem, local_sem
        self.acc, self.inbox, self.extra = [], [], []
        for _ in PARTS:
            self.acc.append(scratch.pop(0))
            self.inbox.append([scratch.pop(0) for _ in range(4)])
            self.extra.append([scratch.pop(0) for _ in range(3)])
        n = len(PARTS)
        self.pending, self.count = [], 0
        self.flights, self.loads, self.where = [None] * n, [None] * n, [None] * n
        self.cuts = [iter(part[6]) for part in PARTS]
        self.trail, self.stage = [[] for _ in PARTS], [0] * n

    def send(self, src, dst, dim):
        copy = pltpu.make_async_remote_copy(
            src_ref=src,
            dst_ref=dst,
            send_sem=self.send_sem.at[self.count],
            recv_sem=self.recv_sem.at[self.count],
            device_id=target(dim, self.s, self.f),
            device_id_type=MESH,
        )
        copy.start()
        self.count += 1
        self.pending.append(copy)
        return copy

    def load(self, p):
        tensor, r0, rows, c0, cols, _, _ = PARTS[p]
        self.loads[p] = pltpu.make_async_copy(
            self.grads[tensor].at[:, pl.ds(r0, rows), pl.ds(c0, cols)], self.acc[p], self.local_sem.at[p]
        )
        self.loads[p].start()

    def resume(self, p):
        _, _, rows, _, cols, order, _ = PARTS[p]
        self.loads[p].wait()
        self.loads[p] = None
        dim = order[0]
        axis = "q" if dim == "X1" else next(self.cuts[p])
        self.trail[p].append((dim, axis))
        region = Region((0, 2), (0, rows), (0, cols))
        self.where[p], theirs = region.halved(axis, bit_of(dim, self.s, self.f))
        self.flights[p] = [self.send(theirs.of(self.acc[p]), self.inbox[p][0], dim)]
        self.stage[p] = 1

    def advance(self, p):
        part, stage, s, f = PARTS[p], self.stage[p], self.s, self.f
        tensor, r0, rows, c0, cols, order, _ = part
        acc, where, extra = self.acc[p], self.where[p], self.extra[p]
        self.stage[p] += 1
        for flight in self.flights[p]:
            flight.wait_recv()
        if stage < 5:
            source = self.inbox[p][stage - 1]
            add_blocks(view(acc, where), view(acc, where), whole_view(source), where.shape)
            if stage == 4:
                self.flights[p] = [self.send(where.of(acc), extra[0], order[4])]
                return
            dim = order[stage]
            axis = "q" if dim == "X1" else next(self.cuts[p])
            self.trail[p].append((dim, axis))
            self.where[p], theirs = where.halved(axis, bit_of(dim, s, f))
            self.flights[p] = [self.send(theirs.of(acc), self.inbox[p][stage], dim)]
        elif stage == 5:
            add_blocks(whole_view(extra[1]), view(acc, where), whole_view(extra[0]), where.shape)
            self.flights[p] = [self.send(extra[1], extra[2], order[5])]
        elif stage == 6:
            total = self.totals[tensor]
            add_blocks(flat_view(total, where, r0, c0), whole_view(extra[1]), whole_view(extra[2]), where.shape)
            self.trail[p] = [move for move in reversed(self.trail[p]) if move[1] != "q"]
            self.spread(p)
        else:
            dim, axis = self.trail[p].pop(0)
            start, size = getattr(where, axis)
            setattr(where, axis, (start - bit_of(dim, s, f) * size, 2 * size))
            if self.trail[p]:
                self.spread(p)

    def spread(self, p):
        tensor, r0, _, c0, _, _, _ = PARTS[p]
        region = self.where[p].flat(self.totals[tensor], r0, c0)
        self.flights[p] = [self.send(region, region, self.trail[p][0][0])]


class Late:
    STAGES = 6
    FLIPS = ((1, 0), (0, 1), (1, 1))

    def __init__(self, reduce, number, grad, total, scratch):
        self.reduce, self.grad, self.total = reduce, grad, total
        self.c0, self.axes = LATE[number]
        self.acc, self.from_core, *self.inbox = scratch
        self.where = Region((0, 2), (0, 160), (0, 512))
        self.cuts, self.trail, self.stage = iter("ccr"), [], 0
        self.flights = []

    def bit(self, dim):
        return bit_of(dim, self.reduce.s, self.reduce.f)

    def begin(self):
        core = self.bit("C")
        for high in range(2):
            theirs = self.grad.at[span((2 * high + 1 - core) * 160, 160, 16), pl.ds(self.c0, 512)]
            self.flights.append(self.reduce.send(theirs, self.from_core.at[high], "C"))

    def scatter(self, axis, inbox):
        moves = [(dim, "q" if dim == "X1" else next(self.cuts)) for dim in AXES[axis]]
        self.trail.append(moves)
        here = self.where

        def cut(flips):
            region = here
            for (dim, along), flip in zip(moves, flips):
                bit = self.bit(dim)
                region = region.halved(along, 1 - bit if flip else bit)[0]
            return region

        self.flights = [
            self.reduce.send(
                cut(flips).of(self.acc),
                inbox.at[k],
                tuple(dim for (dim, _), flip in zip(moves, flips) if flip),
            )
            for k, flips in enumerate(self.FLIPS)
        ]
        self.where = cut((0, 0))

    def spread(self):
        moves = [move for move in self.trail.pop() if move[1] != "q"]
        self.grow = moves
        region = self.where.flat(self.total, 0, self.c0)
        choices = self.FLIPS if len(moves) == 2 else ((1,),)
        self.flights = [
            self.reduce.send(region, region, tuple(dim for (dim, _), flip in zip(moves, flips) if flip))
            for flips in choices
        ]

    def summed(self, inbox):
        spot = (
            pl.ds(*self.where.q),
            span(*self.where.r, 16),
            span(*self.where.c, 128),
        )
        terms = [self.acc[spot]] + [inbox[k] for k in range(3)]
        first, second, third, fourth = (term.astype(jnp.float32) for term in terms)
        return spot, ((first + second) + (third + fourth)).astype(jnp.bfloat16)

    def advance(self):
        for flight in self.flights:
            flight.wait_recv()
        stage = self.stage
        self.stage += 1
        if stage == 0:
            core = self.bit("C")
            for high in range(2):
                mine = span((2 * high + core) * 160, 160, 16)
                self.acc[high] = self.grad[mine, pl.ds(self.c0, 512)] + self.from_core[high]
            self.scatter(self.axes[0], self.inbox[0])
        elif stage == 1:
            spot, value = self.summed(self.inbox[0])
            self.acc[spot] = value
            self.scatter(self.axes[1], self.inbox[1])
        elif stage == 2:
            spot, value = self.summed(self.inbox[1])
            self.acc[spot] = value
            self.flights = [
                self.reduce.send(
                    self.where.of(self.acc),
                    self.inbox[2].at[k],
                    tuple(dim for dim, flip in zip(AXES[self.axes[2]], flips) if flip),
                )
                for k, flips in enumerate(self.FLIPS)
            ]
        elif stage == 3:
            _, value = self.summed(self.inbox[2])
            rows, cols = self.where.r, self.where.c
            self.total[span(*rows, 16), span(cols[0] + self.c0, cols[1], 128)] = value[0]
            self.spread()
        else:
            for dim, axis in reversed(self.grow):
                start, size = getattr(self.where, axis)
                setattr(self.where, axis, (start - self.bit(dim) * size, 2 * size))
            if self.trail:
                self.spread()


def late_scratch():
    shapes = []
    for _, axes in LATE:
        one = (1, 160, 256) if axes[0] == "X" else (2, 160, 128)
        shapes += [(2, 160, 512)] * 2 + [(3, *one), (3, 1, 80, 128), (3, 1, 80, 128)]
    return [pltpu.VMEM(shape, jnp.bfloat16) for shape in shapes]


def reduce_scratch():
    scratch, sends = [], 10 + 17 * len(LATE)
    for part in PARTS:
        shapes = part_shapes(part)
        scratch += [pltpu.VMEM((2, part[2], part[4]), jnp.bfloat16)]
        scratch += [pltpu.VMEM(shape, jnp.bfloat16) for shape in shapes]
        scratch += [pltpu.VMEM(shapes[-1], jnp.bfloat16)] * 3
        sends += 11
    return scratch, sends


PIECES = (
    (0, 0, 0, 160, 1024, "Y0", "Z0", "c"),
    (1, 0, 1024, 160, 256, None, None, "whole"),
    (2, 0, 1280, 160, 256, None, None, "whole"),
    (3, 1, 0, 256, 640, "X0", "Z1", "r"),
    (4, 2, 0, 160, 2048, "Z1", "Y1", "c"),
    (5, 2, 2048, 160, 2048, "Y0", "Z0", "c"),
    (6, 3, 0, 512, 640, "X0", "Y1", "r"),
)
WHOLES = ((640, 1536), (1024, 640), (640, 4096), (2048, 640))


def own_gains(gain_shards, gain_own, f):
    def placed(share):
        shift = lax.broadcasted_iota(jnp.int32, (256, 4 * share), 1) - lax.broadcasted_iota(
            jnp.int32, (256, 4 * share), 0
        )
        chosen = jnp.where(shift == share * f, 1.0, 0.0).astype(jnp.bfloat16)
        return jnp.dot(gain_shards[...].astype(jnp.bfloat16), chosen, preferred_element_type=jnp.float32)

    gain_own[...] = jnp.where(lax.broadcasted_iota(jnp.int32, (8, 640), 0) < 4, placed(160), 0.0)
    heads = placed(64)
    gain_own[4:5, 0:256] = heads[4:5, :]
    gain_own[4:5, 256:512] = heads[5:6, :]


class Gather:
    def __init__(self, s, f, shards, outs, send_sem, recv_sem, local_sem):
        self.s, self.f, self.shards, self.outs = s, f, shards, outs
        self.send_sem, self.recv_sem, self.local_sem = send_sem, recv_sem, local_sem
        self.copies, self.count = [], 0
        self.core, high = bit_of("C", s, f), bit_of("X1", s, f)
        self.far = 2 * (1 - high) + self.core
        self.flights, self.sides, self.loads = {}, {}, {}

    def send(self, src, dst, dim):
        copy = pltpu.make_async_remote_copy(
            src_ref=src,
            dst_ref=dst,
            send_sem=self.send_sem.at[self.count],
            recv_sem=self.recv_sem.at[self.count],
            device_id=target(dim, self.s, self.f),
            device_id_type=MESH,
        )
        copy.start()
        self.count += 1
        self.copies.append(copy)
        return copy

    def quarter(self, piece, bit_one, bit_two):
        _, _, c0, rows, cols, _, _, cut = piece
        half = rows // 2
        if cut == "c":
            return (bit_two * half, half), (bit_one * (cols // 2), cols // 2)
        return (bit_two * half + bit_one * (half // 2), half // 2), (0, cols)

    def spot(self, piece, share, box):
        (r, nr), (c, nc) = box
        return self.outs[piece[1]].at[span(r + share * piece[3], nr, 16), span(c + piece[2], nc, 128)]

    def first(self, piece):
        if piece[7] == "whole":
            return (0, piece[3]), (0, piece[4])
        return self.quarter(piece, bit_of(piece[5], self.s, self.f), bit_of(piece[6], self.s, self.f))

    def begin(self, pieces):
        for i in pieces:
            piece = PIECES[i]
            (r, nr), (c, nc) = quarter = self.first(piece)
            src = self.shards[i].at[span(r, nr, 16), span(c, nc, 128)]
            self.flights[i] = self.send(src, self.spot(piece, self.f, quarter), "X1")
        for i in pieces:
            piece = PIECES[i]
            dst = self.spot(piece, self.f, ((0, piece[3]), (0, piece[4])))
            self.sides[i] = [self.send(self.shards[i], dst, "C")]
            self.loads[i] = pltpu.make_async_copy(self.shards[i], dst, self.local_sem.at[i])
            self.loads[i].start()

    def fan(self, i):
        piece, s, f = PIECES[i], self.s, self.f
        self.flights[i].wait_recv()
        here = self.spot(piece, self.far, self.first(piece))
        self.sides[i].append(self.send(here, here, "C"))
        if piece[7] == "whole":
            return
        one, two = bit_of(piece[5], s, f), bit_of(piece[6], s, f)
        self.flights[i] = [
            (self.send(here, here, piece[5]), (1 - one, two)),
            (self.send(here, here, piece[6]), (one, 1 - two)),
            (self.send(here, here, (piece[5], piece[6])), (1 - one, 1 - two)),
        ]

    def relay(self, i):
        piece = PIECES[i]
        for flight, bits in self.flights[i]:
            flight.wait_recv()
            here = self.spot(piece, self.far, self.quarter(piece, *bits))
            self.sides[i].append(self.send(here, here, "C"))

    def arrive(self, i):
        for copy in self.sides[i]:
            copy.wait_recv()
        self.loads[i].wait()


SENDS = 9 * len(PIECES) + 7


NT = (((1,), (1,)), ((), ()))


def dot(left, right):
    return jnp.dot(left, right, preferred_element_type=jnp.float32)


def dot_nt(left, right):
    return lax.dot_general(left, right, NT, preferred_element_type=jnp.float32)


def block(i, size):
    if isinstance(i, int):
        return pl.ds(i * size, size)
    return pl.ds(pl.multiple_of(i * size, size), size)


def each(count, body):
    def step(i, carry):
        body(i)
        return carry

    lax.fori_loop(0, count, step, 0)


def unrolled(count, body):
    for i in range(count):
        body(i)


def scale_of(y):
    return lax.rsqrt(jnp.mean(y * y, -1, keepdims=True) + epsilon)


def norm_back(dz, y, r, g):
    gained = g * dz
    return r * gained - y * (r * r * r) * jnp.mean(gained * y, -1, keepdims=True)


def fold(terms):
    rows, cols = terms.shape
    return jnp.sum(terms.reshape(rows // 8, 8, cols), 0)


def turn(v, cosine, sine):
    a, b = v[:, :128], v[:, 128:]
    return jnp.concatenate([a * cosine - b * sine, b * cosine + a * sine], 1)


def turn_back(v, cosine, sine):
    a, b = v[:, :128], v[:, 128:]
    return jnp.concatenate([a * cosine + b * sine, b * cosine - a * sine], 1)


def forward_kernel(*refs):
    x_far, cot_far, doc, frequency, gain_shards = refs[:5]
    shards = refs[5:12]
    outs, gains, gain_grads, weight, cosine, sine = refs[12:25], *refs[25:30]
    (
        x, cot, d_hidden, d_att, d_att_scaled, queries, pair, soft, raw, normed,
        grad_down, grad_gate_up, grad_output, w_qkv, w_output, w_gate_up, w_down,
        turned_v, att, att_t, projected, hidden, normed_two, normed_two_t,
        product, slope, level, gate, up, down, d_down, d_proj, layer_out, sums, weight_sums,
        gain_own, gain_mid, gain_in, normed_spots, *from_core,
    ) = refs[30:-6]
    send_sem, recv_sem, local_sem, out_sem, in_sem, pair_sem = refs[-6:]
    s, f = place()
    greet(s, f, CORNERS)
    gather = Gather(s, f, shards, (w_qkv, w_output, w_gate_up, w_down), send_sem, recv_sem, local_sem)
    gather.begin((1, 2, 0))
    load_x = pltpu.make_async_copy(x_far, x, in_sem.at[0])
    load_x.start()
    load_cot = pltpu.make_async_copy(cot_far, cot, in_sem.at[1])
    load_cot.start()
    own_gains(gain_shards, gain_own, f)
    flight = gather.send(gain_own, gain_in.at[0], "C")
    lanes = lambda i: gains[pl.ds(i, 1), :]
    written = []

    def write(src, number):
        copy = pltpu.make_async_copy(src, outs[number], out_sem.at[number])
        copy.start()
        written.append(copy)

    token = lax.broadcasted_iota(jnp.int32, (1, 512), 1) + s * 512
    position = (token - doc[...]).astype(jnp.float32)
    position = jnp.broadcast_to(position, (8, 512)).T

    def table(i):
        rows = block(i, 64)
        angle = spots[rows, 0:1] * frequency[0:1, :]
        cosine[rows, :] = jnp.cos(angle)
        sine[rows, :] = jnp.sin(angle)

    spots = normed_spots
    spots[...] = position
    flight.wait_recv()
    gain_mid[...] = gain_own[...] + gain_in[0]
    flight = gather.send(gain_mid, gain_in.at[1], "X1")
    unrolled(8, table)
    for i in (1, 2, 0):
        gather.fan(i)
    gather.begin((3, 4, 5, 6))
    flight.wait_recv()
    gains[...] = gain_mid[...] + gain_in[1]
    load_x.wait()

    def norm_in(i):
        rows = block(i, 64)
        y = x[rows, :].astype(jnp.float32)
        normed[rows, :] = (y * scale_of(y) * lanes(0)).astype(jnp.bfloat16)

    unrolled(8, norm_in)
    write(normed, 7)
    gather.arrive(1)
    gather.arrive(2)
    pair_raw = dot(normed[...], w_qkv[:, 1024:1536])
    raw[:, 1024:1280] = pair_raw[:, :256]
    pair[512:1024, 256:512] = pair_raw[:, 256:].astype(jnp.bfloat16)

    def shape_key(i):
        rows = block(i, 128)
        y = raw[rows, 1024:1280]
        y = turn(y * scale_of(y) * gains[pl.ds(4, 1), 256:512], cosine[rows, :], sine[rows, :])
        pair[pl.ds(512 + i * 128, 128), 0:256] = y.astype(jnp.bfloat16)

    unrolled(4, shape_key)
    pass_on = pltpu.make_async_remote_copy(
        src_ref=pair.at[pl.ds(512, 512), :],
        dst_ref=pair.at[pl.ds(0, 512), :],
        send_sem=pair_sem.at[0],
        recv_sem=pair_sem.at[1],
        device_id=neighbour(s, f, 1),
        device_id_type=MESH,
    )
    pass_on.start()
    gather.relay(0)
    gather.arrive(0)
    write(w_qkv, 11)

    def shape_query(h):
        raw[:, block(h, 256)] = dot(normed[...], w_qkv[:, block(h, 256)])

        def rows_of(i):
            rows = block(i, 128)
            y = raw[rows, block(h, 256)]
            y = turn(y * scale_of(y) * gains[pl.ds(4, 1), 0:256], cosine[rows, :], sine[rows, :])
            at = pl.ds(pl.multiple_of(h * 256 + i % 2 * 128, 128), 128)
            queries[i // 2, at, :] = (y * 0.0625).astype(jnp.bfloat16)

        unrolled(4, rows_of)

    each(4, shape_query)
    write(raw, 6)
    write(queries, 3)
    gather.fan(3)
    gather.fan(4)
    row = [lax.broadcasted_iota(jnp.int32, (1, 256), 1) + i * 256 for i in range(2)]
    lowest = [
        jnp.maximum(row[i] + 1, doc[0:1, 256 * i : 256 * (i + 1)] - (s - 1) * 512) for i in range(2)
    ]

    def weigh(i, h, first, count):
        total = None
        query = queries[i, block(h, 256), :]
        for c in range(first, first + count, 2):
            low = i * 256 + c * 128
            score = dot_nt(pair[low : low + 256, 0:256], query)
            key = lax.broadcasted_iota(jnp.int32, (256, 256), 0) + low
            seen = (key >= lowest[i]) & (key <= row[i] + 512)
            p = jnp.where(seen, jnp.exp(score), 0.0)
            soft[i, c * 128 : c * 128 + 256, block(h, 256)] = p.astype(jnp.bfloat16)
            total = fold(p) if total is None else total + fold(p)
        return total

    for i, first, count in ((0, 4, 2), (1, 2, 4)):

        def own_keys(h, i=i, first=first, count=count):
            weight_sums[i, h] = weigh(i, h, first, count)

        each(4, own_keys)
        gather.fan(5 + i)
    gather.relay(3)
    pass_on.wait_recv()
    write(pair, 4)
    turned_v[...] = pair[:, 256:512].T
    for i, first, count in ((0, 0, 4), (1, 0, 2)):

        def attend(h, i=i, first=first, count=count):
            total = weight_sums[i, h] + weigh(i, h, first, count)
            inverse = 1.0 / jnp.sum(total, 0, keepdims=True)
            weight[pl.ds(4 * i + h, 1), :] = inverse
            mixed = dot(turned_v[:, 256 * i : 256 * i + 768], soft[i, :, block(h, 256)]) * inverse
            att_t[block(h, 256), 256 * i : 256 * (i + 1)] = mixed.astype(jnp.bfloat16)
            att[256 * i : 256 * (i + 1), block(h, 256)] = mixed.T.astype(jnp.bfloat16)

        each(4, attend)
        gather.relay(4 + i)
    write(soft, 5)
    gather.arrive(3)
    projected[...] = dot(att[...], w_output[...])

    def mid(i):
        rows = block(i, 64)
        y = projected[rows, :]
        z = x[rows, :].astype(jnp.float32) + y * scale_of(y) * lanes(1)
        hidden[rows, :] = z
        normed_two[rows, :] = (z * scale_of(z) * lanes(2)).astype(jnp.bfloat16)

    unrolled(8, mid)
    normed_two_t[...] = normed_two[...].T
    gather.relay(6)
    gather.arrive(4)
    gather.arrive(5)

    def feed(j):
        cols = block(j, 512)
        gate[...] = dot(normed_two[...], w_gate_up[:, cols])
        up[...] = dot(normed_two[...], w_gate_up[:, pl.ds(pl.multiple_of(2048 + j * 512, 512), 512)])

        def bend(i):
            rows = block(i, 64)
            g, u = gate[rows, :], up[rows, :]
            square = g * g
            t = jnp.tanh(0.7978845608028654 * g * (1.0 + 0.044715 * square))
            half = 0.5 * (1.0 + t)
            gelu = g * half
            rise = half + 0.5 * g * (1.0 - t * t) * (0.7978845608028654 * (1.0 + 0.134145 * square))
            product[rows, cols] = (gelu * u).astype(jnp.bfloat16)
            slope[rows, cols] = (rise * u).astype(jnp.bfloat16)
            level[rows, cols] = gelu.astype(jnp.bfloat16)

        unrolled(8, bend)

    each(4, feed)
    gather.arrive(6)
    down[...] = dot(product[...], w_down[...])
    sums[...] = jnp.zeros_like(sums)
    load_cot.wait()

    def end(i):
        rows = block(i, 64)
        y, dz = down[rows, :], cot[rows, :].astype(jnp.float32)
        r = scale_of(y)
        layer_out[rows, :] = (hidden[rows, :] + y * r * lanes(3)).astype(jnp.bfloat16)
        d_down[rows, :] = norm_back(dz, y, r, lanes(3)).astype(jnp.bfloat16)
        sums[2] += fold(dz * y * r)

    unrolled(8, end)
    write(layer_out, 0)

    def feed_back(j):
        cols = block(j, 512)
        gate[...] = dot_nt(d_down[...], w_down[cols, :])

        def bend(i):
            rows = block(i, 128)
            d = gate[rows, :]
            slope[rows, cols] = (d * slope[rows, cols].astype(jnp.float32)).astype(jnp.bfloat16)
            level[rows, cols] = (d * level[rows, cols].astype(jnp.float32)).astype(jnp.bfloat16)

        unrolled(4, bend)
        for grad, at in ((slope, 0), (level, 2048)):
            block_ = dot(normed_two_t[...], grad[:, cols]).astype(jnp.bfloat16)
            for q in range(4):
                grad_gate_up[q // 2, q % 2, :, pl.ds(pl.multiple_of(at + j * 512, 512), 512)] = block_[
                    160 * q : 160 * (q + 1), :
                ]

    def down_back(q):
        grad_down[lax.div(q, 2), lax.rem(q, 2)] = dot(product[:, block(q, 512)].T, d_down[...]).astype(
            jnp.bfloat16
        )

    core, exchanged = bit_of("C", s, f), {}
    tensors = (grad_down, grad_gate_up, grad_output)

    def exchange(p):
        tensor, r0, rows, c0, cols, _, _ = PARTS[p]
        theirs = tensors[tensor].at[pl.ds(0, 2), 1 - core, pl.ds(r0, rows), pl.ds(c0, cols)]
        exchanged[p] = gather.send(theirs, from_core[p], "C")

    def add_exchanged(p):
        tensor, r0, rows, c0, cols, _, _ = PARTS[p]
        exchanged[p].wait_recv()
        step = rows_per_step(rows, cols)
        for q in range(2):

            def add(i, q=q):
                at = pl.ds(pl.multiple_of(r0 + i * step, 16), step)
                tensors[tensor][q, core, at, pl.ds(c0, cols)] += from_core[p][q, block(i, step), :]

            each(rows // step, add)

    each(4, feed_back)
    for p in (1, 2, 3):
        exchange(p)
    each(4, down_back)
    for p in (0, 4):
        exchange(p)
    down[...] = dot_nt(slope[...], w_gate_up[:, 0:2048])
    down[...] += dot_nt(level[...], w_gate_up[:, 2048:4096])

    def mid_back(i):
        rows = block(i, 64)
        dz, y = down[rows, :], hidden[rows, :]
        r = scale_of(y)
        total = cot[rows, :].astype(jnp.float32) + norm_back(dz, y, r, lanes(2))
        sums[1] += fold(dz * y * r)
        d_hidden[rows, :] = total
        y = projected[rows, :]
        r = scale_of(y)
        d_proj[rows, :] = norm_back(total, y, r, lanes(1)).astype(jnp.bfloat16)
        sums[0] += fold(total * y * r)

    unrolled(8, mid_back)
    write(d_hidden, 1)
    columns = weight[...].T

    def output_back(h):
        grad_output[lax.div(h, 2), lax.rem(h, 2)] = dot(att_t[block(h, 256), :], d_proj[...]).astype(jnp.bfloat16)

    each(4, output_back)
    exchange(5)
    for h in range(4):
        part = pl.ds(256 * h, 256)
        back = dot_nt(d_proj[...], w_output[part, :])
        for i in range(2):
            mine = back[256 * i : 256 * (i + 1), :]
            n = 4 * i + h
            d_att[i, part, :] = mine.astype(jnp.bfloat16)
            d_att_scaled[i, part, :] = (mine * columns[:, n : n + 1]).astype(jnp.bfloat16)
    write(d_att, 2)
    write(d_att_scaled, 10)
    for p in (1, 2, 3):
        add_exchanged(p)
    write(grad_gate_up.at[:, core], 9)
    for p in (0, 4):
        add_exchanged(p)
    write(grad_down.at[:, core], 8)
    add_exchanged(5)
    write(grad_output.at[:, core], 12)
    gain_grads[...] = jnp.zeros_like(gain_grads)
    for i in range(3):
        gain_grads[pl.ds(i + 1, 1), :] = jnp.sum(sums[i], 0, keepdims=True)
    for copy in written:
        copy.wait()
    pass_on.wait_send()
    for copy in gather.copies:
        copy.wait_send()


def forward(x, cot, doc, frequency, gain_shards, shards):
    b, f32 = jnp.bfloat16, jnp.float32
    outs = [
        ((512, 640), b), ((512, 640), f32), ((2, 1024, 256), b), ((2, 1024, 256), b), ((1024, 512), b),
        ((2, 768, 1024), b), ((512, 1280), f32), ((512, 640), b),
        ((2, 512, 640), b), ((2, 160, 4096), b), ((2, 1024, 256), b), ((640, 1536), b), ((2, 256, 640), b),
    ]
    near = [((8, 640), f32), ((8, 640), f32), ((8, 256), f32), ((512, 128), f32), ((512, 128), f32)]
    scratch = [
        ((512, 640), b), ((512, 640), b), ((512, 640), f32), ((2, 1024, 256), b), ((2, 1024, 256), b),
        ((2, 1024, 256), b), ((1024, 512), b), ((2, 768, 1024), b), ((512, 1280), f32), ((512, 640), b),
        ((2, 2, 512, 640), b), ((2, 2, 160, 4096), b), ((2, 2, 256, 640), b),
        ((640, 1536), b), ((1024, 640), b), ((640, 4096), b), ((2048, 640), b),
        ((256, 1024), b), ((512, 1024), b), ((1024, 512), b), ((512, 640), f32), ((512, 640), f32),
        ((512, 640), b), ((640, 512), b), ((512, 2048), b), ((512, 2048), b), ((512, 2048), b),
        ((512, 512), f32), ((512, 512), f32), ((512, 640), f32), ((512, 640), b), ((512, 640), b),
        ((512, 640), b), ((3, 8, 640), f32), ((2, 4, 8, 256), f32),
        ((8, 640), f32), ((8, 640), f32), ((2, 8, 640), f32), ((512, 8), f32),
    ]
    scratch += [((2, part[2], part[4]), b) for part in PARTS]
    sems = (SENDS, SENDS, 7, len(outs), 2, 2)
    far, vmem = pl.BlockSpec(memory_space=pl.ANY), pl.BlockSpec(memory_space=pltpu.VMEM)
    return pl.pallas_call(
        forward_kernel,
        out_shape=[jax.ShapeDtypeStruct(*o) for o in outs + near],
        in_specs=[far] * 2 + [vmem] * 3 + [far] * 7,
        out_specs=[far] * len(outs) + [vmem] * len(near),
        scratch_shapes=[pltpu.VMEM(*o) for o in scratch] + [pltpu.SemaphoreType.DMA((n,)) for n in sems],
        compiler_params=pltpu.CompilerParams(
            collective_id=2, has_side_effects=True, vmem_limit_bytes=60 << 20
        ),
        name="forward",
    )(x, cot, doc, frequency, gain_shards, *shards)


def backward_kernel(*refs):
    fars, near = refs[:10], refs[10:15]
    cosine, sine, gains, gain_grads, weight = near
    grads, refs = refs[15:18], refs[18:]
    input_grad, totals, gain_total = refs[0], refs[1:5], refs[5]
    (
        d_att, d_att_scaled, soft, pair, queries, raw, normed, w_qkv, x, d_hidden, *rest
    ) = refs[6:]
    (
        turned_k, d_soft, d_scores, d_queries, d_pair, first, other, d_raw, normed_t, d_normed,
        grad_qkv, sums, head_sums, gain_in, gain_sum, *rest
    ) = rest
    in_sem, pair_sem, send_sem, recv_sem, local_sem = rest[-5:]
    s, f = place()
    boxes = list(rest[:-5])
    reduce = Reduce(s, f, grads, totals, boxes[15:], send_sem, recv_sem, local_sem)
    lates = [Late(reduce, n, grad_qkv, totals[3], boxes[5 * n : 5 * n + 5]) for n in range(len(LATE))]
    for p in EARLY:
        reduce.load(p)
    greet(s, f, tuple(AXES.values()))
    for p in EARLY:
        reduce.resume(p)
    loads = []
    for i, (src, dst) in enumerate(
        zip(fars, (d_att, pair, soft, d_att_scaled, queries, raw, normed, w_qkv, x, d_hidden))
    ):
        loads.append(pltpu.make_async_copy(src, dst, in_sem.at[i]))
        loads[-1].start()

    def all_of(parts):
        for p in parts:
            reduce.advance(p)

    d_pair[...] = jnp.zeros_like(d_pair)
    sums[...] = jnp.zeros_like(sums)
    head_sums[...] = jnp.zeros_like(head_sums)
    for load in loads[:5]:
        load.wait()
    turned_k[...] = pair[:, 0:256].T
    for i in range(2):

        def one_head(h, i=i):
            cols = block(h, 256)
            inverse = weight[pl.ds(4 * i + h, 1), :]
            total = None
            for c in range(3):
                low = 256 * (i + c)
                back = dot_nt(pair[low : low + 256, 256:512], d_att[i, cols, :])
                d_soft[256 * c : 256 * (c + 1), :] = back
                part = fold(soft[i, 256 * c : 256 * (c + 1), cols].astype(jnp.float32) * back)
                total = part if total is None else total + part
            inner = jnp.sum(total, 0, keepdims=True) * inverse
            for c in range(3):
                rows = pl.ds(256 * c, 256)
                p = soft[i, rows, cols].astype(jnp.float32)
                d_scores[i, rows, cols] = (p * ((d_soft[rows, :] - inner) * inverse)).astype(jnp.bfloat16)

        each(4, one_head)

    def to_pair(i, low, count):
        at, here = pl.ds(low, count), pl.ds(low - 256 * i, count)
        d_pair[at, 0:256] += dot(d_scores[i, here, :], queries[i])
        d_pair[at, 256:512] += dot(soft[i, here, :], d_att_scaled[i])

    to_pair(0, 0, 512)
    to_pair(1, 256, 256)
    first[...] = d_pair[0:512, :].astype(jnp.bfloat16)
    pass_back = pltpu.make_async_remote_copy(
        src_ref=first,
        dst_ref=other,
        send_sem=pair_sem.at[0],
        recv_sem=pair_sem.at[1],
        device_id=neighbour(s, f, -1),
        device_id_type=MESH,
    )
    pass_back.start()
    to_pair(0, 512, 256)
    to_pair(1, 512, 512)
    for load in loads[5:]:
        load.wait()
    normed_t[...] = normed[...].T
    for i in range(2):

        def query_back(h, i=i):
            cols = block(h, 256)
            mixed = dot(turned_k[:, 256 * i : 256 * i + 768], d_scores[i, :, cols]) * 0.0625
            d_queries[...] = mixed.T

            def rows_of(n):
                rows = pl.ds(256 * i + n * 128, 128)
                dz = turn_back(d_queries[block(n, 128), :], cosine[rows, :], sine[rows, :])
                y = raw[rows, cols]
                r = scale_of(y)
                d_raw[rows, cols] = norm_back(dz, y, r, gains[pl.ds(4, 1), 0:256]).astype(jnp.bfloat16)
                head_sums[0] += fold(dz * y * r)

            unrolled(2, rows_of)

        each(4, query_back)
    all_of(EARLY)
    pass_back.wait_recv()

    def key_back(i):
        rows = block(i, 128)
        own = pl.ds(512 + i * 128, 128)
        dz = d_pair[own, 0:256] + other[rows, 0:256].astype(jnp.float32)
        dz = turn_back(dz, cosine[rows, :], sine[rows, :])
        y = raw[rows, 1024:1280]
        r = scale_of(y)
        d_raw[rows, 1024:1280] = norm_back(dz, y, r, gains[pl.ds(4, 1), 256:512]).astype(jnp.bfloat16)
        head_sums[1] += fold(dz * y * r)
        d_value = d_pair[own, 256:512] + other[rows, 256:512].astype(jnp.float32)
        d_raw[rows, 1280:1536] = d_value.astype(jnp.bfloat16)

    unrolled(4, key_back)

    def weigh_in(j):
        cols = block(j, 512)
        grad_qkv[:, cols] = dot(normed_t[...], d_raw[:, cols]).astype(jnp.bfloat16)

    each(3, weigh_in)
    for late in lates:
        late.begin()
    d_normed[...] = dot_nt(d_raw[...], w_qkv[...])
    lanes_in = gains[pl.ds(0, 1), :]

    def norm_in_back(i):
        rows = block(i, 64)
        y, dz = x[rows, :].astype(jnp.float32), d_normed[rows, :]
        r = scale_of(y)
        input_grad[rows, :] = d_hidden[rows, :] + norm_back(dz, y, r, lanes_in)
        sums[...] += fold(dz * y * r)

    unrolled(8, norm_in_back)
    gain_sum[0] = gain_grads[...]
    gain_sum[0, pl.ds(0, 1), :] = jnp.sum(sums[...], 0, keepdims=True)
    gain_sum[0, pl.ds(4, 1), 0:256] = jnp.sum(head_sums[0], 0, keepdims=True)
    gain_sum[0, pl.ds(4, 1), 256:512] = jnp.sum(head_sums[1], 0, keepdims=True)
    flights = [reduce.send(gain_sum.at[0], gain_in.at[0], "C")]
    for stage in range(8):
        if stage < Late.STAGES:
            for late in lates:
                late.advance()
        if stage < 4:
            total = gain_sum[stage]
            for k, flight in enumerate(flights):
                flight.wait_recv()
                total = total + gain_in[max(3 * stage - 2, 0) + k]
            gain_sum[stage + 1] = total
        if stage < 3:
            high, low = AXES["XYZ"[stage]]
            flights = [
                reduce.send(gain_sum.at[stage + 1], gain_in.at[3 * stage + 1 + k], dims)
                for k, dims in enumerate(((high,), (low,), (high, low)))
            ]
        all_of(EARLY)
    gain_total[...] = gain_sum[4]
    pass_back.wait_send()
    for copy in reduce.pending:
        copy.wait_send()


def backward(fars, near, grads):
    b, f32 = jnp.bfloat16, jnp.float32
    outs = [((512, 640), f32)] + [(shape, b) for shape in SHARES] + [((8, 640), f32)]
    held = [
        ((2, 1024, 256), b), ((2, 1024, 256), b), ((2, 768, 1024), b), ((1024, 512), b), ((2, 1024, 256), b),
        ((512, 1280), f32), ((512, 640), b), ((640, 1536), b), ((512, 640), b), ((512, 640), f32),
    ]
    scratch = [
        ((256, 1024), b), ((768, 256), f32), ((2, 768, 1024), b), ((256, 256), f32), ((1024, 512), f32),
        ((512, 512), b), ((512, 512), b), ((512, 1536), b), ((640, 512), b), ((512, 640), f32),
        ((640, 1536), b), ((8, 640), f32), ((2, 8, 256), f32), ((10, 8, 640), f32), ((5, 8, 640), f32),
    ]
    parts, sends = reduce_scratch()
    sems = (len(held), 2, sends, sends, len(PARTS))
    far, vmem = pl.BlockSpec(memory_space=pl.ANY), pl.BlockSpec(memory_space=pltpu.VMEM)
    return pl.pallas_call(
        backward_kernel,
        out_shape=[jax.ShapeDtypeStruct(*o) for o in outs],
        in_specs=[far] * 10 + [vmem] * 5 + [far] * 3,
        out_specs=[vmem] * len(outs),
        scratch_shapes=[pltpu.VMEM(*o) for o in held + scratch]
        + late_scratch()
        + parts
        + [pltpu.SemaphoreType.DMA((n,)) for n in sems],
        compiler_params=pltpu.CompilerParams(
            collective_id=3, has_side_effects=True, vmem_limit_bytes=60 << 20
        ),
        name="backward",
    )(*fars, *near, *grads)


FREQUENCY = (rope_base ** (-np.arange(128) / 128.0)).astype(np.float32)[None, :]


def finish_kernel(*refs):
    fars, outs, near, sem = refs[:6], refs[6:15], refs[15:21], refs[21]
    loads = []
    for i, (src, dst) in enumerate(zip(fars, near)):
        loads.append(pltpu.make_async_copy(src, dst, sem.at[i]))
        loads[-1].start()
    layer_out, input_grad, down, gate_up, output, qkv = near
    cuts = (
        (2, down, 8, 0),
        (3, gate_up, 6, 0),
        (3, gate_up, 7, 2048),
        (4, output, 5, 0),
        (5, qkv, 2, 0),
        (5, qkv, 3, 1024),
        (5, qkv, 4, 1280),
    )
    waited = set()
    for number, src, at, first in cuts:
        if number not in waited:
            loads[number].wait()
            waited.add(number)
        out = outs[at]
        rows, cols = out.shape

        def widen(i, out=out, src=src, first=first, cols=cols):
            part = block(i, 32)
            out[part, :] = src[part, first : first + cols].astype(jnp.float32)

        each(rows // 32, widen)
    for number in range(2):
        loads[number].wait()
        outs[number][...] = near[number][...]


def finish(layer_out, input_grad, down, gate_up, output, qkv):
    shapes = ((160, 1024), (160, 256), (160, 256), (256, 640), (160, 2048), (160, 2048), (512, 640))
    return pl.pallas_call(
        finish_kernel,
        out_shape=[
            jax.ShapeDtypeStruct((512, 640), jnp.bfloat16),
            jax.ShapeDtypeStruct((512, 640), jnp.float32),
        ]
        + [jax.ShapeDtypeStruct(shape, jnp.float32) for shape in shapes],
        in_specs=[pl.BlockSpec(memory_space=pl.ANY)] * 6,
        out_specs=[pl.BlockSpec(memory_space=pltpu.VMEM)] * 9,
        scratch_shapes=[
            pltpu.VMEM((512, 640), jnp.bfloat16),
            pltpu.VMEM((512, 640), jnp.float32),
        ]
        + [pltpu.VMEM(shape, jnp.bfloat16) for shape in SHARES]
        + [pltpu.SemaphoreType.DMA((6,))],
        compiler_params=pltpu.CompilerParams(vmem_limit_bytes=60 << 20),
        name="finish",
    )(layer_out, input_grad, down, gate_up, output, qkv)


def body(
    inputs,
    doc_start,
    w_query,
    w_key,
    w_value,
    w_output,
    w_gate,
    w_up,
    w_down,
    norm_attn_in,
    norm_attn_out,
    norm_ffn_in,
    norm_ffn_out,
    norm_query,
    norm_key,
    cotangent,
):
    packed = sum(
        jnp.pad(g.astype(jnp.float32)[None, :], ((i, 7 - i), (0, 256 - g.shape[0])))
        for i, g in enumerate((norm_attn_in, norm_attn_out, norm_ffn_in, norm_ffn_out, norm_query, norm_key))
    )
    (
        layer_out, d_hidden, d_att, queries, pair, soft, raw, normed, grad_down, grad_gate_up,
        d_att_scaled, w_qkv, grad_output, gains, gain_grads, weight, cosine, sine,
    ) = forward(
        inputs[0], cotangent[0], doc_start, jnp.asarray(FREQUENCY), packed,
        (w_query, w_key, w_value, w_output, w_gate, w_up, w_down),
    )
    input_grad, down, gate_up_share, output, qkv, gain_grads = backward(
        (d_att, pair, soft, d_att_scaled, queries, raw, normed, w_qkv, inputs[0], d_hidden),
        (cosine, sine, gains, gain_grads, weight),
        (grad_down, grad_gate_up, grad_output),
    )
    layer_out, input_grad, *shares = finish(layer_out, input_grad, down, gate_up_share, output, qkv)
    at = lax.axis_index("fsdp")
    wide = lax.dynamic_slice(gain_grads, (0, at * 160), (4, 160))
    return (
        layer_out[None],
        input_grad[None],
        *shares,
        wide[0],
        wide[1],
        wide[2],
        wide[3],
        lax.dynamic_slice(gain_grads[4, :256], (at * 64,), (64,)),
        lax.dynamic_slice(gain_grads[4, 256:512], (at * 64,), (64,)),
    )


def solution(mesh):
    in_specs = (
        P("fsdp", "seq", None),
        P("fsdp", "seq"),
        P("fsdp", None),
        P("fsdp", None),
        P("fsdp", None),
        P("fsdp", None),
        P("fsdp", None),
        P("fsdp", None),
        P("fsdp", None),
        P("fsdp"),
        P("fsdp"),
        P("fsdp"),
        P("fsdp"),
        P("fsdp"),
        P("fsdp"),
        P("fsdp", "seq", None),
    )
    out_specs = (
        P("fsdp", "seq", None),
        P("fsdp", "seq", None),
        P("fsdp", None),
        P("fsdp", None),
        P("fsdp", None),
        P("fsdp", None),
        P("fsdp", None),
        P("fsdp", None),
        P("fsdp", None),
        P("fsdp"),
        P("fsdp"),
        P("fsdp"),
        P("fsdp"),
        P("fsdp"),
        P("fsdp"),
    )
    return jax.shard_map(body, mesh=mesh, in_specs=in_specs, out_specs=out_specs, check_vma=False)
```

```python
import jax
import jax.numpy as jnp
import numpy as np
from jax import lax
from jax.experimental import pallas as pl
from jax.experimental.pallas import tpu as pltpu
from jax.sharding import PartitionSpec as P

epsilon = 1e-06
rope_base = 10000.0


MESH = pl.DeviceIdType.MESH
DIMS = ("C", "X1", "X0", "Y1", "Y0", "Z1", "Z0")
AXES = {"X": ("X1", "X0"), "Y": ("Y1", "Y0"), "Z": ("Z1", "Z0")}
CORNERS = (("Y0", "Z0"), ("X0", "Z1"), ("Z1", "Y1"), ("X0", "Y1"))


def place():
    return lax.axis_index("seq"), lax.axis_index("fsdp")


def bit_of(dim, s, f):
    if dim == "C":
        return lax.rem(f, 2)
    if dim == "X1":
        return lax.div(f, 2)
    if dim == "X0":
        return lax.rem(lax.rem(lax.div(s, 4), 2) + lax.div(f, 2), 2)
    at = lax.rem(s, 4) if dim[0] == "Y" else lax.div(s, 8)
    if dim[1] == "1":
        return lax.div(at, 2)
    return lax.rem(lax.rem(at, 2) + lax.div(at, 2), 2)


def partner(dim, s, f):
    if dim == "C":
        return (s, f + 1 - 2 * lax.rem(f, 2))
    step = 1 - 2 * lax.rem(lax.div(s, 4), 2)
    if dim == "X0":
        return (s + 4 * step, f)
    if dim == "X1":
        return (s + 4 * step, f + 2 - 4 * lax.div(f, 2))
    at, scale = (lax.rem(s, 4), 1) if dim[0] == "Y" else (lax.div(s, 8), 8)
    if dim[1] == "1":
        return (s + scale * (3 - 2 * at), f)
    return (s + scale * (1 - 2 * lax.rem(at, 2)), f)


def target(dims, s, f):
    for dim in (dims,) if isinstance(dims, str) else dims:
        s, f = partner(dim, s, f)
    return s, f


def neighbour(s, f, by):
    return (lax.rem(s + 32 + by, 32), f)


def greet(s, f, corners):
    barrier = pltpu.get_barrier_semaphore()
    for dim in DIMS:
        pl.semaphore_signal(barrier, inc=1, device_id=partner(dim, s, f), device_id_type=MESH)
    for by in (1, -1):
        pl.semaphore_signal(barrier, inc=1, device_id=neighbour(s, f, by), device_id_type=MESH)
    for one, two in corners:
        corner = partner(two, *partner(one, s, f))
        pl.semaphore_signal(barrier, inc=1, device_id=corner, device_id_type=MESH)
    pl.semaphore_wait(barrier, len(DIMS) + 2 + len(corners))


def span(start, size, tile):
    if isinstance(start, int):
        return pl.ds(start, size)
    return pl.ds(pl.multiple_of(start, tile), size)


class Region:
    def __init__(self, q, r, c):
        self.q, self.r, self.c = q, r, c

    def of(self, ref):
        return ref.at[pl.ds(*self.q), span(*self.r, 16), span(*self.c, 128)]

    def flat(self, ref, r0=0, c0=0):
        return ref.at[span(self.r[0] + r0, self.r[1], 16), span(self.c[0] + c0, self.c[1], 128)]

    def halved(self, axis, bit):
        start, size = getattr(self, axis)
        half = size // 2
        mine = Region(self.q, self.r, self.c)
        setattr(mine, axis, (start + bit * half, half))
        theirs = Region(self.q, self.r, self.c)
        setattr(theirs, axis, (start + (1 - bit) * half, half))
        return mine, theirs

    @property
    def shape(self):
        return (self.q[1], self.r[1], self.c[1])


def rows_per_step(rows, cols):
    best = 16
    for n in (32, 48, 64, 80, 96, 128, 160):
        if rows % n == 0 and n * cols <= 48 * 2048:
            best = n
    return best


def add_blocks(out, first, second, shape):
    quarters, rows, cols = shape
    step = rows_per_step(rows, cols)
    for q in range(quarters):

        def body(i, carry, q=q):
            at = i * step
            ref, index = out(q, at, step)
            ref_a, index_a = first(q, at, step)
            ref_b, index_b = second(q, at, step)
            ref[index] = ref_a[index_a] + ref_b[index_b]
            return carry

        lax.fori_loop(0, rows // step, body, 0)


def view(ref, region):
    def pick(q, at, step):
        rows = span(region.r[0] + at, step, 16)
        return ref, (region.q[0] + q, rows, span(region.c[0], region.c[1], 128))

    return pick


def flat_view(ref, region, r0, c0):
    def pick(q, at, step):
        return ref, (span(region.r[0] + r0 + at, step, 16), span(region.c[0] + c0, region.c[1], 128))

    return pick


def whole_view(ref):
    def pick(q, at, step):
        return ref, (q, span(at, step, 16), slice(None))

    return pick


ORDERS = (
    ("X1", "Y1", "Z1", "X0", "Y0", "Z0"),
    ("Y1", "Z1", "X0", "X1", "Y0", "Z0"),
    ("Z1", "X0", "Y0", "X1", "Z0", "Y1"),
    ("X0", "Y0", "Z0", "X1", "Y1", "Z1"),
    ("Y0", "Z0", "X1", "Y1", "Z1", "X0"),
    ("Z0", "X1", "Y1", "Z1", "X0", "Y0"),
)
PARTS = (
    (0, 0, 256, 0, 640, ORDERS[3], "rrr"),
    (1, 0, 160, 0, 1536, ORDERS[0], "ccr"),
    (1, 0, 160, 1536, 1536, ORDERS[2], "ccr"),
    (1, 0, 160, 3072, 1024, ORDERS[1], "ccc"),
    (0, 256, 256, 0, 640, ORDERS[4], "rrr"),
    (2, 0, 256, 0, 640, ORDERS[5], "rrr"),
)
EARLY = (1, 2, 3, 0, 4, 5)
LATE = ((0, "XYZ"), (512, "YXZ"), (1024, "ZXY"))
SHARES = ((512, 640), (160, 4096), (256, 640), (160, 1536))


def part_shapes(part):
    _, _, rows, _, cols, order, splits = part
    shapes, shape, cut = [], [2, rows, cols], iter(splits)
    for dim in order[:4]:
        axis = 0 if dim == "X1" else {"r": 1, "c": 2}[next(cut)]
        shape[axis] //= 2
        shapes.append(tuple(shape))
    return shapes


class Reduce:
    STAGES = 10

    def __init__(self, s, f, grads, totals, scratch, send_sem, recv_sem, local_sem):
        self.s, self.f, self.grads, self.totals = s, f, grads, totals
        self.send_sem, self.recv_sem, self.local_sem = send_sem, recv_sem, local_sem
        self.acc, self.inbox, self.extra = [], [], []
        for _ in PARTS:
            self.acc.append(scratch.pop(0))
            self.inbox.append([scratch.pop(0) for _ in range(4)])
            self.extra.append([scratch.pop(0) for _ in range(3)])
        n = len(PARTS)
        self.pending, self.count = [], 0
        self.flights, self.loads, self.where = [None] * n, [None] * n, [None] * n
        self.cuts = [iter(part[6]) for part in PARTS]
        self.trail, self.stage = [[] for _ in PARTS], [0] * n

    def send(self, src, dst, dim):
        copy = pltpu.make_async_remote_copy(
            src_ref=src,
            dst_ref=dst,
            send_sem=self.send_sem.at[self.count],
            recv_sem=self.recv_sem.at[self.count],
            device_id=target(dim, self.s, self.f),
            device_id_type=MESH,
        )
        copy.start()
        self.count += 1
        self.pending.append(copy)
        return copy

    def load(self, p):
        tensor, r0, rows, c0, cols, _, _ = PARTS[p]
        self.loads[p] = pltpu.make_async_copy(
            self.grads[tensor].at[:, pl.ds(r0, rows), pl.ds(c0, cols)], self.acc[p], self.local_sem.at[p]
        )
        self.loads[p].start()

    def resume(self, p):
        _, _, rows, _, cols, order, _ = PARTS[p]
        self.loads[p].wait()
        self.loads[p] = None
        dim = order[0]
        axis = "q" if dim == "X1" else next(self.cuts[p])
        self.trail[p].append((dim, axis))
        region = Region((0, 2), (0, rows), (0, cols))
        self.where[p], theirs = region.halved(axis, bit_of(dim, self.s, self.f))
        self.flights[p] = [self.send(theirs.of(self.acc[p]), self.inbox[p][0], dim)]
        self.stage[p] = 1

    def advance(self, p):
        part, stage, s, f = PARTS[p], self.stage[p], self.s, self.f
        tensor, r0, rows, c0, cols, order, _ = part
        acc, where, extra = self.acc[p], self.where[p], self.extra[p]
        self.stage[p] += 1
        for flight in self.flights[p]:
            flight.wait_recv()
        if stage < 5:
            source = self.inbox[p][stage - 1]
            add_blocks(view(acc, where), view(acc, where), whole_view(source), where.shape)
            if stage == 4:
                self.flights[p] = [self.send(where.of(acc), extra[0], order[4])]
                return
            dim = order[stage]
            axis = "q" if dim == "X1" else next(self.cuts[p])
            self.trail[p].append((dim, axis))
            self.where[p], theirs = where.halved(axis, bit_of(dim, s, f))
            self.flights[p] = [self.send(theirs.of(acc), self.inbox[p][stage], dim)]
        elif stage == 5:
            add_blocks(whole_view(extra[1]), view(acc, where), whole_view(extra[0]), where.shape)
            self.flights[p] = [self.send(extra[1], extra[2], order[5])]
        elif stage == 6:
            total = self.totals[tensor]
            add_blocks(flat_view(total, where, r0, c0), whole_view(extra[1]), whole_view(extra[2]), where.shape)
            self.trail[p] = [move for move in reversed(self.trail[p]) if move[1] != "q"]
            self.spread(p)
        else:
            dim, axis = self.trail[p].pop(0)
            start, size = getattr(where, axis)
            setattr(where, axis, (start - bit_of(dim, s, f) * size, 2 * size))
            if self.trail[p]:
                self.spread(p)

    def spread(self, p):
        tensor, r0, _, c0, _, _, _ = PARTS[p]
        region = self.where[p].flat(self.totals[tensor], r0, c0)
        self.flights[p] = [self.send(region, region, self.trail[p][0][0])]


class Late:
    STAGES = 6
    FLIPS = ((1, 0), (0, 1), (1, 1))

    def __init__(self, reduce, number, grad, total, scratch):
        self.reduce, self.grad, self.total = reduce, grad, total
        self.c0, self.axes = LATE[number]
        self.acc, self.from_core, *self.inbox = scratch
        self.where = Region((0, 2), (0, 160), (0, 512))
        self.cuts, self.trail, self.stage = iter("ccr"), [], 0
        self.flights = []

    def bit(self, dim):
        return bit_of(dim, self.reduce.s, self.reduce.f)

    def begin(self):
        core = self.bit("C")
        for high in range(2):
            theirs = self.grad.at[span((2 * high + 1 - core) * 160, 160, 16), pl.ds(self.c0, 512)]
            self.flights.append(self.reduce.send(theirs, self.from_core.at[high], "C"))

    def scatter(self, axis, inbox):
        moves = [(dim, "q" if dim == "X1" else next(self.cuts)) for dim in AXES[axis]]
        self.trail.append(moves)
        here = self.where

        def cut(flips):
            region = here
            for (dim, along), flip in zip(moves, flips):
                bit = self.bit(dim)
                region = region.halved(along, 1 - bit if flip else bit)[0]
            return region

        self.flights = [
            self.reduce.send(
                cut(flips).of(self.acc),
                inbox.at[k],
                tuple(dim for (dim, _), flip in zip(moves, flips) if flip),
            )
            for k, flips in enumerate(self.FLIPS)
        ]
        self.where = cut((0, 0))

    def spread(self):
        moves = [move for move in self.trail.pop() if move[1] != "q"]
        self.grow = moves
        region = self.where.flat(self.total, 0, self.c0)
        choices = self.FLIPS if len(moves) == 2 else ((1,),)
        self.flights = [
            self.reduce.send(region, region, tuple(dim for (dim, _), flip in zip(moves, flips) if flip))
            for flips in choices
        ]

    def summed(self, inbox):
        spot = (
            pl.ds(*self.where.q),
            span(*self.where.r, 16),
            span(*self.where.c, 128),
        )
        terms = [self.acc[spot]] + [inbox[k] for k in range(3)]
        first, second, third, fourth = (term.astype(jnp.float32) for term in terms)
        return spot, ((first + second) + (third + fourth)).astype(jnp.bfloat16)

    def advance(self):
        for flight in self.flights:
            flight.wait_recv()
        stage = self.stage
        self.stage += 1
        if stage == 0:
            core = self.bit("C")
            for high in range(2):
                mine = span((2 * high + core) * 160, 160, 16)
                self.acc[high] = self.grad[mine, pl.ds(self.c0, 512)] + self.from_core[high]
            self.scatter(self.axes[0], self.inbox[0])
        elif stage == 1:
            spot, value = self.summed(self.inbox[0])
            self.acc[spot] = value
            self.scatter(self.axes[1], self.inbox[1])
        elif stage == 2:
            spot, value = self.summed(self.inbox[1])
            self.acc[spot] = value
            self.flights = [
                self.reduce.send(
                    self.where.of(self.acc),
                    self.inbox[2].at[k],
                    tuple(dim for dim, flip in zip(AXES[self.axes[2]], flips) if flip),
                )
                for k, flips in enumerate(self.FLIPS)
            ]
        elif stage == 3:
            _, value = self.summed(self.inbox[2])
            rows, cols = self.where.r, self.where.c
            self.total[span(*rows, 16), span(cols[0] + self.c0, cols[1], 128)] = value[0]
            self.spread()
        else:
            for dim, axis in reversed(self.grow):
                start, size = getattr(self.where, axis)
                setattr(self.where, axis, (start - self.bit(dim) * size, 2 * size))
            if self.trail:
                self.spread()


def late_scratch():
    shapes = []
    for _, axes in LATE:
        one = (1, 160, 256) if axes[0] == "X" else (2, 160, 128)
        shapes += [(2, 160, 512)] * 2 + [(3, *one), (3, 1, 80, 128), (3, 1, 80, 128)]
    return [pltpu.VMEM(shape, jnp.bfloat16) for shape in shapes]


def reduce_scratch():
    scratch, sends = [], 10 + 17 * len(LATE)
    for part in PARTS:
        shapes = part_shapes(part)
        scratch += [pltpu.VMEM((2, part[2], part[4]), jnp.bfloat16)]
        scratch += [pltpu.VMEM(shape, jnp.bfloat16) for shape in shapes]
        scratch += [pltpu.VMEM(shapes[-1], jnp.bfloat16)] * 3
        sends += 11
    return scratch, sends


PIECES = (
    (0, 0, 0, 160, 1024, "Y0", "Z0", "c"),
    (1, 0, 1024, 160, 256, None, None, "whole"),
    (2, 0, 1280, 160, 256, None, None, "whole"),
    (3, 1, 0, 256, 640, "X0", "Z1", "r"),
    (4, 2, 0, 160, 2048, "Z1", "Y1", "c"),
    (5, 2, 2048, 160, 2048, "Y0", "Z0", "c"),
    (6, 3, 0, 512, 640, "X0", "Y1", "r"),
)
WHOLES = ((640, 1536), (1024, 640), (640, 4096), (2048, 640))


def own_gains(gain_shards, gain_own, f):
    def placed(share):
        shift = lax.broadcasted_iota(jnp.int32, (256, 4 * share), 1) - lax.broadcasted_iota(
            jnp.int32, (256, 4 * share), 0
        )
        chosen = jnp.where(shift == share * f, 1.0, 0.0).astype(jnp.bfloat16)
        return jnp.dot(gain_shards[...].astype(jnp.bfloat16), chosen, preferred_element_type=jnp.float32)

    gain_own[...] = jnp.where(lax.broadcasted_iota(jnp.int32, (8, 640), 0) < 4, placed(160), 0.0)
    heads = placed(64)
    gain_own[4:5, 0:256] = heads[4:5, :]
    gain_own[4:5, 256:512] = heads[5:6, :]


class Gather:
    def __init__(self, s, f, shards, outs, send_sem, recv_sem, local_sem):
        self.s, self.f, self.shards, self.outs = s, f, shards, outs
        self.send_sem, self.recv_sem, self.local_sem = send_sem, recv_sem, local_sem
        self.copies, self.count = [], 0
        self.core, high = bit_of("C", s, f), bit_of("X1", s, f)
        self.far = 2 * (1 - high) + self.core
        self.flights, self.sides, self.loads = {}, {}, {}

    def send(self, src, dst, dim):
        copy = pltpu.make_async_remote_copy(
            src_ref=src,
            dst_ref=dst,
            send_sem=self.send_sem.at[self.count],
            recv_sem=self.recv_sem.at[self.count],
            device_id=target(dim, self.s, self.f),
            device_id_type=MESH,
        )
        copy.start()
        self.count += 1
        self.copies.append(copy)
        return copy

    def quarter(self, piece, bit_one, bit_two):
        _, _, c0, rows, cols, _, _, cut = piece
        half = rows // 2
        if cut == "c":
            return (bit_two * half, half), (bit_one * (cols // 2), cols // 2)
        return (bit_two * half + bit_one * (half // 2), half // 2), (0, cols)

    def spot(self, piece, share, box):
        (r, nr), (c, nc) = box
        return self.outs[piece[1]].at[span(r + share * piece[3], nr, 16), span(c + piece[2], nc, 128)]

    def first(self, piece):
        if piece[7] == "whole":
            return (0, piece[3]), (0, piece[4])
        return self.quarter(piece, bit_of(piece[5], self.s, self.f), bit_of(piece[6], self.s, self.f))

    def begin(self, pieces):
        for i in pieces:
            piece = PIECES[i]
            (r, nr), (c, nc) = quarter = self.first(piece)
            src = self.shards[i].at[span(r, nr, 16), span(c, nc, 128)]
            self.flights[i] = self.send(src, self.spot(piece, self.f, quarter), "X1")
        for i in pieces:
            piece = PIECES[i]
            dst = self.spot(piece, self.f, ((0, piece[3]), (0, piece[4])))
            self.sides[i] = [self.send(self.shards[i], dst, "C")]
            self.loads[i] = pltpu.make_async_copy(self.shards[i], dst, self.local_sem.at[i])
            self.loads[i].start()

    def fan(self, i):
        piece, s, f = PIECES[i], self.s, self.f
        self.flights[i].wait_recv()
        here = self.spot(piece, self.far, self.first(piece))
        self.sides[i].append(self.send(here, here, "C"))
        if piece[7] == "whole":
            return
        one, two = bit_of(piece[5], s, f), bit_of(piece[6], s, f)
        self.flights[i] = [
            (self.send(here, here, piece[5]), (1 - one, two)),
            (self.send(here, here, piece[6]), (one, 1 - two)),
            (self.send(here, here, (piece[5], piece[6])), (1 - one, 1 - two)),
        ]

    def relay(self, i):
        piece = PIECES[i]
        for flight, bits in self.flights[i]:
            flight.wait_recv()
            here = self.spot(piece, self.far, self.quarter(piece, *bits))
            self.sides[i].append(self.send(here, here, "C"))

    def arrive(self, i):
        for copy in self.sides[i]:
            copy.wait_recv()
        self.loads[i].wait()


SENDS = 9 * len(PIECES) + 7


NT = (((1,), (1,)), ((), ()))


def dot(left, right):
    return jnp.dot(left, right, preferred_element_type=jnp.float32)


def dot_nt(left, right):
    return lax.dot_general(left, right, NT, preferred_element_type=jnp.float32)


def block(i, size):
    if isinstance(i, int):
        return pl.ds(i * size, size)
    return pl.ds(pl.multiple_of(i * size, size), size)


def each(count, body):
    def step(i, carry):
        body(i)
        return carry

    lax.fori_loop(0, count, step, 0)


def unrolled(count, body):
    for i in range(count):
        body(i)


def scale_of(y):
    return lax.rsqrt(jnp.mean(y * y, -1, keepdims=True) + epsilon)


def norm_back(dz, y, r, g):
    gained = g * dz
    return r * gained - y * (r * r * r) * jnp.mean(gained * y, -1, keepdims=True)


def fold(terms):
    rows, cols = terms.shape
    return jnp.sum(terms.reshape(rows // 8, 8, cols), 0)


def turn(v, cosine, sine):
    a, b = v[:, :128], v[:, 128:]
    return jnp.concatenate([a * cosine - b * sine, b * cosine + a * sine], 1)


def turn_back(v, cosine, sine):
    a, b = v[:, :128], v[:, 128:]
    return jnp.concatenate([a * cosine + b * sine, b * cosine - a * sine], 1)


def forward_kernel(*refs):
    x_far, cot_far, doc, frequency, gain_shards = refs[:5]
    shards = refs[5:12]
    outs, gains, gain_grads, weight, cosine, sine = refs[12:25], *refs[25:30]
    (
        x, cot, d_hidden, d_att, d_att_scaled, queries, pair, soft, raw, normed,
        grad_down, grad_gate_up, grad_output, w_qkv, w_output, w_gate_up, w_down,
        turned_v, att, att_t, projected, hidden, normed_two, normed_two_t,
        product, slope, level, gate, up, down, d_down, d_proj, layer_out, sums, weight_sums,
        gain_own, gain_mid, gain_in, normed_spots, *from_core,
    ) = refs[30:-6]
    send_sem, recv_sem, local_sem, out_sem, in_sem, pair_sem = refs[-6:]
    s, f = place()
    greet(s, f, CORNERS)
    gather = Gather(s, f, shards, (w_qkv, w_output, w_gate_up, w_down), send_sem, recv_sem, local_sem)
    gather.begin((1, 2, 0))
    load_x = pltpu.make_async_copy(x_far, x, in_sem.at[0])
    load_x.start()
    load_cot = pltpu.make_async_copy(cot_far, cot, in_sem.at[1])
    load_cot.start()
    own_gains(gain_shards, gain_own, f)
    flight = gather.send(gain_own, gain_in.at[0], "C")
    lanes = lambda i: gains[pl.ds(i, 1), :]
    written = []

    def write(src, number):
        copy = pltpu.make_async_copy(src, outs[number], out_sem.at[number])
        copy.start()
        written.append(copy)

    token = lax.broadcasted_iota(jnp.int32, (1, 512), 1) + s * 512
    position = (token - doc[...]).astype(jnp.float32)
    position = jnp.broadcast_to(position, (8, 512)).T

    def table(i):
        rows = block(i, 64)
        angle = spots[rows, 0:1] * frequency[0:1, :]
        cosine[rows, :] = jnp.cos(angle)
        sine[rows, :] = jnp.sin(angle)

    spots = normed_spots
    spots[...] = position
    flight.wait_recv()
    gain_mid[...] = gain_own[...] + gain_in[0]
    flight = gather.send(gain_mid, gain_in.at[1], "X1")
    unrolled(8, table)
    for i in (1, 2, 0):
        gather.fan(i)
    gather.begin((3, 4, 5, 6))
    flight.wait_recv()
    gains[...] = gain_mid[...] + gain_in[1]
    load_x.wait()

    def norm_in(i):
        rows = block(i, 64)
        y = x[rows, :].astype(jnp.float32)
        normed[rows, :] = (y * scale_of(y) * lanes(0)).astype(jnp.bfloat16)

    unrolled(8, norm_in)
    write(normed, 7)
    gather.arrive(1)
    gather.arrive(2)
    pair_raw = dot(normed[...], w_qkv[:, 1024:1536])
    raw[:, 1024:1280] = pair_raw[:, :256]
    pair[512:1024, 256:512] = pair_raw[:, 256:].astype(jnp.bfloat16)

    def shape_key(i):
        rows = block(i, 128)
        y = raw[rows, 1024:1280]
        y = turn(y * scale_of(y) * gains[pl.ds(4, 1), 256:512], cosine[rows, :], sine[rows, :])
        pair[pl.ds(512 + i * 128, 128), 0:256] = y.astype(jnp.bfloat16)

    unrolled(4, shape_key)
    pass_on = pltpu.make_async_remote_copy(
        src_ref=pair.at[pl.ds(512, 512), :],
        dst_ref=pair.at[pl.ds(0, 512), :],
        send_sem=pair_sem.at[0],
        recv_sem=pair_sem.at[1],
        device_id=neighbour(s, f, 1),
        device_id_type=MESH,
    )
    pass_on.start()
    gather.relay(0)
    gather.arrive(0)
    write(w_qkv, 11)

    def shape_query(h):
        raw[:, block(h, 256)] = dot(normed[...], w_qkv[:, block(h, 256)])

        def rows_of(i):
            rows = block(i, 128)
            y = raw[rows, block(h, 256)]
            y = turn(y * scale_of(y) * gains[pl.ds(4, 1), 0:256], cosine[rows, :], sine[rows, :])
            at = pl.ds(pl.multiple_of(h * 256 + i % 2 * 128, 128), 128)
            queries[i // 2, at, :] = (y * 0.0625).astype(jnp.bfloat16)

        unrolled(4, rows_of)

    unrolled(4, shape_query)
    write(raw, 6)
    write(queries, 3)
    gather.fan(3)
    gather.fan(4)
    row = [lax.broadcasted_iota(jnp.int32, (1, 256), 1) + i * 256 for i in range(2)]
    lowest = [
        jnp.maximum(row[i] + 1, doc[0:1, 256 * i : 256 * (i + 1)] - (s - 1) * 512) for i in range(2)
    ]

    def weigh(i, h, first, count):
        total = None
        query = queries[i, block(h, 256), :]
        for c in range(first, first + count, 2):
            low = i * 256 + c * 128
            score = dot_nt(pair[low : low + 256, 0:256], query)
            key = lax.broadcasted_iota(jnp.int32, (256, 256), 0) + low
            seen = (key >= lowest[i]) & (key <= row[i] + 512)
            p = jnp.where(seen, jnp.exp(score), 0.0)
            soft[i, c * 128 : c * 128 + 256, block(h, 256)] = p.astype(jnp.bfloat16)
            total = fold(p) if total is None else total + fold(p)
        return total

    for i, first, count in ((0, 4, 2), (1, 2, 4)):

        def own_keys(h, i=i, first=first, count=count):
            weight_sums[i, h] = weigh(i, h, first, count)

        unrolled(4, own_keys)
        gather.fan(5 + i)
    gather.relay(3)
    pass_on.wait_recv()
    write(pair, 4)
    turned_v[...] = pair[:, 256:512].T
    for i, first, count in ((0, 0, 4), (1, 0, 2)):

        def attend(h, i=i, first=first, count=count):
            total = weight_sums[i, h] + weigh(i, h, first, count)
            inverse = 1.0 / jnp.sum(total, 0, keepdims=True)
            weight[pl.ds(4 * i + h, 1), :] = inverse
            mixed = dot(turned_v[:, 256 * i : 256 * i + 768], soft[i, :, block(h, 256)]) * inverse
            att_t[block(h, 256), 256 * i : 256 * (i + 1)] = mixed.astype(jnp.bfloat16)
            att[256 * i : 256 * (i + 1), block(h, 256)] = mixed.T.astype(jnp.bfloat16)

        unrolled(4, attend)
        gather.relay(4 + i)
    write(soft, 5)
    gather.arrive(3)
    projected[...] = dot(att[...], w_output[...])

    def mid(i):
        rows = block(i, 64)
        y = projected[rows, :]
        z = x[rows, :].astype(jnp.float32) + y * scale_of(y) * lanes(1)
        hidden[rows, :] = z
        normed_two[rows, :] = (z * scale_of(z) * lanes(2)).astype(jnp.bfloat16)

    unrolled(8, mid)
    normed_two_t[...] = normed_two[...].T
    gather.relay(6)
    gather.arrive(4)
    gather.arrive(5)

    def feed(j):
        cols = block(j, 512)
        gate[...] = dot(normed_two[...], w_gate_up[:, cols])
        up[...] = dot(normed_two[...], w_gate_up[:, pl.ds(pl.multiple_of(2048 + j * 512, 512), 512)])

        def bend(i):
            rows = block(i, 64)
            g, u = gate[rows, :], up[rows, :]
            square = g * g
            t = jnp.tanh(0.7978845608028654 * g * (1.0 + 0.044715 * square))
            half = 0.5 * (1.0 + t)
            gelu = g * half
            rise = half + 0.5 * g * (1.0 - t * t) * (0.7978845608028654 * (1.0 + 0.134145 * square))
            product[rows, cols] = (gelu * u).astype(jnp.bfloat16)
            slope[rows, cols] = (rise * u).astype(jnp.bfloat16)
            level[rows, cols] = gelu.astype(jnp.bfloat16)

        unrolled(8, bend)

    each(4, feed)
    gather.arrive(6)
    down[...] = dot(product[...], w_down[...])
    sums[...] = jnp.zeros_like(sums)
    load_cot.wait()

    def end(i):
        rows = block(i, 64)
        y, dz = down[rows, :], cot[rows, :].astype(jnp.float32)
        r = scale_of(y)
        layer_out[rows, :] = (hidden[rows, :] + y * r * lanes(3)).astype(jnp.bfloat16)
        d_down[rows, :] = norm_back(dz, y, r, lanes(3)).astype(jnp.bfloat16)
        sums[2] += fold(dz * y * r)

    unrolled(8, end)
    write(layer_out, 0)

    def feed_back(j):
        cols = block(j, 512)
        gate[...] = dot_nt(d_down[...], w_down[cols, :])

        def bend(i):
            rows = block(i, 128)
            d = gate[rows, :]
            slope[rows, cols] = (d * slope[rows, cols].astype(jnp.float32)).astype(jnp.bfloat16)
            level[rows, cols] = (d * level[rows, cols].astype(jnp.float32)).astype(jnp.bfloat16)

        unrolled(4, bend)
        for grad, at in ((slope, 0), (level, 2048)):
            block_ = dot(normed_two_t[...], grad[:, cols]).astype(jnp.bfloat16)
            for q in range(4):
                grad_gate_up[q // 2, q % 2, :, pl.ds(pl.multiple_of(at + j * 512, 512), 512)] = block_[
                    160 * q : 160 * (q + 1), :
                ]

    def down_back(q):
        grad_down[lax.div(q, 2), lax.rem(q, 2)] = dot(product[:, block(q, 512)].T, d_down[...]).astype(
            jnp.bfloat16
        )

    core, exchanged = bit_of("C", s, f), {}
    tensors = (grad_down, grad_gate_up, grad_output)

    def exchange(p):
        tensor, r0, rows, c0, cols, _, _ = PARTS[p]
        theirs = tensors[tensor].at[pl.ds(0, 2), 1 - core, pl.ds(r0, rows), pl.ds(c0, cols)]
        exchanged[p] = gather.send(theirs, from_core[p], "C")

    def add_exchanged(p):
        tensor, r0, rows, c0, cols, _, _ = PARTS[p]
        exchanged[p].wait_recv()
        step = rows_per_step(rows, cols)
        for q in range(2):

            def add(i, q=q):
                at = pl.ds(pl.multiple_of(r0 + i * step, 16), step)
                tensors[tensor][q, core, at, pl.ds(c0, cols)] += from_core[p][q, block(i, step), :]

            each(rows // step, add)

    each(4, feed_back)
    for p in (1, 2, 3):
        exchange(p)
    each(4, down_back)
    for p in (0, 4):
        exchange(p)
    down[...] = dot_nt(slope[...], w_gate_up[:, 0:2048])
    down[...] += dot_nt(level[...], w_gate_up[:, 2048:4096])

    def mid_back(i):
        rows = block(i, 64)
        dz, y = down[rows, :], hidden[rows, :]
        r = scale_of(y)
        total = cot[rows, :].astype(jnp.float32) + norm_back(dz, y, r, lanes(2))
        sums[1] += fold(dz * y * r)
        d_hidden[rows, :] = total
        y = projected[rows, :]
        r = scale_of(y)
        d_proj[rows, :] = norm_back(total, y, r, lanes(1)).astype(jnp.bfloat16)
        sums[0] += fold(total * y * r)

    unrolled(8, mid_back)
    write(d_hidden, 1)
    columns = weight[...].T

    def output_back(h):
        grad_output[lax.div(h, 2), lax.rem(h, 2)] = dot(att_t[block(h, 256), :], d_proj[...]).astype(jnp.bfloat16)

    each(4, output_back)
    exchange(5)
    for h in range(4):
        part = pl.ds(256 * h, 256)
        back = dot_nt(d_proj[...], w_output[part, :])
        for i in range(2):
            mine = back[256 * i : 256 * (i + 1), :]
            n = 4 * i + h
            d_att[i, part, :] = mine.astype(jnp.bfloat16)
            d_att_scaled[i, part, :] = (mine * columns[:, n : n + 1]).astype(jnp.bfloat16)
    write(d_att, 2)
    write(d_att_scaled, 10)
    for p in (1, 2, 3):
        add_exchanged(p)
    write(grad_gate_up.at[:, core], 9)
    for p in (0, 4):
        add_exchanged(p)
    write(grad_down.at[:, core], 8)
    add_exchanged(5)
    write(grad_output.at[:, core], 12)
    gain_grads[...] = jnp.zeros_like(gain_grads)
    for i in range(3):
        gain_grads[pl.ds(i + 1, 1), :] = jnp.sum(sums[i], 0, keepdims=True)
    for copy in written:
        copy.wait()
    pass_on.wait_send()
    for copy in gather.copies:
        copy.wait_send()


def forward(x, cot, doc, frequency, gain_shards, shards):
    b, f32 = jnp.bfloat16, jnp.float32
    outs = [
        ((512, 640), b), ((512, 640), f32), ((2, 1024, 256), b), ((2, 1024, 256), b), ((1024, 512), b),
        ((2, 768, 1024), b), ((512, 1280), f32), ((512, 640), b),
        ((2, 512, 640), b), ((2, 160, 4096), b), ((2, 1024, 256), b), ((640, 1536), b), ((2, 256, 640), b),
    ]
    near = [((8, 640), f32), ((8, 640), f32), ((8, 256), f32), ((512, 128), f32), ((512, 128), f32)]
    scratch = [
        ((512, 640), b), ((512, 640), b), ((512, 640), f32), ((2, 1024, 256), b), ((2, 1024, 256), b),
        ((2, 1024, 256), b), ((1024, 512), b), ((2, 768, 1024), b), ((512, 1280), f32), ((512, 640), b),
        ((2, 2, 512, 640), b), ((2, 2, 160, 4096), b), ((2, 2, 256, 640), b),
        ((640, 1536), b), ((1024, 640), b), ((640, 4096), b), ((2048, 640), b),
        ((256, 1024), b), ((512, 1024), b), ((1024, 512), b), ((512, 640), f32), ((512, 640), f32),
        ((512, 640), b), ((640, 512), b), ((512, 2048), b), ((512, 2048), b), ((512, 2048), b),
        ((512, 512), f32), ((512, 512), f32), ((512, 640), f32), ((512, 640), b), ((512, 640), b),
        ((512, 640), b), ((3, 8, 640), f32), ((2, 4, 8, 256), f32),
        ((8, 640), f32), ((8, 640), f32), ((2, 8, 640), f32), ((512, 8), f32),
    ]
    scratch += [((2, part[2], part[4]), b) for part in PARTS]
    sems = (SENDS, SENDS, 7, len(outs), 2, 2)
    far, vmem = pl.BlockSpec(memory_space=pl.ANY), pl.BlockSpec(memory_space=pltpu.VMEM)
    return pl.pallas_call(
        forward_kernel,
        out_shape=[jax.ShapeDtypeStruct(*o) for o in outs + near],
        in_specs=[far] * 2 + [vmem] * 3 + [far] * 7,
        out_specs=[far] * len(outs) + [vmem] * len(near),
        scratch_shapes=[pltpu.VMEM(*o) for o in scratch] + [pltpu.SemaphoreType.DMA((n,)) for n in sems],
        compiler_params=pltpu.CompilerParams(
            collective_id=2, has_side_effects=True, vmem_limit_bytes=60 << 20
        ),
        name="forward",
    )(x, cot, doc, frequency, gain_shards, *shards)


def backward_kernel(*refs):
    fars, near = refs[:10], refs[10:15]
    cosine, sine, gains, gain_grads, weight = near
    grads, refs = refs[15:18], refs[18:]
    input_grad, totals, gain_total = refs[0], refs[1:5], refs[5]
    (
        d_att, d_att_scaled, soft, pair, queries, raw, normed, w_qkv, x, d_hidden, *rest
    ) = refs[6:]
    (
        turned_k, d_soft, d_scores, d_queries, d_pair, first, other, d_raw, normed_t, d_normed,
        grad_qkv, sums, head_sums, gain_in, gain_sum, *rest
    ) = rest
    in_sem, pair_sem, send_sem, recv_sem, local_sem = rest[-5:]
    s, f = place()
    boxes = list(rest[:-5])
    reduce = Reduce(s, f, grads, totals, boxes[15:], send_sem, recv_sem, local_sem)
    lates = [Late(reduce, n, grad_qkv, totals[3], boxes[5 * n : 5 * n + 5]) for n in range(len(LATE))]
    for p in EARLY:
        reduce.load(p)
    greet(s, f, tuple(AXES.values()))
    for p in EARLY:
        reduce.resume(p)
    loads = []
    for i, (src, dst) in enumerate(
        zip(fars, (d_att, pair, soft, d_att_scaled, queries, raw, normed, w_qkv, x, d_hidden))
    ):
        loads.append(pltpu.make_async_copy(src, dst, in_sem.at[i]))
        loads[-1].start()

    def all_of(parts):
        for p in parts:
            reduce.advance(p)

    d_pair[...] = jnp.zeros_like(d_pair)
    sums[...] = jnp.zeros_like(sums)
    head_sums[...] = jnp.zeros_like(head_sums)
    for load in loads[:5]:
        load.wait()
    turned_k[...] = pair[:, 0:256].T
    for i in range(2):

        def one_head(h, i=i):
            cols = block(h, 256)
            inverse = weight[pl.ds(4 * i + h, 1), :]
            total = None
            for c in range(3):
                low = 256 * (i + c)
                back = dot_nt(pair[low : low + 256, 256:512], d_att[i, cols, :])
                d_soft[256 * c : 256 * (c + 1), :] = back
                part = fold(soft[i, 256 * c : 256 * (c + 1), cols].astype(jnp.float32) * back)
                total = part if total is None else total + part
            inner = jnp.sum(total, 0, keepdims=True) * inverse
            for c in range(3):
                rows = pl.ds(256 * c, 256)
                p = soft[i, rows, cols].astype(jnp.float32)
                d_scores[i, rows, cols] = (p * ((d_soft[rows, :] - inner) * inverse)).astype(jnp.bfloat16)

        unrolled(4, one_head)

    def to_pair(i, low, count):
        at, here = pl.ds(low, count), pl.ds(low - 256 * i, count)
        d_pair[at, 0:256] += dot(d_scores[i, here, :], queries[i])
        d_pair[at, 256:512] += dot(soft[i, here, :], d_att_scaled[i])

    to_pair(0, 0, 512)
    to_pair(1, 256, 256)
    first[...] = d_pair[0:512, :].astype(jnp.bfloat16)
    pass_back = pltpu.make_async_remote_copy(
        src_ref=first,
        dst_ref=other,
        send_sem=pair_sem.at[0],
        recv_sem=pair_sem.at[1],
        device_id=neighbour(s, f, -1),
        device_id_type=MESH,
    )
    pass_back.start()
    to_pair(0, 512, 256)
    to_pair(1, 512, 512)
    for load in loads[5:]:
        load.wait()
    normed_t[...] = normed[...].T
    for i in range(2):

        def query_back(h, i=i):
            cols = block(h, 256)
            mixed = dot(turned_k[:, 256 * i : 256 * i + 768], d_scores[i, :, cols]) * 0.0625
            d_queries[...] = mixed.T

            def rows_of(n):
                rows = pl.ds(256 * i + n * 128, 128)
                dz = turn_back(d_queries[block(n, 128), :], cosine[rows, :], sine[rows, :])
                y = raw[rows, cols]
                r = scale_of(y)
                d_raw[rows, cols] = norm_back(dz, y, r, gains[pl.ds(4, 1), 0:256]).astype(jnp.bfloat16)
                head_sums[0] += fold(dz * y * r)

            unrolled(2, rows_of)

        unrolled(4, query_back)
    all_of(EARLY)
    pass_back.wait_recv()

    def key_back(i):
        rows = block(i, 128)
        own = pl.ds(512 + i * 128, 128)
        dz = d_pair[own, 0:256] + other[rows, 0:256].astype(jnp.float32)
        dz = turn_back(dz, cosine[rows, :], sine[rows, :])
        y = raw[rows, 1024:1280]
        r = scale_of(y)
        d_raw[rows, 1024:1280] = norm_back(dz, y, r, gains[pl.ds(4, 1), 256:512]).astype(jnp.bfloat16)
        head_sums[1] += fold(dz * y * r)
        d_value = d_pair[own, 256:512] + other[rows, 256:512].astype(jnp.float32)
        d_raw[rows, 1280:1536] = d_value.astype(jnp.bfloat16)

    unrolled(4, key_back)

    def weigh_in(j):
        cols = block(j, 512)
        grad_qkv[:, cols] = dot(normed_t[...], d_raw[:, cols]).astype(jnp.bfloat16)

    each(3, weigh_in)
    for late in lates:
        late.begin()
    d_normed[...] = dot_nt(d_raw[...], w_qkv[...])
    lanes_in = gains[pl.ds(0, 1), :]

    def norm_in_back(i):
        rows = block(i, 64)
        y, dz = x[rows, :].astype(jnp.float32), d_normed[rows, :]
        r = scale_of(y)
        input_grad[rows, :] = d_hidden[rows, :] + norm_back(dz, y, r, lanes_in)
        sums[...] += fold(dz * y * r)

    unrolled(8, norm_in_back)
    gain_sum[0] = gain_grads[...]
    gain_sum[0, pl.ds(0, 1), :] = jnp.sum(sums[...], 0, keepdims=True)
    gain_sum[0, pl.ds(4, 1), 0:256] = jnp.sum(head_sums[0], 0, keepdims=True)
    gain_sum[0, pl.ds(4, 1), 256:512] = jnp.sum(head_sums[1], 0, keepdims=True)
    flights = [reduce.send(gain_sum.at[0], gain_in.at[0], "C")]
    for stage in range(8):
        if stage < Late.STAGES:
            for late in lates:
                late.advance()
        if stage < 4:
            total = gain_sum[stage]
            for k, flight in enumerate(flights):
                flight.wait_recv()
                total = total + gain_in[max(3 * stage - 2, 0) + k]
            gain_sum[stage + 1] = total
        if stage < 3:
            high, low = AXES["XYZ"[stage]]
            flights = [
                reduce.send(gain_sum.at[stage + 1], gain_in.at[3 * stage + 1 + k], dims)
                for k, dims in enumerate(((high,), (low,), (high, low)))
            ]
        all_of(EARLY)
    gain_total[...] = gain_sum[4]
    pass_back.wait_send()
    for copy in reduce.pending:
        copy.wait_send()


def backward(fars, near, grads):
    b, f32 = jnp.bfloat16, jnp.float32
    outs = [((512, 640), f32)] + [(shape, b) for shape in SHARES] + [((8, 640), f32)]
    held = [
        ((2, 1024, 256), b), ((2, 1024, 256), b), ((2, 768, 1024), b), ((1024, 512), b), ((2, 1024, 256), b),
        ((512, 1280), f32), ((512, 640), b), ((640, 1536), b), ((512, 640), b), ((512, 640), f32),
    ]
    scratch = [
        ((256, 1024), b), ((768, 256), f32), ((2, 768, 1024), b), ((256, 256), f32), ((1024, 512), f32),
        ((512, 512), b), ((512, 512), b), ((512, 1536), b), ((640, 512), b), ((512, 640), f32),
        ((640, 1536), b), ((8, 640), f32), ((2, 8, 256), f32), ((10, 8, 640), f32), ((5, 8, 640), f32),
    ]
    parts, sends = reduce_scratch()
    sems = (len(held), 2, sends, sends, len(PARTS))
    far, vmem = pl.BlockSpec(memory_space=pl.ANY), pl.BlockSpec(memory_space=pltpu.VMEM)
    return pl.pallas_call(
        backward_kernel,
        out_shape=[jax.ShapeDtypeStruct(*o) for o in outs],
        in_specs=[far] * 10 + [vmem] * 5 + [far] * 3,
        out_specs=[vmem] * len(outs),
        scratch_shapes=[pltpu.VMEM(*o) for o in held + scratch]
        + late_scratch()
        + parts
        + [pltpu.SemaphoreType.DMA((n,)) for n in sems],
        compiler_params=pltpu.CompilerParams(
            collective_id=3, has_side_effects=True, vmem_limit_bytes=60 << 20
        ),
        name="backward",
    )(*fars, *near, *grads)


FREQUENCY = (rope_base ** (-np.arange(128) / 128.0)).astype(np.float32)[None, :]


def finish_kernel(*refs):
    fars, outs, near, sem = refs[:6], refs[6:15], refs[15:21], refs[21]
    loads = []
    for i, (src, dst) in enumerate(zip(fars, near)):
        loads.append(pltpu.make_async_copy(src, dst, sem.at[i]))
        loads[-1].start()
    layer_out, input_grad, down, gate_up, output, qkv = near
    cuts = (
        (2, down, 8, 0),
        (3, gate_up, 6, 0),
        (3, gate_up, 7, 2048),
        (4, output, 5, 0),
        (5, qkv, 2, 0),
        (5, qkv, 3, 1024),
        (5, qkv, 4, 1280),
    )
    waited = set()
    for number, src, at, first in cuts:
        if number not in waited:
            loads[number].wait()
            waited.add(number)
        out = outs[at]
        rows, cols = out.shape

        def widen(i, out=out, src=src, first=first, cols=cols):
            part = block(i, 32)
            out[part, :] = src[part, first : first + cols].astype(jnp.float32)

        each(rows // 32, widen)
    for number in range(2):
        loads[number].wait()
        outs[number][...] = near[number][...]


def finish(layer_out, input_grad, down, gate_up, output, qkv):
    shapes = ((160, 1024), (160, 256), (160, 256), (256, 640), (160, 2048), (160, 2048), (512, 640))
    return pl.pallas_call(
        finish_kernel,
        out_shape=[
            jax.ShapeDtypeStruct((512, 640), jnp.bfloat16),
            jax.ShapeDtypeStruct((512, 640), jnp.float32),
        ]
        + [jax.ShapeDtypeStruct(shape, jnp.float32) for shape in shapes],
        in_specs=[pl.BlockSpec(memory_space=pl.ANY)] * 6,
        out_specs=[pl.BlockSpec(memory_space=pltpu.VMEM)] * 9,
        scratch_shapes=[
            pltpu.VMEM((512, 640), jnp.bfloat16),
            pltpu.VMEM((512, 640), jnp.float32),
        ]
        + [pltpu.VMEM(shape, jnp.bfloat16) for shape in SHARES]
        + [pltpu.SemaphoreType.DMA((6,))],
        compiler_params=pltpu.CompilerParams(vmem_limit_bytes=60 << 20),
        name="finish",
    )(layer_out, input_grad, down, gate_up, output, qkv)


def body(
    inputs,
    doc_start,
    w_query,
    w_key,
    w_value,
    w_output,
    w_gate,
    w_up,
    w_down,
    norm_attn_in,
    norm_attn_out,
    norm_ffn_in,
    norm_ffn_out,
    norm_query,
    norm_key,
    cotangent,
):
    packed = sum(
        jnp.pad(g.astype(jnp.float32)[None, :], ((i, 7 - i), (0, 256 - g.shape[0])))
        for i, g in enumerate((norm_attn_in, norm_attn_out, norm_ffn_in, norm_ffn_out, norm_query, norm_key))
    )
    (
        layer_out, d_hidden, d_att, queries, pair, soft, raw, normed, grad_down, grad_gate_up,
        d_att_scaled, w_qkv, grad_output, gains, gain_grads, weight, cosine, sine,
    ) = forward(
        inputs[0], cotangent[0], doc_start, jnp.asarray(FREQUENCY), packed,
        (w_query, w_key, w_value, w_output, w_gate, w_up, w_down),
    )
    input_grad, down, gate_up_share, output, qkv, gain_grads = backward(
        (d_att, pair, soft, d_att_scaled, queries, raw, normed, w_qkv, inputs[0], d_hidden),
        (cosine, sine, gains, gain_grads, weight),
        (grad_down, grad_gate_up, grad_output),
    )
    layer_out, input_grad, *shares = finish(layer_out, input_grad, down, gate_up_share, output, qkv)
    at = lax.axis_index("fsdp")
    wide = lax.dynamic_slice(gain_grads, (0, at * 160), (4, 160))
    return (
        layer_out[None],
        input_grad[None],
        *shares,
        wide[0],
        wide[1],
        wide[2],
        wide[3],
        lax.dynamic_slice(gain_grads[4, :256], (at * 64,), (64,)),
        lax.dynamic_slice(gain_grads[4, 256:512], (at * 64,), (64,)),
    )


def solution(mesh):
    in_specs = (
        P("fsdp", "seq", None),
        P("fsdp", "seq"),
        P("fsdp", None),
        P("fsdp", None),
        P("fsdp", None),
        P("fsdp", None),
        P("fsdp", None),
        P("fsdp", None),
        P("fsdp", None),
        P("fsdp"),
        P("fsdp"),
        P("fsdp"),
        P("fsdp"),
        P("fsdp"),
        P("fsdp"),
        P("fsdp", "seq", None),
    )
    out_specs = (
        P("fsdp", "seq", None),
        P("fsdp", "seq", None),
        P("fsdp", None),
        P("fsdp", None),
        P("fsdp", None),
        P("fsdp", None),
        P("fsdp", None),
        P("fsdp", None),
        P("fsdp", None),
        P("fsdp"),
        P("fsdp"),
        P("fsdp"),
        P("fsdp"),
        P("fsdp"),
        P("fsdp"),
    )
    return jax.shard_map(body, mesh=mesh, in_specs=in_specs, out_specs=out_specs, check_vma=False)
```
